32 devices in a mesh: gx: 8 (over z, y), gy: 4 (over x, core).
Axes of the slice: x: 2, y: 2, z: 4, core: 2. Of those that a mesh axis runs over, the one named last changes fastest.
Arguments:
- strips: float32 [2048, 2, 16, 128], P(('gx', 'gy')), may hold values from -6 to 6
- routes: int32 [2048, 8], P(('gx', 'gy')), may hold values from 0 to 128, as said below
- conv1_weight: float32 [16, 1, 3, 3, 3], replicated, may hold values from -1.25 to 1.25
- conv1_bias: float32 [16], replicated, may hold values from -3 to 3
- conv2_weight: float32 [32, 16, 3, 3, 3], replicated, may hold values from -0.3125 to 0.3125
- conv2_bias: float32 [32], replicated, may hold values from -3 to 3
Outputs:
- features: float32 [32, 1, 512, 512], P(None, None, 'gx', 'gy')
The draws below stay inside these ranges and needn't reach their ends.
Inputs may be any that keep to these rules, and one draw needn't show every extreme that they name: `routes`: slots with v = 0 are all zero. Each device's region receives exactly 64 live strips and their footprints cover every cell of it; one holder keeps at most 2 live strips for one destination, and exactly 2 for some; some holder keeps 64 live strips.
All inputs are finite; a program needn't handle non-finite values.
Results may differ from the reference program's by a relative error of at most 0.0003.
Values sent between devices are 32-bit elements; how exact they have to be, the bound alone decides.
No kernel may reach another device: no remote copies, remote signals or barrier semaphores. Data moves between devices by JAX's collectives and lax.ppermute only.
A program may use at most 192 MiB of HBM per device.

```python
import jax
import jax.numpy as jnp
from jax import lax

BZ = 2
BY = 128
BX = 128
BLK = 2
SY = 16
SX = 128
SROWS = 16
SCOLS = 4
C1 = 16
C2 = 32
STRIPS = 64
SENDERS = 32
PAIR = 2
SPREAD = 1
OWN = 64
N_GX = 8
N_GY = 4


def draw_routes(key, part):
    base_key = jax.random.fold_in(key, 7)
    key_owner, key_lead, key_rows, key_cols, key_shift, key_ramp = jax.random.split(base_key, 6)
    region_cols = BX * BLK
    entries = SENDERS * STRIPS
    owners = jax.random.permutation(key_owner, SENDERS).astype(jnp.int32)
    lead_pos = jax.random.randint(key_lead, (SENDERS,), 0, SPREAD)
    destination = jnp.repeat(jnp.arange(SENDERS, dtype=jnp.int32), STRIPS)
    strip_id = jnp.tile(jnp.arange(STRIPS, dtype=jnp.int32), SENDERS)
    holder = owners[lead_pos[destination] + strip_id // PAIR]
    lattice_row = strip_id // SCOLS
    lattice_col = strip_id % SCOLS
    step_y = (BY - SY + SROWS - 2) // (SROWS - 1)
    jit_y = (SY - step_y) // 2
    step_x = (region_cols - SX + SCOLS - 2) // (SCOLS - 1)
    jit_x = (SX - step_x) // 2
    inner_y = ((lattice_row > 0) & (lattice_row < SROWS - 1)).astype(jnp.int32)
    inner_x = ((lattice_col > 0) & (lattice_col < SCOLS - 1)).astype(jnp.int32)
    wobble_y = jax.random.randint(key_rows, (entries,), -jit_y, jit_y + 1)
    wobble_x = jax.random.randint(key_cols, (entries,), -jit_x, jit_x + 1)
    top_off = jnp.clip(lattice_row * (BY - SY) // (SROWS - 1) + inner_y * wobble_y, 0, BY - SY)
    left_off = jnp.clip(lattice_col * (region_cols - SX) // (SCOLS - 1) + inner_x * wobble_x, 0, region_cols - SX)
    shifts = jax.random.randint(key_shift, (entries, 3), 0, 16)
    ramp_width = jax.random.randint(key_ramp, (entries,), 1, 9)
    live_flag = jnp.ones((entries,), jnp.int32)
    rows_all = jnp.stack([destination, live_flag, top_off, left_off, shifts[:, 0], shifts[:, 1], shifts[:, 2], ramp_width], axis=1).astype(jnp.int32)
    sorted_idx = jnp.argsort(holder, stable=True)
    counts = jnp.zeros((SENDERS,), jnp.int32).at[holder].add(1)
    starts = jnp.cumsum(counts) - counts
    sorted_owner = holder[sorted_idx]
    slot_pos = jnp.arange(entries, dtype=jnp.int32) - starts[sorted_owner]
    target_row = sorted_owner * OWN + slot_pos
    return jnp.zeros((SENDERS * OWN, 8), jnp.int32).at[target_row].set(rows_all[sorted_idx])


def block_levels(rng, extent, cuts, smallest, top_value):
    gain, own = 1.0, jax.random.fold_in(rng, 6)
    for dim, blocks in cuts:
        heights = jnp.exp(jax.random.uniform(jax.random.fold_in(own, dim), (blocks,), jnp.float32, smallest / len(cuts), top_value / len(cuts)))
        gain = gain * jnp.repeat(heights, extent[dim] // blocks).reshape([-1 if axis == dim else 1 for axis in range(len(extent))])
    return gain


def scatter_about(key, extent, width, bound, shards=(), held_as=jnp.bfloat16):
    level = block_levels(key, extent, shards, -0.22, 0.18) if shards else 1.0
    drawn = jax.random.normal(key, extent, jnp.float32) * width * level
    return jnp.minimum(jnp.maximum(drawn, -bound), bound).astype(held_as)


def setup_inputs(seed: int = 0) -> dict:
    streams_of = jax.random.split(jax.random.key(seed), 7)
    return {
        "strips": scatter_about(streams_of[0], (SENDERS * OWN, BZ, SY, SX), 1.0, 6.0, ((0, 32),), jnp.float32),
        "routes": draw_routes(jax.random.fold_in(streams_of[6], 71), 0),
        "conv1_weight": scatter_about(streams_of[2], (C1, 1, 3, 3, 3), 27 ** -0.5, 1.25, (), jnp.float32),
        "conv1_bias": scatter_about(streams_of[3], (C1,), 0.5, 3.0, (), jnp.float32),
        "conv2_weight": scatter_about(streams_of[4], (C2, C1, 3, 3, 3), (C1 * 27) ** -0.5, 0.3125, (), jnp.float32),
        "conv2_bias": scatter_about(streams_of[5], (C2,), 0.5, 3.0, (), jnp.float32),
    }


PRECISE = lax.Precision.HIGHEST


def interp_table(sixteenths, length):
    fraction = sixteenths.astype(jnp.float32) / 16.0
    out_pos = lax.broadcasted_iota(jnp.int32, (length, length), 0)
    in_pos = lax.broadcasted_iota(jnp.int32, (length, length), 1)
    on_diag = (in_pos == out_pos).astype(jnp.float32)
    off_diag = (in_pos == out_pos + 1).astype(jnp.float32)
    return (1.0 - fraction)[:, None, None] * on_diag[None] + fraction[:, None, None] * off_diag[None]


def ramp_table(ramp_width, length):
    position = lax.broadcasted_iota(jnp.int32, (1, length), 1)
    to_edge = jnp.minimum(position + 1, length - position)
    return jnp.minimum(to_edge, ramp_width[:, None]).astype(jnp.float32)


def resample(strip_data, params):
    planes = strip_data.shape[1]
    strip_rows = strip_data.shape[2]
    strip_cols = strip_data.shape[3]
    along_x = interp_table(params[:, 6], strip_cols) * ramp_table(params[:, 7], strip_cols)[:, :, None]
    along_y = interp_table(params[:, 5], strip_rows) * ramp_table(params[:, 7], strip_rows)[:, :, None]
    along_z = interp_table(params[:, 4], planes)
    shifted = jnp.einsum("kzyc,kxc->kzyx", strip_data, along_x, precision=PRECISE)
    shifted = jnp.einsum("kzbx,kyb->kzyx", shifted, along_y, precision=PRECISE)
    return jnp.einsum("kza,kayx->kzyx", along_z, shifted, precision=PRECISE)


def convolve(volume, kernel, stride):
    result = lax.conv_general_dilated(volume[None], kernel, (stride, stride, stride), "VALID",
                                      dimension_numbers=("NCDHW", "OIDHW", "NCDHW"), precision=PRECISE)
    return result[0]


def reference(strips, routes, conv1_weight, conv1_bias, conv2_weight, conv2_bias):
    region_cols = BX * BLK
    grid_rows = BY * N_GX
    grid_cols = region_cols * N_GY
    held_all = strips.reshape(SENDERS, OWN, BZ, SY, SX)
    lists_all = routes.reshape(SENDERS, OWN, 8)

    def per_owner(running, owner_item):
        owner_block, params = owner_item
        pieces = resample(owner_block, params)
        ramp_rows = ramp_table(params[:, 7], SY)
        ramp_cols = ramp_table(params[:, 7], SX)

        def per_slot(state, slot_index):
            numerator, weight_total = state
            route_row = params[slot_index]
            is_live = route_row[1].astype(jnp.float32)
            top_edge = ((route_row[0] // N_GY) * BY + route_row[2]).astype(jnp.int32)
            left_edge = ((route_row[0] % N_GY) * region_cols + route_row[3]).astype(jnp.int32)
            anchor = jnp.zeros((), jnp.int32)
            current = lax.dynamic_slice(numerator, (anchor, top_edge, left_edge), (BZ, SY, SX))
            numerator = lax.dynamic_update_slice(numerator, current + is_live * pieces[slot_index],
                                                 (anchor, top_edge, left_edge))
            weight_patch = lax.dynamic_slice(weight_total, (top_edge, left_edge), (SY, SX))
            added = is_live * ramp_rows[slot_index][:, None] * ramp_cols[slot_index][None, :]
            weight_total = lax.dynamic_update_slice(weight_total, weight_patch + added, (top_edge, left_edge))
            return (numerator, weight_total), None

        running = lax.scan(per_slot, running, jnp.arange(OWN, dtype=jnp.int32))[0]
        return running, None

    start_state = (jnp.zeros((BZ, grid_rows, grid_cols), jnp.float32),
                   jnp.zeros((grid_rows, grid_cols), jnp.float32))
    numerator, weight_total = lax.scan(per_owner, start_state, (held_all, lists_all))[0]
    joined_volume = numerator / weight_total[None]
    padded = jnp.pad(joined_volume, ((1, 1), (2, 1), (1, 1)))

    def one_band(band_index):
        band_start = (band_index * BY).astype(jnp.int32)
        anchor = jnp.zeros((), jnp.int32)
        window = lax.dynamic_slice(padded, (anchor, band_start, anchor), (BZ + 2, BY + 3, grid_cols + 2))
        hidden = jax.nn.relu(convolve(window[None], conv1_weight, 1) + conv1_bias[:, None, None, None])
        row_ids = lax.broadcasted_iota(jnp.int32, (BY + 1, 1), 0) + band_start - 1
        hidden = hidden * (row_ids >= 0).astype(jnp.float32)
        deepened = jnp.pad(hidden, ((0, 0), (1, 0), (0, 0), (1, 0)))
        return convolve(deepened, conv2_weight, 2) + conv2_bias[:, None, None, None]

    all_bands = lax.map(one_band, jnp.arange(N_GX, dtype=jnp.int32))
    return jnp.transpose(all_bands, (1, 2, 0, 3, 4)).reshape(C2, BZ // 2, grid_rows // 2, grid_cols // 2)
```

```python
import jax
import jax.numpy as jnp
import numpy as np
from jax import lax
from jax.experimental import pallas as pl
from jax.experimental.pallas import tpu as pltpu
from jax.sharding import PartitionSpec as P

BZ = 2
BY = 128
BX = 128
BLK = 2
STRIPS = 64
SY = 16
SX = 128
C1 = 16
C2 = 32

COLS = BX * BLK
HALF = COLS // 2
TOP = 2
SROW = 136
OUT_ROWS = 4
HID_ROWS = 9
WIN = 16
BLOCKS = BY // (2 * OUT_ROWS)
PHASES = 5
K1 = 3 * BZ * WIN
HID = HID_ROWS * C1 * BZ
K2 = 3 * HID
OUTM = OUT_ROWS * C2

EXACT = lax.Precision.HIGHEST
F32 = jnp.float32
BF16 = jnp.bfloat16


def iota(shape, dim):
    return lax.broadcasted_iota(jnp.int32, shape, dim)


def split_kernel(x):
    hi = x.astype(BF16)
    return hi, (x - hi.astype(F32)).astype(BF16)


def split_host(x):
    hi = lax.reduce_precision(x, 8, 7)
    return hi.astype(BF16), (x - hi).astype(BF16)


def pack_body(per_pair, slots, routes, strips, outgoing, outgoing_params, count):
    held = routes.shape[0]
    senders = slots // per_pair

    def clear(i, carry):
        count[i] = 0
        return carry

    lax.fori_loop(0, senders, clear, 0)
    if slots != STRIPS:
        outgoing[...] = jnp.zeros(outgoing.shape, F32)

        def clear_params(i, carry):
            for q in range(8):
                outgoing_params[i, q] = 0
            return carry

        lax.fori_loop(0, slots, clear_params, 0)

    def place(k, carry):
        @pl.when(routes[k, 1] == 1)
        def _():
            dest = routes[k, 0]
            rank = count[dest]
            count[dest] = rank + 1
            slot = jnp.minimum(dest * per_pair + rank, slots - 1)
            outgoing[slot] = strips[k]
            for q in range(8):
                outgoing_params[slot, q] = routes[k, q]

        return carry

    lax.fori_loop(0, held, place, 0)


def pack(strips, routes, senders, per_pair):
    slots = senders * per_pair
    held = strips.shape[0]
    rows = BZ * SY
    return pl.pallas_call(
        lambda *refs: pack_body(per_pair, slots, *refs),
        in_specs=[
            pl.BlockSpec(memory_space=pltpu.SMEM),
            pl.BlockSpec(memory_space=pltpu.VMEM),
        ],
        out_specs=[
            pl.BlockSpec(memory_space=pltpu.VMEM),
            pl.BlockSpec(memory_space=pltpu.SMEM),
        ],
        out_shape=[
            jax.ShapeDtypeStruct((slots, rows, SX), F32),
            jax.ShapeDtypeStruct((slots, 8), jnp.int32),
        ],
        scratch_shapes=[pltpu.SMEM((senders,), jnp.int32)],
        name="pack",
    )(routes, strips.reshape(held, rows, SX))


def join_body(slots, params, columns, strips, joined, right_message, left_message, data, place_y):
    lane = iota((SY, SX), 1)
    sub = iota((SY, SX), 0)
    row_lane = iota((SY, 256), 1)
    row_sub = iota((SY, 256), 0)

    def one(k, carry):
        live = params[k, 1].astype(F32)
        top = params[k, 2]
        left = params[k, 3]
        frac_z = params[k, 4].astype(F32) * (1.0 / 16.0)
        frac_y = params[k, 5].astype(F32) * (1.0 / 16.0)
        frac_x = params[k, 6].astype(F32) * (1.0 / 16.0)
        ramp = params[k, 7]
        weight = jnp.minimum(jnp.minimum(lane + 1, SX - lane), ramp).astype(F32)
        here = weight * (1.0 - frac_x)
        there = jnp.where(lane < SX - 1, weight * frac_x, 0.0)
        stay_z = live * (1.0 - frac_z)
        move_z = live * frac_z
        first = strips[k, :SY, :]
        second = strips[k, SY:, :]
        plane0 = stay_z * first + move_z * second
        plane1 = stay_z * second
        shift = left & (SX - 1)
        for z, plane in enumerate((plane0, plane1)):
            piece = here * plane + there * pltpu.roll(plane, SX - 1, 1)
            turned = pltpu.roll(piece, shift, 1)
            low = jnp.where(lane >= left, turned, 0.0)
            high = jnp.where(lane < left, turned, 0.0)
            for side, part in enumerate((low, high)):
                coarse, fine = split_kernel(part)
                at = z * COLS + side * SX
                data[pl.ds(k * SY, SY), at : at + SX] = coarse
                data[pl.ds(k * SY, SY), BZ * COLS + at : BZ * COLS + at + SX] = fine
        y = row_lane - TOP - top
        weight_y = jnp.minimum(jnp.minimum(y + 1, SY - y), ramp).astype(F32)
        spread = jnp.where(row_sub == y, weight_y * (1.0 - frac_y), 0.0) + jnp.where(
            row_sub == y + 1, weight_y * frac_y, 0.0
        )
        place_y[pl.ds(k * SY, SY), :] = spread.astype(BF16)
        return carry

    lax.fori_loop(0, slots, one, 0, unroll=4)

    live = columns[:, 1:2]
    top = columns[:, 2:3]
    left = columns[:, 3:4]
    ramp = columns[:, 7:8]
    y = iota((slots, 256), 1) - TOP - top
    weight_y = jnp.where((y >= 0) & (y < SY), jnp.minimum(jnp.minimum(y + 1, SY - y), ramp), 0)
    col = iota((slots, COLS), 1)
    x = jnp.where(col < HALF, 2 * col, 2 * (col - HALF) + 1) - left
    weight_x = jnp.where((x >= 0) & (x < SX), jnp.minimum(jnp.minimum(x + 1, SX - x), ramp), 0)
    weight_y = (weight_y * live).astype(F32).astype(BF16)
    weight_x = weight_x.astype(F32).astype(BF16)
    over_rows = (((0,), (0,)), ((), ()))
    total = lax.dot_general(weight_y, weight_x, over_rows, preferred_element_type=F32)[:SROW]
    sums = lax.dot_general(place_y[...], data[...], over_rows, preferred_element_type=F32)[:SROW]
    sums = sums[:, : BZ * COLS] + sums[:, BZ * COLS :]

    src = iota((COLS, COLS), 0)
    dst = iota((COLS, COLS), 1)
    order = (src == jnp.where(dst < HALF, 2 * dst, 2 * (dst - HALF) + 1)).astype(F32).astype(BF16)
    row = iota((SROW, COLS), 0)
    inside = (row >= TOP) & (row < TOP + BY)
    pick_row = iota((8, COLS), 0)
    pick_col = iota((8, COLS), 1)
    pick = jnp.where(
        ((pick_row == 0) & (pick_col == HALF - 1))
        | ((pick_row == 1) & (pick_col == COLS - 1))
        | ((pick_row == 2) & (pick_col == 0)),
        1.0,
        0.0,
    )
    edges = []
    for z in range(BZ):
        coarse, fine = split_kernel(sums[:, z * COLS : (z + 1) * COLS])
        ordered = jnp.dot(coarse, order, preferred_element_type=F32) + jnp.dot(
            fine, order, preferred_element_type=F32
        )
        value = jnp.where(inside, ordered / jnp.where(inside, total, 1.0), 0.0)
        joined[z] = value
        edges.append(
            lax.dot_general(
                pick, value, (((1,), (1,)), ((), ())), precision=EXACT, preferred_element_type=F32
            )
        )
    right_message[...] = jnp.concatenate(edges, axis=0)
    left_message[...] = jnp.concatenate(edges, axis=0)


def join(strips, params):
    slots = params.shape[0]
    vmem = pl.BlockSpec(memory_space=pltpu.VMEM)
    return pl.pallas_call(
        lambda *refs: join_body(slots, *refs),
        in_specs=[pl.BlockSpec(memory_space=pltpu.SMEM), vmem, vmem],
        out_specs=[vmem, vmem, vmem],
        out_shape=[
            jax.ShapeDtypeStruct((BZ, SROW, COLS), F32),
            jax.ShapeDtypeStruct((16, SROW), F32),
            jax.ShapeDtypeStruct((16, SROW), F32),
        ],
        scratch_shapes=[
            pltpu.VMEM((slots * SY, 2 * BZ * COLS), BF16),
            pltpu.VMEM((slots * SY, 256), BF16),
        ],
        compiler_params=pltpu.CompilerParams(vmem_limit_bytes=48 * 2**20),
        name="join",
    )(params, params, strips)


def phases_body(joined, from_left, from_right, phases, down_message, up_message):
    lane = iota((SROW, HALF), 1)
    row16 = iota((16, HALF), 0)
    lane16 = iota((16, HALF), 1)
    over_rows = (((0,), (0,)), ((), ()))
    for z in range(BZ):

        def column(message, row, lane_at):
            pick = jnp.where((row16 == 8 * z + row) & (lane16 == lane_at), 1.0, 0.0)
            return lax.dot_general(
                message[...], pick, over_rows, precision=EXACT, preferred_element_type=F32
            )

        even = joined[z, :, :HALF]
        odd = joined[z, :, HALF:]
        parts = (
            jnp.where(lane == 0, column(from_left, 0, 0), pltpu.roll(even, 1, 1)),
            jnp.where(lane == 0, column(from_left, 1, 0), pltpu.roll(odd, 1, 1)),
            even,
            odd,
            jnp.where(lane == HALF - 1, column(from_right, 2, HALF - 1), pltpu.roll(even, HALF - 1, 1)),
        )
        for j, part in enumerate(parts):
            phases[j, z] = part
            down_message[j, z] = part[BY : BY + 8]
            up_message[j, z] = part[0:8]


def make_phases(joined, from_left, from_right):
    vmem = pl.BlockSpec(memory_space=pltpu.VMEM)
    return pl.pallas_call(
        phases_body,
        in_specs=[vmem, vmem, vmem],
        out_specs=[vmem, vmem, vmem],
        out_shape=[
            jax.ShapeDtypeStruct((PHASES, BZ, SROW, HALF), F32),
            jax.ShapeDtypeStruct((PHASES, BZ, 8, HALF), F32),
            jax.ShapeDtypeStruct((PHASES, BZ, 8, HALF), F32),
        ],
        name="phases",
    )(joined, from_left, from_right)


def conv_body(edge, from_above, from_below, phases_in, first, second, bias, out, phases, coarse_h, fine_h):
    row8 = iota((8, HALF), 0)
    for j in range(PHASES):
        for z in range(BZ):
            phases[j, z, 8 : SROW - 8, :] = phases_in[j, z, 8 : SROW - 8, :]
            phases[j, z, 0:8, :] = jnp.where(row8 < TOP, from_above[j, z], phases_in[j, z, 0:8, :])
            below = jnp.where(row8 == 2, from_below[j, z], 0.0)
            phases[j, z, SROW - 8 : SROW, :] = jnp.where(
                row8 < 2, phases_in[j, z, SROW - 8 : SROW, :], below
            )
    no_row = edge[0] == 0
    no_col = edge[1] == 0
    lane = iota((HID, 256), 1)
    hid_row = iota((HID, 256), 0)
    ones = jnp.ones((16, 256), BF16)

    def pair(step, carry):
        blocks = (step, step + BLOCKS // 2)
        wide = {}
        for j in range(PHASES):
            for z in range(BZ):
                cut = [
                    phases[j, z, pl.ds(pl.multiple_of(8 * b, 8), WIN), :] for b in blocks
                ]
                wide[j, z] = split_kernel(jnp.concatenate(cut, axis=1))
        for group in range(3):
            coarse = [wide[group + dx, z][0] for dx in range(3) for z in range(BZ)]
            fine = [wide[group + dx, z][1] for dx in range(3) for z in range(BZ)]
            stacked = jnp.concatenate(coarse + fine + coarse + [ones], axis=0)
            hidden = jnp.dot(first[...], stacked, preferred_element_type=F32)
            hidden = jnp.maximum(hidden, 0.0)
            outside = no_row & (step == 0) & (hid_row < C1 * BZ) & (lane < HALF)
            if group == 0:
                outside = outside | (no_col & ((lane & (HALF - 1)) == 0))
            hidden = jnp.where(outside, 0.0, hidden)
            coarse, fine = split_kernel(hidden)
            coarse_h[group * HID : (group + 1) * HID, :] = coarse
            fine_h[group * HID : (group + 1) * HID, :] = fine
        both = jnp.dot(second[...], coarse_h[...], preferred_element_type=F32)
        rest = jnp.dot(second[:OUTM, :], fine_h[...], preferred_element_type=F32)
        result = both[:OUTM] + both[OUTM:] + rest
        for side, b in enumerate(blocks):
            for r in range(OUT_ROWS):
                at = OUT_ROWS * b + r
                out[pl.ds(at, C2, stride=BY // 2), :] = (
                    result[r * C2 : (r + 1) * C2, side * HALF : (side + 1) * HALF] + bias[...]
                )
        return carry

    lax.fori_loop(0, BLOCKS // 2, pair, 0)


def convolve(edge, from_above, from_below, phases, first, second, bias):
    vmem = pl.BlockSpec(memory_space=pltpu.VMEM)
    return pl.pallas_call(
        conv_body,
        in_specs=[pl.BlockSpec(memory_space=pltpu.SMEM)] + [vmem] * 6,
        out_specs=vmem,
        out_shape=jax.ShapeDtypeStruct((C2 * BY // 2, HALF), F32),
        scratch_shapes=[
            pltpu.VMEM((PHASES, BZ, SROW, HALF), F32),
            pltpu.VMEM((K2, 256), BF16),
            pltpu.VMEM((K2, 256), BF16),
        ],
        compiler_params=pltpu.CompilerParams(vmem_limit_bytes=48 * 2**20),
        name="convolve",
    )(edge, from_above, from_below, phases, first, second, bias)


def first_table(weight, bias):
    kernel = weight[:, 0]
    planes = jnp.stack([kernel[:, 1:3], kernel[:, 0:2]], axis=1)
    reach = np.zeros((HID_ROWS, 3, WIN), np.float32)
    for i in range(HID_ROWS):
        for dy in range(3):
            reach[i, dy, i + dy] = 1.0
    table = jnp.einsum("czpyx,iys->iczxps", planes, jnp.asarray(reach), precision=EXACT)
    coarse, fine = split_host(table.reshape(HID, K1))
    each = jnp.tile(jnp.repeat(bias, BZ), HID_ROWS)
    one = lax.reduce_precision(each, 8, 7)
    two = lax.reduce_precision(each - one, 8, 7)
    three = each - one - two
    tail = jnp.stack([one, two, three], axis=1).astype(BF16)
    tail = jnp.pad(tail, ((0, 0), (0, 16 - 3)))
    return jnp.concatenate([coarse, coarse, fine, tail], axis=1)


def second_table(weight):
    reach = np.zeros((OUT_ROWS, 3, HID_ROWS), np.float32)
    for i in range(OUT_ROWS):
        for dy in range(3):
            reach[i, dy, 2 * i + dy] = 1.0
    table = jnp.einsum("oczyx,iyh->ioxhcz", weight[:, :, 1:3], jnp.asarray(reach), precision=EXACT)
    coarse, fine = split_host(table.reshape(OUTM, K2))
    return jnp.concatenate([coarse, fine], axis=0)


def shift(values, axis, by):
    length = lax.axis_size(axis)
    pairs = [(i, i + by) for i in range(length) if 0 <= i + by < length]
    return lax.ppermute(values, axis, pairs)


def body(strips, routes, conv1_weight, conv1_bias, conv2_weight, conv2_bias):
    senders = lax.axis_size("gx") * lax.axis_size("gy")
    per_pair = max(1, STRIPS // senders)
    outgoing, outgoing_params = pack(strips, routes, senders, per_pair)
    axes = ("gx", "gy")
    arrived = lax.all_to_all(outgoing, axes, split_axis=0, concat_axis=0, tiled=True)
    arrived_params = lax.all_to_all(outgoing_params, axes, split_axis=0, concat_axis=0, tiled=True)
    first = first_table(conv1_weight, conv1_bias)
    second = second_table(conv2_weight)
    bias = jnp.broadcast_to(conv2_bias[:, None], (C2, HALF))
    edge = jnp.stack([lax.axis_index("gx"), lax.axis_index("gy")]).astype(jnp.int32)

    joined, right_message, left_message = join(arrived, arrived_params)
    from_left = shift(right_message, "gy", 1)
    from_right = shift(left_message, "gy", -1)
    phases, down_message, up_message = make_phases(joined, from_left, from_right)
    from_above = shift(down_message, "gx", 1)
    from_below = shift(up_message, "gx", -1)
    features = convolve(edge, from_above, from_below, phases, first, second, bias)
    return features.reshape(C2, 1, BY // 2, HALF)


def solution(mesh):
    in_specs = (P(("gx", "gy"), None, None, None), P(("gx", "gy"), None), P(), P(), P(), P())
    out_specs = P(None, None, "gx", "gy")
    return jax.shard_map(body, mesh=mesh, in_specs=in_specs, out_specs=out_specs, check_vma=False)
```

```python
import jax
import jax.numpy as jnp
import numpy as np
from jax import lax
from jax.experimental import pallas as pl
from jax.experimental.pallas import tpu as pltpu
from jax.sharding import PartitionSpec as P

BZ = 2
BY = 128
BX = 128
BLK = 2
STRIPS = 64
SY = 16
SX = 128
C1 = 16
C2 = 32

COLS = BX * BLK
HALF = COLS // 2
TOP = 2
SROW = 136
OUT_ROWS = 4
HID_ROWS = 9
WIN = 16
BLOCKS = BY // (2 * OUT_ROWS)
PHASES = 5
K1 = 3 * BZ * WIN
HID = HID_ROWS * C1 * BZ
K2 = 3 * HID
OUTM = OUT_ROWS * C2

EXACT = lax.Precision.HIGHEST
F32 = jnp.float32
BF16 = jnp.bfloat16


def iota(shape, dim):
    return lax.broadcasted_iota(jnp.int32, shape, dim)


def split_kernel(x):
    hi = x.astype(BF16)
    return hi, (x - hi.astype(F32)).astype(BF16)


def split_host(x):
    hi = lax.reduce_precision(x, 8, 7)
    return hi.astype(BF16), (x - hi).astype(BF16)


def chunk_of(per_pair):
    return BZ * SY // 2 * per_pair + 1


def pack_body(per_pair, routes, route_rows, strips, payload, count, sems):
    pairs = BZ * SY // 2
    chunk = chunk_of(per_pair)
    held = route_rows.shape[1]
    senders = payload.shape[0] // chunk
    full = held == STRIPS

    def clear(i, carry):
        count[i] = 0
        return carry

    lax.fori_loop(0, senders, clear, 0, unroll=8)

    def copy(k, at):
        source = strips.at[pl.ds(k * pairs, pairs)]
        return pltpu.make_async_copy(source, payload.at[pl.ds(at, pairs)], sems.at[0 if full else k])

    def when_live(k, run):
        if full:
            run()
        else:
            pl.when(routes[1, k] == 1)(run)

    def place(k, carry):
        def run():
            dest = routes[0, k]
            rank = jnp.minimum(count[dest], per_pair - 1)
            count[dest] = rank + 1
            copy(k, dest * chunk + rank * pairs).start()

        when_live(k, run)
        return carry

    lax.fori_loop(0, held, place, 0, unroll=8)

    match = (route_rows[0:1, :] == iota((senders, held), 0)) & (route_rows[1:2, :] == 1)
    flags = jnp.where(match, 1.0, 0.0)
    before = jnp.where(iota((held, held), 0) < iota((held, held), 1), 1.0, 0.0)
    earlier = jnp.dot(flags.astype(BF16), before.astype(BF16), preferred_element_type=F32)
    fields = jnp.concatenate([route_rows[...].astype(F32), jnp.zeros((120, held), F32)], axis=0)
    fields = fields.astype(BF16)
    for r in range(per_pair):
        chosen = jnp.where(match & (earlier == float(r)), 1.0, 0.0).astype(BF16)
        sent = lax.dot_general(
            chosen, fields, (((1,), (1,)), ((), ())), preferred_element_type=F32
        )
        for dest in range(senders):
            payload[dest * chunk + chunk - 1, r : r + 1, :] = sent[dest : dest + 1, :]

    if full:
        everything = held * pairs
        pltpu.make_async_copy(strips, payload.at[pl.ds(0, everything)], sems.at[0]).wait()
    else:

        def finish(k, carry):
            when_live(k, lambda: copy(k, 0).wait())
            return carry

        lax.fori_loop(0, held, finish, 0)


def pack(strips, routes_t, senders, per_pair):
    held = strips.shape[0]
    pairs = BZ * SY // 2
    vmem = pl.BlockSpec(memory_space=pltpu.VMEM)
    return pl.pallas_call(
        lambda *refs: pack_body(per_pair, *refs),
        in_specs=[
            pl.BlockSpec(memory_space=pltpu.SMEM),
            vmem,
            pl.BlockSpec(memory_space=pl.ANY),
        ],
        out_specs=vmem,
        out_shape=jax.ShapeDtypeStruct((senders * chunk_of(per_pair), 2, SX), F32),
        scratch_shapes=[
            pltpu.SMEM((senders,), jnp.int32),
            pltpu.SemaphoreType.DMA((1 if held == STRIPS else held,)),
        ],
        name="pack",
    )(routes_t, routes_t, strips.reshape(held * pairs, 2, SX))


def join_body(per_pair, grid, edge, routes, strips, joined, messages, data, place_y, params, sem):
    senders = routes.shape[0]
    slots = senders * per_pair
    chunk = 2 * chunk_of(per_pair)
    fetch = pltpu.make_async_copy(routes.at[:, chunk_of(per_pair) - 1], params, sem)
    fetch.start()
    fetch.wait()
    lane = iota((SY, SX), 1)
    sub = iota((SY, SX), 0)
    row_lane = iota((SY, 256), 1)
    row_sub = iota((SY, 256), 0)

    def one(h, r):
        k = h * per_pair + r
        live = params[h, r, 1].astype(jnp.int32)
        top = params[h, r, 2].astype(jnp.int32)
        left = params[h, r, 3].astype(jnp.int32)
        frac_z = params[h, r, 4] * (1.0 / 16.0)
        frac_y = params[h, r, 5] * (1.0 / 16.0)
        frac_x = params[h, r, 6] * (1.0 / 16.0)
        ramp = params[h, r, 7].astype(jnp.int32)
        weight = jnp.minimum(jnp.minimum(lane + 1, SX - lane), ramp).astype(F32)
        here = weight * (1.0 - frac_x)
        there = jnp.where(lane < SX - 1, weight * frac_x, 0.0)
        stay_z = 1.0 - frac_z
        move_z = frac_z
        at = h * chunk + r * BZ * SY
        first = strips[pl.ds(at, SY), :]
        second = strips[pl.ds(at + SY, SY), :]
        if slots != STRIPS:
            first = jnp.where(live == 1, first, 0.0)
            second = jnp.where(live == 1, second, 0.0)
        plane0 = stay_z * first + move_z * second
        plane1 = stay_z * second
        shift = left & (SX - 1)
        for z, plane in enumerate((plane0, plane1)):
            piece = here * plane + there * pltpu.roll(plane, SX - 1, 1)
            turned = pltpu.roll(piece, shift, 1)
            low = jnp.where(lane >= left, turned, 0.0)
            high = jnp.where(lane < left, turned, 0.0)
            for side, part in enumerate((low, high)):
                coarse, fine = split_kernel(part)
                at = z * COLS + side * SX
                data[pl.ds(k * SY, SY), at : at + SX] = coarse
                data[pl.ds(k * SY, SY), BZ * COLS + at : BZ * COLS + at + SX] = fine
        y = row_lane - TOP - top
        weight_y = jnp.minimum(jnp.minimum(y + 1, SY - y), ramp).astype(F32)
        spread = jnp.where(row_sub == y, weight_y * (1.0 - frac_y), 0.0) + jnp.where(
            row_sub == y + 1, weight_y * frac_y, 0.0
        )
        place_y[pl.ds(k * SY, SY), :] = spread.astype(BF16)

    def holder(h, carry):
        for r in range(per_pair):
            one(h, r)
        return carry

    lax.fori_loop(0, senders, holder, 0, unroll=4 // per_pair)

    columns = jnp.concatenate(
        [strips[pl.ds(chunk - 2 + r, senders, stride=chunk), :] for r in range(per_pair)], axis=0
    ).astype(jnp.int32)

    def field(q):
        return columns[:, q : q + 1]

    live = field(1)
    top = field(2)
    left = field(3)
    ramp = field(7)
    y = iota((slots, 256), 1) - TOP - top
    weight_y = jnp.where((y >= 0) & (y < SY), jnp.minimum(jnp.minimum(y + 1, SY - y), ramp), 0)
    col = iota((slots, COLS), 1)
    x = jnp.where(col < HALF, 2 * col, 2 * (col - HALF) + 1) - left
    weight_x = jnp.where((x >= 0) & (x < SX), jnp.minimum(jnp.minimum(x + 1, SX - x), ramp), 0)
    weight_y = jnp.where(live == 1, weight_y, 0).astype(F32).astype(BF16)
    weight_x = weight_x.astype(F32).astype(BF16)
    over_rows = (((0,), (0,)), ((), ()))
    total = lax.dot_general(weight_y, weight_x, over_rows, preferred_element_type=F32)[:SROW]
    sums = lax.dot_general(place_y[...], data[...], over_rows, preferred_element_type=F32)[:SROW]
    sums = sums[:, : BZ * COLS] + sums[:, BZ * COLS :]

    src = iota((COLS, COLS), 0)
    dst = iota((COLS, COLS), 1)
    order = (src == jnp.where(dst < HALF, 2 * dst, 2 * (dst - HALF) + 1)).astype(F32).astype(BF16)
    row = iota((SROW, COLS), 0)
    inside = (row >= TOP) & (row < TOP + BY)
    pick_row = iota((8, COLS), 0)
    pick_col = iota((8, COLS), 1)
    pick = jnp.where(
        ((pick_row == 0) & (pick_col == HALF - 1))
        | ((pick_row == 1) & (pick_col == COLS - 1))
        | ((pick_row == 2) & (pick_col == 0)),
        1.0,
        0.0,
    )
    right_rows = []
    left_rows = []
    down_rows = []
    up_rows = []
    for z in range(BZ):
        coarse, fine = split_kernel(sums[:, z * COLS : (z + 1) * COLS])
        ordered = jnp.dot(coarse, order, preferred_element_type=F32) + jnp.dot(
            fine, order, preferred_element_type=F32
        )
        value = jnp.where(inside, ordered / jnp.where(inside, total, 1.0), 0.0)
        joined[z] = value
        columns_as_rows = lax.dot_general(
            pick, value, (((1,), (1,)), ((), ())), precision=EXACT, preferred_element_type=F32
        )[:, TOP : TOP + BY]
        right_rows.append(columns_as_rows[0:2])
        left_rows.append(columns_as_rows[2:3])
        for half in range(2):
            cut = value[:, half * HALF : (half + 1) * HALF]
            down_rows.append(cut[BY : BY + 2])
            up_rows.append(cut[TOP : TOP + 1])

    def tile(rows):
        have = sum(r.shape[0] for r in rows)
        if have < 8:
            rows = rows + [jnp.zeros((8 - have, HALF), F32)]
        return jnp.concatenate(rows, axis=0)

    right = tile(right_rows)
    left = tile(left_rows)
    down = tile(down_rows)
    up = tile(up_rows)
    at_row = edge[0]
    at_col = edge[1]
    rows, cols = grid

    def send(dy, dx, values):
        to_row = at_row + dy
        to_col = at_col + dx

        @pl.when((to_row >= 0) & (to_row < rows) & (to_col >= 0) & (to_col < cols))
        def _():
            messages[to_row * cols + to_col] = values

    for dy in (-1, 0, 1):
        send(dy, 1, right)
        send(dy, -1, left)
    send(1, 0, down)
    send(-1, 0, up)


def join(grid, edge, arrived, per_pair):
    senders = arrived.shape[0] // chunk_of(per_pair)
    slots = senders * per_pair
    vmem = pl.BlockSpec(memory_space=pltpu.VMEM)
    return pl.pallas_call(
        lambda *refs: join_body(per_pair, grid, *refs),
        in_specs=[pl.BlockSpec(memory_space=pltpu.SMEM), pl.BlockSpec(memory_space=pl.ANY), vmem],
        out_specs=[vmem, vmem],
        out_shape=[
            jax.ShapeDtypeStruct((BZ, SROW, COLS), F32),
            jax.ShapeDtypeStruct((senders, 8, HALF), F32),
        ],
        scratch_shapes=[
            pltpu.VMEM((slots * SY, 2 * BZ * COLS), BF16),
            pltpu.VMEM((slots * SY, 256), BF16),
            pltpu.SMEM((senders, 2, SX), F32),
            pltpu.SemaphoreType.DMA,
        ],
        compiler_params=pltpu.CompilerParams(vmem_limit_bytes=48 * 2**20),
        name="join",
    )(
        edge,
        arrived.reshape(senders, chunk_of(per_pair), 2, SX),
        arrived.reshape(arrived.shape[0] * 2, SX),
    )


def conv_body(grid, edge, joined, received, first, second, bias, out, phases, coarse_h, fine_h):
    at_row = edge[0]
    at_col = edge[1]
    rows, cols = grid
    halo = {}
    for dy in (-1, 0, 1):
        for dx in (-1, 0, 1):
            if (dy, dx) == (0, 0):
                continue
            row = at_row + dy
            col = at_col + dx
            there = (row >= 0) & (row < rows) & (col >= 0) & (col < cols)
            index = jnp.where(there, row * cols + col, 0)
            halo[dy, dx] = jnp.where(there, received[index], 0.0)
    wide_lane = iota((8, 256), 1)

    def along(above, here, below):
        zero = jnp.zeros((8, 128), F32)
        turned = [
            pltpu.roll(jnp.concatenate([part, zero], axis=1), by, 1)
            for part, by in ((above, 256 - (BY - TOP)), (here, TOP), (below, TOP + BY))
        ]
        low = jnp.where(wide_lane < TOP, turned[0], turned[1])
        return jnp.where(
            wide_lane < TOP + BY, low, jnp.where(wide_lane == TOP + BY, turned[2], 0.0)
        )

    from_left = along(halo[-1, -1], halo[0, -1], halo[1, -1])
    from_right = along(halo[-1, 1], halo[0, 1], halo[1, 1])
    from_above = halo[-1, 0]
    from_below = halo[1, 0]
    pick_row = iota((8, HALF), 0)
    pick_lane = iota((8, HALF), 1)
    tall_lane = iota((SROW, HALF), 1)
    row8 = iota((8, HALF), 0)

    def column(message, row, lane_at):
        chosen = jnp.where((pick_row == row) & (pick_lane == lane_at), 1.0, 0.0)
        return lax.dot_general(
            message, chosen, (((0,), (0,)), ((), ())), precision=EXACT, preferred_element_type=F32
        )[:SROW]

    for z in range(BZ):
        halves = []
        for half in range(2):
            own = joined[z, :, half * HALF : (half + 1) * HALF]
            at = 4 * z + 2 * half
            above = jnp.concatenate([from_above[at : at + 2], own[2:8]], axis=0)
            at = 2 * z + half
            below = jnp.concatenate(
                [own[SROW - 8 : SROW - 6], from_below[at : at + 1], jnp.zeros((5, HALF), F32)], axis=0
            )
            halves.append(jnp.concatenate([above, own[8 : SROW - 8], below], axis=0))
        even, odd = halves
        phases[0, z] = jnp.where(tall_lane == 0, column(from_left, 2 * z, 0), pltpu.roll(even, 1, 1))
        phases[1, z] = jnp.where(tall_lane == 0, column(from_left, 2 * z + 1, 0), pltpu.roll(odd, 1, 1))
        phases[2, z] = even
        phases[3, z] = odd
        phases[4, z] = jnp.where(
            tall_lane == HALF - 1, column(from_right, z, HALF - 1), pltpu.roll(even, HALF - 1, 1)
        )
    no_row = edge[0] == 0
    no_col = edge[1] == 0
    lane = iota((HID, 256), 1)
    hid_row = iota((HID, 256), 0)
    ones = jnp.ones((16, 256), BF16)

    def pair(step, carry):
        blocks = (step, step + BLOCKS // 2)
        wide = {}
        for j in range(PHASES):
            for z in range(BZ):
                cut = [
                    phases[j, z, pl.ds(pl.multiple_of(8 * b, 8), WIN), :] for b in blocks
                ]
                wide[j, z] = split_kernel(jnp.concatenate(cut, axis=1))
        for group in range(3):
            coarse = [wide[group + dx, z][0] for dx in range(3) for z in range(BZ)]
            fine = [wide[group + dx, z][1] for dx in range(3) for z in range(BZ)]
            stacked = jnp.concatenate(coarse + fine + coarse + [ones], axis=0)
            hidden = jnp.dot(first[...], stacked, preferred_element_type=F32)
            hidden = jnp.maximum(hidden, 0.0)
            outside = no_row & (step == 0) & (hid_row < C1 * BZ) & (lane < HALF)
            if group == 0:
                outside = outside | (no_col & ((lane & (HALF - 1)) == 0))
            hidden = jnp.where(outside, 0.0, hidden)
            coarse, fine = split_kernel(hidden)
            coarse_h[group * HID : (group + 1) * HID, :] = coarse
            fine_h[group * HID : (group + 1) * HID, :] = fine
        both = jnp.dot(second[...], coarse_h[...], preferred_element_type=F32)
        rest = jnp.dot(second[:OUTM, :], fine_h[...], preferred_element_type=F32)
        result = both[:OUTM] + both[OUTM:] + rest
        for side, b in enumerate(blocks):
            for r in range(OUT_ROWS):
                at = OUT_ROWS * b + r
                out[pl.ds(at, C2, stride=BY // 2), :] = (
                    result[r * C2 : (r + 1) * C2, side * HALF : (side + 1) * HALF] + bias[...]
                )
        return carry

    lax.fori_loop(0, BLOCKS // 2, pair, 0)


def convolve(grid, edge, joined, received, first, second, bias):
    vmem = pl.BlockSpec(memory_space=pltpu.VMEM)
    return pl.pallas_call(
        lambda *refs: conv_body(grid, *refs),
        in_specs=[pl.BlockSpec(memory_space=pltpu.SMEM)] + [vmem] * 5,
        out_specs=vmem,
        out_shape=jax.ShapeDtypeStruct((C2 * BY // 2, HALF), F32),
        scratch_shapes=[
            pltpu.VMEM((PHASES, BZ, SROW, HALF), F32),
            pltpu.VMEM((K2, 256), BF16),
            pltpu.VMEM((K2, 256), BF16),
        ],
        compiler_params=pltpu.CompilerParams(vmem_limit_bytes=48 * 2**20),
        name="convolve",
    )(edge, joined, received, first, second, bias)


def first_table(weight, bias):
    kernel = weight[:, 0]
    planes = jnp.stack([kernel[:, 1:3], kernel[:, 0:2]], axis=1)
    reach = np.zeros((HID_ROWS, 3, WIN), np.float32)
    for i in range(HID_ROWS):
        for dy in range(3):
            reach[i, dy, i + dy] = 1.0
    table = jnp.einsum("czpyx,iys->iczxps", planes, jnp.asarray(reach), precision=EXACT)
    coarse, fine = split_host(table.reshape(HID, K1))
    each = jnp.tile(jnp.repeat(bias, BZ), HID_ROWS)
    one = lax.reduce_precision(each, 8, 7)
    two = lax.reduce_precision(each - one, 8, 7)
    three = each - one - two
    tail = jnp.stack([one, two, three], axis=1).astype(BF16)
    tail = jnp.pad(tail, ((0, 0), (0, 16 - 3)))
    return jnp.concatenate([coarse, coarse, fine, tail], axis=1)


def second_table(weight):
    reach = np.zeros((OUT_ROWS, 3, HID_ROWS), np.float32)
    for i in range(OUT_ROWS):
        for dy in range(3):
            reach[i, dy, 2 * i + dy] = 1.0
    table = jnp.einsum("oczyx,iyh->ioxhcz", weight[:, :, 1:3], jnp.asarray(reach), precision=EXACT)
    coarse, fine = split_host(table.reshape(OUTM, K2))
    return jnp.concatenate([coarse, fine], axis=0)


def body(strips, routes, conv1_weight, conv1_bias, conv2_weight, conv2_bias):
    rows = lax.axis_size("gx")
    cols = lax.axis_size("gy")
    senders = rows * cols
    per_pair = max(1, STRIPS // senders)
    axes = ("gx", "gy")
    at_row = lax.axis_index("gx").astype(jnp.int32)
    at_col = lax.axis_index("gy").astype(jnp.int32)
    edge = jnp.stack([at_row, at_col])
    routes_t = routes.T
    outgoing = pack(strips, routes_t, senders, per_pair)
    arrived = lax.all_to_all(outgoing, axes, split_axis=0, concat_axis=0, tiled=True)
    first = first_table(conv1_weight, conv1_bias)
    second = second_table(conv2_weight)
    bias = jnp.broadcast_to(conv2_bias[:, None], (C2, HALF))
    joined, messages = join((rows, cols), edge, arrived, per_pair)
    received = lax.all_to_all(messages, axes, split_axis=0, concat_axis=0, tiled=True)
    features = convolve((rows, cols), edge, joined, received, first, second, bias)
    return features.reshape(C2, 1, BY // 2, HALF)


def solution(mesh):
    in_specs = (P(("gx", "gy"), None, None, None), P(("gx", "gy"), None), P(), P(), P(), P())
    out_specs = P(None, None, "gx", "gy")
    return jax.shard_map(body, mesh=mesh, in_specs=in_specs, out_specs=out_specs, check_vma=False)
```

```python
import jax
import jax.numpy as jnp
import numpy as np
from jax import lax
from jax.experimental import pallas as pl
from jax.experimental.pallas import tpu as pltpu
from jax.sharding import PartitionSpec as P

BZ = 2
BY = 128
BX = 128
BLK = 2
STRIPS = 64
SY = 16
SX = 128
C1 = 16
C2 = 32

COLS = BX * BLK
HALF = COLS // 2
TOP = 2
SROW = 136
OUT_ROWS = 4
HID_ROWS = 9
WIN = 16
BLOCKS = BY // (2 * OUT_ROWS)
PHASES = 5
UNROLL = 8
JOIN_UNROLL = 8
K1 = 3 * BZ * WIN
HID = HID_ROWS * C1 * BZ
K2 = 3 * HID
OUTM = OUT_ROWS * C2

EXACT = lax.Precision.HIGHEST
F32 = jnp.float32
BF16 = jnp.bfloat16


def iota(shape, dim):
    return lax.broadcasted_iota(jnp.int32, shape, dim)


def split_kernel(x):
    hi = x.astype(BF16)
    return hi, (x - hi.astype(F32)).astype(BF16)


def split_host(x):
    hi = lax.reduce_precision(x, 8, 7)
    return hi.astype(BF16), (x - hi).astype(BF16)


def chunk_of(per_pair):
    return BZ * SY // 2 * per_pair + 1


def pack_body(per_pair, routes, route_rows, strips, payload, count, sems):
    pairs = BZ * SY // 2
    chunk = chunk_of(per_pair)
    held = route_rows.shape[1]
    senders = payload.shape[0] // chunk
    full = held == STRIPS

    def clear(i, carry):
        count[i] = 0
        return carry

    lax.fori_loop(0, senders, clear, 0, unroll=8)

    def copy(k, at):
        source = strips.at[pl.ds(k * pairs, pairs)]
        return pltpu.make_async_copy(source, payload.at[pl.ds(at, pairs)], sems.at[0 if full else k])

    def when_live(k, run):
        if full:
            run()
        else:
            pl.when(routes[1, k] == 1)(run)

    def place(k, carry):
        def run():
            dest = routes[0, k]
            rank = jnp.minimum(count[dest], per_pair - 1)
            count[dest] = rank + 1
            copy(k, dest * chunk + rank * pairs).start()

        when_live(k, run)
        return carry

    lax.fori_loop(0, held, place, 0, unroll=8)

    match = (route_rows[0:1, :] == iota((senders, held), 0)) & (route_rows[1:2, :] == 1)
    flags = jnp.where(match, 1.0, 0.0)
    before = jnp.where(iota((held, held), 0) < iota((held, held), 1), 1.0, 0.0)
    earlier = jnp.dot(flags.astype(BF16), before.astype(BF16), preferred_element_type=F32)
    fields = jnp.concatenate([route_rows[...].astype(F32), jnp.zeros((120, held), F32)], axis=0)
    fields = fields.astype(BF16)
    for r in range(per_pair):
        chosen = jnp.where(match & (earlier == float(r)), 1.0, 0.0).astype(BF16)
        sent = lax.dot_general(
            chosen, fields, (((1,), (1,)), ((), ())), preferred_element_type=F32
        )
        for dest in range(senders):
            payload[dest * chunk + chunk - 1, r : r + 1, :] = sent[dest : dest + 1, :]

    if full:
        everything = held * pairs
        pltpu.make_async_copy(strips, payload.at[pl.ds(0, everything)], sems.at[0]).wait()
    else:

        def finish(k, carry):
            when_live(k, lambda: copy(k, 0).wait())
            return carry

        lax.fori_loop(0, held, finish, 0)


def pack(strips, routes_t, senders, per_pair):
    held = strips.shape[0]
    pairs = BZ * SY // 2
    vmem = pl.BlockSpec(memory_space=pltpu.VMEM)
    return pl.pallas_call(
        lambda *refs: pack_body(per_pair, *refs),
        in_specs=[
            pl.BlockSpec(memory_space=pltpu.SMEM),
            vmem,
            pl.BlockSpec(memory_space=pl.ANY),
        ],
        out_specs=vmem,
        out_shape=jax.ShapeDtypeStruct((senders * chunk_of(per_pair), 2, SX), F32),
        scratch_shapes=[
            pltpu.SMEM((senders,), jnp.int32),
            pltpu.SemaphoreType.DMA((1 if held == STRIPS else held,)),
        ],
        name="pack",
    )(routes_t, routes_t, strips.reshape(held * pairs, 2, SX))


def join_body(per_pair, grid, edge, routes, strips, joined, messages, data, place_y, params, sem):
    senders = routes.shape[0]
    slots = senders * per_pair
    chunk = 2 * chunk_of(per_pair)
    fetch = pltpu.make_async_copy(routes.at[:, chunk_of(per_pair) - 1], params, sem)
    fetch.start()
    columns = jnp.concatenate(
        [strips[pl.ds(chunk - 2 + r, senders, stride=chunk), :] for r in range(per_pair)], axis=0
    ).astype(jnp.int32)

    def field(q):
        return columns[:, q : q + 1]

    live = field(1)
    top = field(2)
    left = field(3)
    ramp = field(7)
    y = iota((slots, 256), 1) - TOP - top
    weight_y = jnp.where((y >= 0) & (y < SY), jnp.minimum(jnp.minimum(y + 1, SY - y), ramp), 0)
    col = iota((slots, COLS), 1)
    x = jnp.where(col < HALF, 2 * col, 2 * (col - HALF) + 1) - left
    weight_x = jnp.where((x >= 0) & (x < SX), jnp.minimum(jnp.minimum(x + 1, SX - x), ramp), 0)
    weight_y = jnp.where(live == 1, weight_y, 0).astype(F32).astype(BF16)
    weight_x = weight_x.astype(F32).astype(BF16)
    over_rows = (((0,), (0,)), ((), ()))
    total = lax.dot_general(weight_y, weight_x, over_rows, preferred_element_type=F32)[:SROW]
    fetch.wait()
    lane = iota((SY, SX), 1)
    row_lane = iota((SY, 256), 1)
    row_sub = iota((SY, 256), 0)

    def one(h, r):
        k = h * per_pair + r
        live = params[h, r, 1].astype(jnp.int32)
        top = params[h, r, 2].astype(jnp.int32)
        left = params[h, r, 3].astype(jnp.int32)
        frac_z = params[h, r, 4] * (1.0 / 16.0)
        frac_y = params[h, r, 5] * (1.0 / 16.0)
        frac_x = params[h, r, 6] * (1.0 / 16.0)
        ramp = params[h, r, 7].astype(jnp.int32)
        weight = jnp.minimum(jnp.minimum(lane + 1, SX - lane), ramp).astype(F32)
        here = weight * (1.0 - frac_x)
        there = jnp.where(lane < SX - 1, weight * frac_x, 0.0)
        stay_z = 1.0 - frac_z
        move_z = frac_z
        at = h * chunk + r * BZ * SY
        first = strips[pl.ds(at, SY), :]
        second = strips[pl.ds(at + SY, SY), :]
        if slots != STRIPS:
            first = jnp.where(live == 1, first, 0.0)
            second = jnp.where(live == 1, second, 0.0)
        plane0 = stay_z * first + move_z * second
        plane1 = stay_z * second
        shift = left & (SX - 1)
        for z, plane in enumerate((plane0, plane1)):
            piece = here * plane + there * pltpu.roll(plane, SX - 1, 1)
            turned = pltpu.roll(piece, shift, 1)
            low = jnp.where(lane >= left, turned, 0.0)
            high = jnp.where(lane < left, turned, 0.0)
            for side, part in enumerate((low, high)):
                coarse, fine = split_kernel(part)
                at = z * COLS + side * SX
                data[pl.ds(k * SY, SY), at : at + SX] = coarse
                data[pl.ds(k * SY, SY), BZ * COLS + at : BZ * COLS + at + SX] = fine
        y = row_lane - TOP - top
        weight_y = jnp.minimum(jnp.minimum(y + 1, SY - y), ramp).astype(F32)
        spread = jnp.where(row_sub == y, weight_y * (1.0 - frac_y), 0.0) + jnp.where(
            row_sub == y + 1, weight_y * frac_y, 0.0
        )
        place_y[pl.ds(k * SY, SY), :] = spread.astype(BF16)

    def holder(h, carry):
        for r in range(per_pair):
            one(h, r)
        return carry

    lax.fori_loop(0, senders, holder, 0, unroll=JOIN_UNROLL)

    sums = lax.dot_general(place_y[...], data[...], over_rows, preferred_element_type=F32)[:SROW]
    sums = sums[:, : BZ * COLS] + sums[:, BZ * COLS :]

    src = iota((COLS, COLS), 0)
    dst = iota((COLS, COLS), 1)
    order = (src == jnp.where(dst < HALF, 2 * dst, 2 * (dst - HALF) + 1)).astype(F32).astype(BF16)
    row = iota((SROW, COLS), 0)
    inside = (row >= TOP) & (row < TOP + BY)
    pick_row = iota((8, COLS), 0)
    pick_col = iota((8, COLS), 1)
    pick = jnp.where(
        ((pick_row == 0) & (pick_col == HALF - 1))
        | ((pick_row == 1) & (pick_col == COLS - 1))
        | ((pick_row == 2) & (pick_col == 0)),
        1.0,
        0.0,
    )
    right_rows = []
    left_rows = []
    down_rows = []
    up_rows = []
    for z in range(BZ):
        coarse, fine = split_kernel(sums[:, z * COLS : (z + 1) * COLS])
        ordered = jnp.dot(coarse, order, preferred_element_type=F32) + jnp.dot(
            fine, order, preferred_element_type=F32
        )
        value = jnp.where(inside, ordered / jnp.where(inside, total, 1.0), 0.0)
        joined[z] = value
        columns_as_rows = lax.dot_general(
            pick, value, (((1,), (1,)), ((), ())), precision=EXACT, preferred_element_type=F32
        )[:, TOP : TOP + BY]
        right_rows.append(columns_as_rows[0:2])
        left_rows.append(columns_as_rows[2:3])
        for half in range(2):
            cut = value[:, half * HALF : (half + 1) * HALF]
            down_rows.append(cut[BY : BY + 2])
            up_rows.append(cut[TOP : TOP + 1])

    def tile(rows):
        have = sum(r.shape[0] for r in rows)
        if have < 8:
            rows = rows + [jnp.zeros((8 - have, HALF), F32)]
        return jnp.concatenate(rows, axis=0)

    right = tile(right_rows)
    left = tile(left_rows)
    down = tile(down_rows)
    up = tile(up_rows)
    at_row = edge[0]
    at_col = edge[1]
    rows, cols = grid

    def send(dy, dx, values):
        to_row = at_row + dy
        to_col = at_col + dx

        @pl.when((to_row >= 0) & (to_row < rows) & (to_col >= 0) & (to_col < cols))
        def _():
            messages[to_row * cols + to_col] = values

    for dy in (-1, 0, 1):
        send(dy, 1, right)
        send(dy, -1, left)
    send(1, 0, down)
    send(-1, 0, up)


def join(grid, edge, arrived, per_pair):
    senders = arrived.shape[0] // chunk_of(per_pair)
    slots = senders * per_pair
    vmem = pl.BlockSpec(memory_space=pltpu.VMEM)
    return pl.pallas_call(
        lambda *refs: join_body(per_pair, grid, *refs),
        in_specs=[pl.BlockSpec(memory_space=pltpu.SMEM), pl.BlockSpec(memory_space=pl.ANY), vmem],
        out_specs=[vmem, vmem],
        out_shape=[
            jax.ShapeDtypeStruct((BZ, SROW, COLS), F32),
            jax.ShapeDtypeStruct((senders, 8, HALF), F32),
        ],
        scratch_shapes=[
            pltpu.VMEM((slots * SY, 2 * BZ * COLS), BF16),
            pltpu.VMEM((slots * SY, 256), BF16),
            pltpu.SMEM((senders, 2, SX), F32),
            pltpu.SemaphoreType.DMA,
        ],
        compiler_params=pltpu.CompilerParams(vmem_limit_bytes=48 * 2**20),
        name="join",
    )(
        edge,
        arrived.reshape(senders, chunk_of(per_pair), 2, SX),
        arrived.reshape(arrived.shape[0] * 2, SX),
    )


def conv_body(grid, edge, joined, received, first, second, bias, out, phases, coarse_h, fine_h):
    at_row = edge[0]
    at_col = edge[1]
    rows, cols = grid
    halo = {}
    for dy in (-1, 0, 1):
        for dx in (-1, 0, 1):
            if (dy, dx) == (0, 0):
                continue
            row = at_row + dy
            col = at_col + dx
            there = (row >= 0) & (row < rows) & (col >= 0) & (col < cols)
            index = jnp.where(there, row * cols + col, 0)
            halo[dy, dx] = jnp.where(there, received[index], 0.0)
    wide_lane = iota((8, 256), 1)

    def along(above, here, below):
        zero = jnp.zeros((8, 128), F32)
        turned = [
            pltpu.roll(jnp.concatenate([part, zero], axis=1), by, 1)
            for part, by in ((above, 256 - (BY - TOP)), (here, TOP), (below, TOP + BY))
        ]
        low = jnp.where(wide_lane < TOP, turned[0], turned[1])
        return jnp.where(
            wide_lane < TOP + BY, low, jnp.where(wide_lane == TOP + BY, turned[2], 0.0)
        )

    from_left = along(halo[-1, -1], halo[0, -1], halo[1, -1])
    from_right = along(halo[-1, 1], halo[0, 1], halo[1, 1])
    from_above = halo[-1, 0]
    from_below = halo[1, 0]
    pick_row = iota((8, HALF), 0)
    pick_lane = iota((8, HALF), 1)
    tall_lane = iota((SROW, HALF), 1)
    row8 = iota((8, HALF), 0)

    def column(message, row, lane_at):
        chosen = jnp.where((pick_row == row) & (pick_lane == lane_at), 1.0, 0.0)
        return lax.dot_general(
            message, chosen, (((0,), (0,)), ((), ())), precision=EXACT, preferred_element_type=F32
        )[:SROW]

    for z in range(BZ):
        halves = []
        for half in range(2):
            own = joined[z, :, half * HALF : (half + 1) * HALF]
            at = 4 * z + 2 * half
            above = jnp.concatenate([from_above[at : at + 2], own[2:8]], axis=0)
            at = 2 * z + half
            below = jnp.concatenate(
                [own[SROW - 8 : SROW - 6], from_below[at : at + 1], jnp.zeros((5, HALF), F32)], axis=0
            )
            halves.append(jnp.concatenate([above, own[8 : SROW - 8], below], axis=0))
        even, odd = halves
        phases[0, z] = jnp.where(tall_lane == 0, column(from_left, 2 * z, 0), pltpu.roll(even, 1, 1))
        phases[1, z] = jnp.where(tall_lane == 0, column(from_left, 2 * z + 1, 0), pltpu.roll(odd, 1, 1))
        phases[2, z] = even
        phases[3, z] = odd
        phases[4, z] = jnp.where(
            tall_lane == HALF - 1, column(from_right, z, HALF - 1), pltpu.roll(even, HALF - 1, 1)
        )
    no_row = edge[0] == 0
    no_col = edge[1] == 0
    keep = jnp.where(no_col & ((iota((1, 256), 1) & (HALF - 1)) == 0), 0.0, 1.0)
    ones = jnp.ones((16, 256), BF16)

    def pair(step, part):
        slot = part % 2
        blocks = (step, step + BLOCKS // 2)
        wide = {}
        for j in range(PHASES):
            for z in range(BZ):
                cut = [
                    phases[j, z, pl.ds(pl.multiple_of(8 * b, 8), WIN), :] for b in blocks
                ]
                wide[j, z] = split_kernel(jnp.concatenate(cut, axis=1))
        for group in range(3):
            coarse = [wide[group + dx, z][0] for dx in range(3) for z in range(BZ)]
            fine = [wide[group + dx, z][1] for dx in range(3) for z in range(BZ)]
            stacked = jnp.concatenate(coarse + fine + coarse + [ones], axis=0)
            hidden = jnp.dot(first[...], stacked, preferred_element_type=F32)
            hidden = jnp.maximum(hidden, 0.0)
            if group == 0:
                hidden = hidden * keep
            coarse, fine = split_kernel(hidden)
            coarse_h[slot, group * HID : (group + 1) * HID, :] = coarse
            fine_h[slot, group * HID : (group + 1) * HID, :] = fine

        if part == 0:

            @pl.when(no_row & (step == 0))
            def _():
                for group in range(3):
                    for scratch in (coarse_h, fine_h):
                        nothing = jnp.zeros((C1 * BZ, HALF), BF16)
                        scratch[slot, group * HID : group * HID + C1 * BZ, :HALF] = nothing

        both = jnp.dot(second[...], coarse_h[slot], preferred_element_type=F32)
        rest = jnp.dot(second[:OUTM, :], fine_h[slot], preferred_element_type=F32)
        result = both[:OUTM] + both[OUTM:] + rest
        for side, b in enumerate(blocks):
            for r in range(OUT_ROWS):
                at = OUT_ROWS * b + r
                out[pl.ds(at, C2, stride=BY // 2), :] = (
                    result[r * C2 : (r + 1) * C2, side * HALF : (side + 1) * HALF] + bias[...]
                )

    def steps(i, carry):
        for part in range(UNROLL):
            pair(UNROLL * i + part, part)
        return carry

    lax.fori_loop(0, BLOCKS // 2 // UNROLL, steps, 0)


def convolve(grid, edge, joined, received, first, second, bias):
    vmem = pl.BlockSpec(memory_space=pltpu.VMEM)
    return pl.pallas_call(
        lambda *refs: conv_body(grid, *refs),
        in_specs=[pl.BlockSpec(memory_space=pltpu.SMEM)] + [vmem] * 5,
        out_specs=vmem,
        out_shape=jax.ShapeDtypeStruct((C2 * BY // 2, HALF), F32),
        scratch_shapes=[
            pltpu.VMEM((PHASES, BZ, SROW, HALF), F32),
            pltpu.VMEM((2, K2, 256), BF16),
            pltpu.VMEM((2, K2, 256), BF16),
        ],
        compiler_params=pltpu.CompilerParams(vmem_limit_bytes=48 * 2**20),
        name="convolve",
    )(edge, joined, received, first, second, bias)


def first_table(weight, bias):
    kernel = weight[:, 0]
    planes = jnp.stack([kernel[:, 1:3], kernel[:, 0:2]], axis=1)
    reach = np.zeros((HID_ROWS, 3, WIN), np.float32)
    for i in range(HID_ROWS):
        for dy in range(3):
            reach[i, dy, i + dy] = 1.0
    table = jnp.einsum("czpyx,iys->iczxps", planes, jnp.asarray(reach), precision=EXACT)
    coarse, fine = split_host(table.reshape(HID, K1))
    each = jnp.tile(jnp.repeat(bias, BZ), HID_ROWS)
    one = lax.reduce_precision(each, 8, 7)
    two = lax.reduce_precision(each - one, 8, 7)
    three = each - one - two
    tail = jnp.stack([one, two, three], axis=1).astype(BF16)
    tail = jnp.pad(tail, ((0, 0), (0, 16 - 3)))
    return jnp.concatenate([coarse, coarse, fine, tail], axis=1)


def second_table(weight):
    reach = np.zeros((OUT_ROWS, 3, HID_ROWS), np.float32)
    for i in range(OUT_ROWS):
        for dy in range(3):
            reach[i, dy, 2 * i + dy] = 1.0
    table = jnp.einsum("oczyx,iyh->ioxhcz", weight[:, :, 1:3], jnp.asarray(reach), precision=EXACT)
    coarse, fine = split_host(table.reshape(OUTM, K2))
    return jnp.concatenate([coarse, fine], axis=0)


def body(strips, routes, conv1_weight, conv1_bias, conv2_weight, conv2_bias):
    rows = lax.axis_size("gx")
    cols = lax.axis_size("gy")
    senders = rows * cols
    per_pair = max(1, STRIPS // senders)
    axes = ("gx", "gy")
    at_row = lax.axis_index("gx").astype(jnp.int32)
    at_col = lax.axis_index("gy").astype(jnp.int32)
    edge = jnp.stack([at_row, at_col])
    routes_t = routes.T
    outgoing = pack(strips, routes_t, senders, per_pair)
    arrived = lax.all_to_all(outgoing, axes, split_axis=0, concat_axis=0, tiled=True)
    first = first_table(conv1_weight, conv1_bias)
    second = second_table(conv2_weight)
    bias = jnp.broadcast_to(conv2_bias[:, None], (C2, HALF))
    joined, messages = join((rows, cols), edge, arrived, per_pair)
    received = lax.all_to_all(messages, axes, split_axis=0, concat_axis=0, tiled=True)
    features = convolve((rows, cols), edge, joined, received, first, second, bias)
    return features.reshape(C2, 1, BY // 2, HALF)


def solution(mesh):
    in_specs = (P(("gx", "gy"), None, None, None), P(("gx", "gy"), None), P(), P(), P(), P())
    out_specs = P(None, None, "gx", "gy")
    return jax.shard_map(body, mesh=mesh, in_specs=in_specs, out_specs=out_specs, check_vma=False)
```

```python
import jax
import jax.numpy as jnp
import numpy as np
from jax import lax
from jax.experimental import pallas as pl
from jax.experimental.pallas import tpu as pltpu
from jax.sharding import PartitionSpec as P

BZ = 2
BY = 128
BX = 128
BLK = 2
STRIPS = 64
SY = 16
SX = 128
C1 = 16
C2 = 32

COLS = BX * BLK
HALF = COLS // 2
TOP = 2
SROW = 136
OUT_ROWS = 4
HID_ROWS = 9
WIN = 16
BLOCKS = BY // (2 * OUT_ROWS)
PHASES = 5
JOIN_UNROLL = 8
K1 = 3 * BZ * WIN
HID = HID_ROWS * C1 * BZ
K2 = 3 * HID
OUTM = OUT_ROWS * C2

EXACT = lax.Precision.HIGHEST
F32 = jnp.float32
BF16 = jnp.bfloat16


def iota(shape, dim):
    return lax.broadcasted_iota(jnp.int32, shape, dim)


def split_kernel(x):
    hi = x.astype(BF16)
    return hi, (x - hi.astype(F32)).astype(BF16)


def split_host(x):
    hi = lax.reduce_precision(x, 8, 7)
    return hi.astype(BF16), (x - hi).astype(BF16)


def chunk_of(per_pair):
    return BZ * SY // 2 * per_pair + 1


def pack_body(per_pair, routes, route_rows, strips, payload, count, sems):
    pairs = BZ * SY // 2
    chunk = chunk_of(per_pair)
    held = route_rows.shape[1]
    senders = payload.shape[0] // chunk
    full = held == STRIPS

    def clear(i, carry):
        count[i] = 0
        return carry

    lax.fori_loop(0, senders, clear, 0, unroll=8)

    def copy(k, at):
        source = strips.at[pl.ds(k * pairs, pairs)]
        return pltpu.make_async_copy(source, payload.at[pl.ds(at, pairs)], sems.at[0 if full else k])

    def when_live(k, run):
        if full:
            run()
        else:
            pl.when(routes[1, k] == 1)(run)

    def place(k, carry):
        def run():
            dest = routes[0, k]
            rank = jnp.minimum(count[dest], per_pair - 1)
            count[dest] = rank + 1
            copy(k, dest * chunk + rank * pairs).start()

        when_live(k, run)
        return carry

    lax.fori_loop(0, held, place, 0, unroll=8)

    match = (route_rows[0:1, :] == iota((senders, held), 0)) & (route_rows[1:2, :] == 1)
    flags = jnp.where(match, 1.0, 0.0)
    before = jnp.where(iota((held, held), 0) < iota((held, held), 1), 1.0, 0.0)
    earlier = jnp.dot(flags.astype(BF16), before.astype(BF16), preferred_element_type=F32)
    fields = jnp.concatenate([route_rows[...].astype(F32), jnp.zeros((120, held), F32)], axis=0)
    fields = fields.astype(BF16)
    for r in range(per_pair):
        chosen = jnp.where(match & (earlier == float(r)), 1.0, 0.0).astype(BF16)
        sent = lax.dot_general(
            chosen, fields, (((1,), (1,)), ((), ())), preferred_element_type=F32
        )
        for dest in range(senders):
            payload[dest * chunk + chunk - 1, r : r + 1, :] = sent[dest : dest + 1, :]

    if full:
        everything = held * pairs
        pltpu.make_async_copy(strips, payload.at[pl.ds(0, everything)], sems.at[0]).wait()
    else:

        def finish(k, carry):
            when_live(k, lambda: copy(k, 0).wait())
            return carry

        lax.fori_loop(0, held, finish, 0)


def pack(strips, routes_t, senders, per_pair):
    held = strips.shape[0]
    pairs = BZ * SY // 2
    vmem = pl.BlockSpec(memory_space=pltpu.VMEM)
    return pl.pallas_call(
        lambda *refs: pack_body(per_pair, *refs),
        in_specs=[
            pl.BlockSpec(memory_space=pltpu.SMEM),
            vmem,
            pl.BlockSpec(memory_space=pl.ANY),
        ],
        out_specs=vmem,
        out_shape=jax.ShapeDtypeStruct((senders * chunk_of(per_pair), 2, SX), F32),
        scratch_shapes=[
            pltpu.SMEM((senders,), jnp.int32),
            pltpu.SemaphoreType.DMA((1 if held == STRIPS else held,)),
        ],
        name="pack",
    )(routes_t, routes_t, strips.reshape(held * pairs, 2, SX))


EDGE_COLUMNS = (COLS - 4, COLS - 3, COLS - 2, COLS - 1, 0, 1, 2)


def pick_columns():
    row = iota((8, COLS), 0)
    col = iota((8, COLS), 1)
    chosen = None
    for i, x in enumerate(EDGE_COLUMNS):
        here = (row == i) & (col == x // 2 + (x % 2) * HALF)
        chosen = here if chosen is None else chosen | here
    return jnp.where(chosen, 1.0, 0.0)


def join_body(per_pair, grid, edge, routes, strips, joined, messages, own_columns, data, place_y, params, sem):
    senders = routes.shape[0]
    slots = senders * per_pair
    chunk = 2 * chunk_of(per_pair)
    fetch = pltpu.make_async_copy(routes.at[:, chunk_of(per_pair) - 1], params, sem)
    fetch.start()
    columns = jnp.concatenate(
        [strips[pl.ds(chunk - 2 + r, senders, stride=chunk), :] for r in range(per_pair)], axis=0
    ).astype(jnp.int32)

    def field(q):
        return columns[:, q : q + 1]

    live = field(1)
    top = field(2)
    left = field(3)
    ramp = field(7)
    y = iota((slots, BY), 1) - top
    weight_y = jnp.where((y >= 0) & (y < SY), jnp.minimum(jnp.minimum(y + 1, SY - y), ramp), 0)
    col = iota((slots, COLS), 1)
    x = jnp.where(col < HALF, 2 * col, 2 * (col - HALF) + 1) - left
    weight_x = jnp.where((x >= 0) & (x < SX), jnp.minimum(jnp.minimum(x + 1, SX - x), ramp), 0)
    weight_y = jnp.where(live == 1, weight_y, 0).astype(F32).astype(BF16)
    weight_x = weight_x.astype(F32).astype(BF16)
    over_rows = (((0,), (0,)), ((), ()))
    total = lax.dot_general(weight_y, weight_x, over_rows, preferred_element_type=F32)
    fetch.wait()
    lane = iota((SY, SX), 1)
    row_lane = iota((SY, BY), 1)
    row_sub = iota((SY, BY), 0)

    def one(h, r):
        k = h * per_pair + r
        live = params[h, r, 1].astype(jnp.int32)
        top = params[h, r, 2].astype(jnp.int32)
        left = params[h, r, 3].astype(jnp.int32)
        frac_z = params[h, r, 4] * (1.0 / 16.0)
        frac_y = params[h, r, 5] * (1.0 / 16.0)
        frac_x = params[h, r, 6] * (1.0 / 16.0)
        ramp = params[h, r, 7].astype(jnp.int32)
        weight = jnp.minimum(jnp.minimum(lane + 1, SX - lane), ramp).astype(F32)
        here = weight * (1.0 - frac_x)
        there = jnp.where(lane < SX - 1, weight * frac_x, 0.0)
        stay_z = 1.0 - frac_z
        move_z = frac_z
        at = h * chunk + r * BZ * SY
        first = strips[pl.ds(at, SY), :]
        second = strips[pl.ds(at + SY, SY), :]
        if slots != STRIPS:
            first = jnp.where(live == 1, first, 0.0)
            second = jnp.where(live == 1, second, 0.0)
        plane0 = stay_z * first + move_z * second
        plane1 = stay_z * second
        shift = left & (SX - 1)
        for z, plane in enumerate((plane0, plane1)):
            piece = here * plane + there * pltpu.roll(plane, SX - 1, 1)
            turned = pltpu.roll(piece, shift, 1)
            low = jnp.where(lane >= left, turned, 0.0)
            high = jnp.where(lane < left, turned, 0.0)
            for side, part in enumerate((low, high)):
                coarse, fine = split_kernel(part)
                at = z * COLS + side * SX
                data[pl.ds(k * SY, SY), at : at + SX] = coarse
                data[pl.ds(k * SY, SY), BZ * COLS + at : BZ * COLS + at + SX] = fine
        y = row_lane - top
        weight_y = jnp.minimum(jnp.minimum(y + 1, SY - y), ramp).astype(F32)
        spread = jnp.where(row_sub == y, weight_y * (1.0 - frac_y), 0.0) + jnp.where(
            row_sub == y + 1, weight_y * frac_y, 0.0
        )
        place_y[pl.ds(k * SY, SY), :] = spread.astype(BF16)

    def holder(h, carry):
        for r in range(per_pair):
            one(h, r)
        return carry

    lax.fori_loop(0, senders, holder, 0, unroll=JOIN_UNROLL)

    sums = lax.dot_general(place_y[...], data[...], over_rows, preferred_element_type=F32)
    sums = sums[:, : BZ * COLS] + sums[:, BZ * COLS :]

    src = iota((COLS, COLS), 0)
    dst = iota((COLS, COLS), 1)
    order = (src == jnp.where(dst < HALF, 2 * dst, 2 * (dst - HALF) + 1)).astype(F32).astype(BF16)
    pick = pick_columns()
    right_rows = []
    left_rows = []
    down_rows = []
    up_rows = []
    for z in range(BZ):
        coarse, fine = split_kernel(sums[:, z * COLS : (z + 1) * COLS])
        ordered = jnp.dot(coarse, order, preferred_element_type=F32) + jnp.dot(
            fine, order, preferred_element_type=F32
        )
        value = ordered / total
        joined[z] = value
        columns_as_rows = lax.dot_general(
            pick, value, (((1,), (1,)), ((), ())), precision=EXACT, preferred_element_type=F32
        )
        own_columns[8 * z : 8 * z + 8, :] = columns_as_rows
        right_rows.append(columns_as_rows[2:4])
        left_rows.append(columns_as_rows[4:5])
        for half in range(2):
            cut = value[:, half * HALF : (half + 1) * HALF]
            down_rows.append(cut[BY - 2 : BY])
            up_rows.append(cut[0:1])

    def tile(rows):
        have = sum(r.shape[0] for r in rows)
        if have < 8:
            rows = rows + [jnp.zeros((8 - have, HALF), F32)]
        return jnp.concatenate(rows, axis=0)

    right = tile(right_rows)
    left = tile(left_rows)
    down = tile(down_rows)
    up = tile(up_rows)
    at_row = edge[0]
    at_col = edge[1]
    rows, cols = grid

    def send(dy, dx, values):
        to_row = at_row + dy
        to_col = at_col + dx

        @pl.when((to_row >= 0) & (to_row < rows) & (to_col >= 0) & (to_col < cols))
        def _():
            messages[to_row * cols + to_col] = values

    for dy in (-1, 0, 1):
        send(dy, 1, right)
        send(dy, -1, left)
    send(1, 0, down)
    send(-1, 0, up)


def join(grid, edge, arrived, per_pair):
    senders = arrived.shape[0] // chunk_of(per_pair)
    slots = senders * per_pair
    vmem = pl.BlockSpec(memory_space=pltpu.VMEM)
    return pl.pallas_call(
        lambda *refs: join_body(per_pair, grid, *refs),
        in_specs=[pl.BlockSpec(memory_space=pltpu.SMEM), pl.BlockSpec(memory_space=pl.ANY), vmem],
        out_specs=[vmem, vmem, vmem],
        out_shape=[
            jax.ShapeDtypeStruct((BZ, BY, COLS), F32),
            jax.ShapeDtypeStruct((senders, 8, HALF), F32),
            jax.ShapeDtypeStruct((8 * BZ, BY), F32),
        ],
        scratch_shapes=[
            pltpu.VMEM((slots * SY, 2 * BZ * COLS), BF16),
            pltpu.VMEM((slots * SY, BY), BF16),
            pltpu.SMEM((senders, 2, SX), F32),
            pltpu.SemaphoreType.DMA,
        ],
        compiler_params=pltpu.CompilerParams(vmem_limit_bytes=48 * 2**20),
        name="join",
    )(
        edge,
        arrived.reshape(senders, chunk_of(per_pair), 2, SX),
        arrived.reshape(arrived.shape[0] * 2, SX),
    )


def two_blocks(wide, blocks, keep, first, second, bias, out, coarse_h, fine_h, top_outside=None):
    ones = jnp.ones((16, 256), BF16)
    for group in range(3):
        coarse = [wide[group + dx, z][0] for dx in range(3) for z in range(BZ)]
        fine = [wide[group + dx, z][1] for dx in range(3) for z in range(BZ)]
        stacked = jnp.concatenate(coarse + fine + coarse + [ones], axis=0)
        hidden = jnp.dot(first[...], stacked, preferred_element_type=F32)
        hidden = jnp.maximum(hidden, 0.0)
        if group == 0 and keep is not None:
            hidden = hidden * keep
        coarse, fine = split_kernel(hidden)
        coarse_h[group * HID : (group + 1) * HID, :] = coarse
        fine_h[group * HID : (group + 1) * HID, :] = fine
    if top_outside is not None:

        @pl.when(top_outside)
        def _():
            for group in range(3):
                for scratch in (coarse_h, fine_h):
                    nothing = jnp.zeros((C1 * BZ, HALF), BF16)
                    scratch[group * HID : group * HID + C1 * BZ, :HALF] = nothing

    both = jnp.dot(second[...], coarse_h[...], preferred_element_type=F32)
    rest = jnp.dot(second[:OUTM, :], fine_h[...], preferred_element_type=F32)
    result = both[:OUTM] + both[OUTM:] + rest
    for side, b in enumerate(blocks):
        for r in range(OUT_ROWS):
            out[pl.ds(OUT_ROWS * b + r, C2, stride=BY // 2), :] = (
                result[r * C2 : (r + 1) * C2, side * HALF : (side + 1) * HALF] + bias[...]
            )


def inner_body(joined, first, second, bias, out, phases, coarse_h, fine_h):
    for z in range(BZ):
        even = joined[z, :, :HALF]
        odd = joined[z, :, HALF:]
        parts = (pltpu.roll(even, 1, 1), pltpu.roll(odd, 1, 1), even, odd, pltpu.roll(even, HALF - 1, 1))
        for j, part in enumerate(parts):
            phases[j, z, TOP : TOP + BY, :] = part
    half = (BLOCKS - 2) // 2
    for step in range(half):
        blocks = (1 + step, 1 + step + half)
        wide = {}
        for j in range(PHASES):
            for z in range(BZ):
                cut = [phases[j, z, 8 * b : 8 * b + WIN, :] for b in blocks]
                wide[j, z] = split_kernel(jnp.concatenate(cut, axis=1))
        slot = step % 2
        two_blocks(
            wide, blocks, None, first, second, bias, out, coarse_h.at[slot], fine_h.at[slot]
        )


def inner(joined, first, second, bias):
    vmem = pl.BlockSpec(memory_space=pltpu.VMEM)
    return pl.pallas_call(
        inner_body,
        in_specs=[vmem] * 4,
        out_specs=vmem,
        out_shape=jax.ShapeDtypeStruct((C2 * BY // 2, HALF), F32),
        scratch_shapes=[
            pltpu.VMEM((PHASES, BZ, SROW, HALF), F32),
            pltpu.VMEM((2, K2, 256), BF16),
            pltpu.VMEM((2, K2, 256), BF16),
        ],
        compiler_params=pltpu.CompilerParams(vmem_limit_bytes=48 * 2**20),
        name="inner",
    )(joined, first, second, bias)


def rim_body(
    grid, edge, joined, received, own_columns, inner_out, first, second, bias, first_rim, second_rim,
    out, coarse_h, fine_h,
):
    at_row = edge[0]
    at_col = edge[1]
    rows, cols = grid
    halo = {}
    for dy in (-1, 0, 1):
        for dx in (-1, 0, 1):
            if (dy, dx) == (0, 0):
                continue
            row = at_row + dy
            col = at_col + dx
            there = (row >= 0) & (row < rows) & (col >= 0) & (col < cols)
            index = jnp.where(there, row * cols + col, 0)
            halo[dy, dx] = jnp.where(there, received[index], 0.0)
    no_row = at_row == 0
    no_col = at_col == 0
    wide_lane = iota((8, 256), 1)

    def stored(above, here, below):
        zero = jnp.zeros((8, 128), F32)
        turned = [
            pltpu.roll(jnp.concatenate([part, zero], axis=1), by, 1)
            for part, by in ((above, 256 - (BY - TOP)), (here, TOP), (below, TOP + BY))
        ]
        low = jnp.where(wide_lane < TOP, turned[0], turned[1])
        return jnp.where(
            wide_lane < TOP + BY, low, jnp.where(wide_lane == TOP + BY, turned[2], 0.0)
        )

    from_left = stored(halo[-1, -1], halo[0, -1], halo[1, -1])
    from_right = stored(halo[-1, 1], halo[0, 1], halo[1, 1])
    from_above = halo[-1, 0]
    from_below = halo[1, 0]

    pick_row = iota((8, HALF), 0)
    pick_lane = iota((8, HALF), 1)
    tall_lane = iota((2 * WIN, HALF), 1)

    def column(message, row, lane_at):
        chosen = jnp.where((pick_row == row) & (pick_lane == lane_at), 1.0, 0.0)
        ends = jnp.concatenate([message[:, :WIN], message[:, SROW - WIN : SROW]], axis=1)
        return lax.dot_general(
            ends, chosen, (((0,), (0,)), ((), ())), precision=EXACT, preferred_element_type=F32
        )

    wide = {}
    for z in range(BZ):
        halves = []
        for half in range(2):
            own = joined[z, :, half * HALF : (half + 1) * HALF]
            at = 4 * z + 2 * half
            bottom = 2 * z + half
            ends = [
                from_above[at : at + 2],
                own[: WIN - TOP],
                own[SROW - WIN - TOP :],
                from_below[bottom : bottom + 1],
                jnp.zeros((SROW - BY - TOP - 1, HALF), F32),
            ]
            halves.append(jnp.concatenate(ends, axis=0))
        even, odd = halves
        parts = (
            jnp.where(tall_lane == 0, column(from_left, 2 * z, 0), pltpu.roll(even, 1, 1)),
            jnp.where(tall_lane == 0, column(from_left, 2 * z + 1, 0), pltpu.roll(odd, 1, 1)),
            even,
            odd,
            jnp.where(
                tall_lane == HALF - 1, column(from_right, z, HALF - 1), pltpu.roll(even, HALF - 1, 1)
            ),
        )
        for j, part in enumerate(parts):
            wide[j, z] = split_kernel(jnp.concatenate([part[:WIN], part[WIN:]], axis=1))

    pick = pick_columns()
    left_rows = []
    right_rows = []
    for z in range(BZ):
        cut = [
            jnp.concatenate([from_above[4 * z + c : 4 * z + c + 1], from_above[4 * z + 2 + c : 4 * z + 3 + c]], axis=1)
            for c in range(2)
        ]
        cut.append(jnp.concatenate([from_below[2 * z : 2 * z + 1], from_below[2 * z + 1 : 2 * z + 2]], axis=1))
        cut.append(jnp.zeros((5, COLS), F32))
        outer = lax.dot_general(
            pick,
            jnp.concatenate(cut, axis=0),
            (((1,), (1,)), ((), ())),
            precision=EXACT,
            preferred_element_type=F32,
        )
        outer = jnp.concatenate([outer, jnp.zeros((8, 256 - 8), F32)], axis=1)
        here = jnp.concatenate([own_columns[8 * z : 8 * z + 8, :], jnp.zeros((8, BY), F32)], axis=1)
        own = jnp.where(
            wide_lane < TOP,
            outer,
            jnp.where(
                wide_lane < TOP + BY,
                pltpu.roll(here, TOP, 1),
                jnp.where(wide_lane == TOP + BY, pltpu.roll(outer, BY, 1), 0.0),
            ),
        )
        one = jnp.ones((1, 256), F32)
        rest = jnp.zeros((2, 256), F32)
        left_rows += [from_left[2 * z : 2 * z + 2], own[4:7], one, rest]
        right_rows += [own[0:4], from_right[z : z + 1], one, rest]
    both = jnp.concatenate(
        [jnp.concatenate(left_rows, axis=0), jnp.concatenate(right_rows, axis=0)], axis=1
    )

    def reach(values):
        return jnp.concatenate([values] + [pltpu.roll(values, 512 - dy, 1) for dy in (1, 2)], axis=0)

    hidden = jnp.dot(first_rim[...], reach(both), precision=EXACT, preferred_element_type=F32)
    hidden = jnp.maximum(hidden, 0.0)
    lane = iota((3 * C1 * BZ, 512), 1)
    depth = iota((3 * C1 * BZ, 512), 0)
    outside = no_row & ((lane & 255) == 0)
    outside = outside | (no_col & (lane < 256) & (depth < C1 * BZ))
    hidden = jnp.where(outside, 0.0, hidden)
    found = jnp.dot(second_rim[...], reach(hidden), precision=EXACT, preferred_element_type=F32)
    every = jnp.where(iota((BY // 2, 256), 1) == 2 * iota((BY // 2, 256), 0), 1.0, 0.0)
    columns = [
        lax.dot_general(
            every,
            found[:, side * 256 : (side + 1) * 256] + bias[:, :1],
            (((1,), (1,)), ((), ())),
            precision=EXACT,
            preferred_element_type=F32,
        )
        for side in range(2)
    ]
    out_lane = iota((BY // 2, HALF), 1)
    for o in range(C2):
        at = o * (BY // 2)
        values = inner_out[at : at + BY // 2, :]
        values = jnp.where(out_lane == 0, columns[0][:, o : o + 1], values)
        out[at : at + BY // 2, :] = jnp.where(out_lane == HALF - 1, columns[1][:, o : o + 1], values)

    keep = jnp.where(no_col & ((iota((1, 256), 1) & (HALF - 1)) == 0), 0.0, 1.0)
    two_blocks(
        wide, (0, BLOCKS - 1), keep, first, second, bias, out, coarse_h, fine_h, top_outside=no_row
    )


def rim(grid, edge, joined, received, own_columns, inner_out, first, second, bias, first_rim, second_rim):
    vmem = pl.BlockSpec(memory_space=pltpu.VMEM)
    return pl.pallas_call(
        lambda *refs: rim_body(grid, *refs),
        in_specs=[pl.BlockSpec(memory_space=pltpu.SMEM)] + [vmem] * 9,
        out_specs=vmem,
        out_shape=jax.ShapeDtypeStruct((C2 * BY // 2, HALF), F32),
        scratch_shapes=[pltpu.VMEM((K2, 256), BF16), pltpu.VMEM((K2, 256), BF16)],
        compiler_params=pltpu.CompilerParams(vmem_limit_bytes=48 * 2**20),
        name="rim",
    )(edge, joined, received, own_columns, inner_out, first, second, bias, first_rim, second_rim)


def rim_tables(weight1, bias1, weight2):
    kernel = weight1[:, 0]
    planes = jnp.stack([kernel[:, 1:3], kernel[:, 0:2]], axis=1)
    reach = np.zeros((3, 3, 8), np.float32)
    for i in range(3):
        for dx in range(3):
            reach[i, dx, i + dx] = 1.0
    table = jnp.einsum("czpyx,kxq->kczypq", planes, jnp.asarray(reach), precision=EXACT)
    ones = np.zeros((3, BZ, 8), np.float32)
    ones[0, 0, PHASES] = 1.0
    table = table + bias1[None, :, None, None, None, None] * jnp.asarray(ones)
    first = table.reshape(3 * C1 * BZ, 3 * BZ * 8)
    second = jnp.transpose(weight2[:, :, 1:3], (0, 3, 4, 1, 2)).reshape(C2, 9 * C1 * BZ)
    return first, second


def first_table(weight, bias):
    kernel = weight[:, 0]
    planes = jnp.stack([kernel[:, 1:3], kernel[:, 0:2]], axis=1)
    reach = np.zeros((HID_ROWS, 3, WIN), np.float32)
    for i in range(HID_ROWS):
        for dy in range(3):
            reach[i, dy, i + dy] = 1.0
    table = jnp.einsum("czpyx,iys->iczxps", planes, jnp.asarray(reach), precision=EXACT)
    coarse, fine = split_host(table.reshape(HID, K1))
    each = jnp.tile(jnp.repeat(bias, BZ), HID_ROWS)
    one = lax.reduce_precision(each, 8, 7)
    two = lax.reduce_precision(each - one, 8, 7)
    three = each - one - two
    tail = jnp.stack([one, two, three], axis=1).astype(BF16)
    tail = jnp.pad(tail, ((0, 0), (0, 16 - 3)))
    return jnp.concatenate([coarse, coarse, fine, tail], axis=1)


def second_table(weight):
    reach = np.zeros((OUT_ROWS, 3, HID_ROWS), np.float32)
    for i in range(OUT_ROWS):
        for dy in range(3):
            reach[i, dy, 2 * i + dy] = 1.0
    table = jnp.einsum("oczyx,iyh->ioxhcz", weight[:, :, 1:3], jnp.asarray(reach), precision=EXACT)
    coarse, fine = split_host(table.reshape(OUTM, K2))
    return jnp.concatenate([coarse, fine], axis=0)


def body(strips, routes, conv1_weight, conv1_bias, conv2_weight, conv2_bias):
    rows = lax.axis_size("gx")
    cols = lax.axis_size("gy")
    senders = rows * cols
    per_pair = max(1, STRIPS // senders)
    axes = ("gx", "gy")
    at_row = lax.axis_index("gx").astype(jnp.int32)
    at_col = lax.axis_index("gy").astype(jnp.int32)
    edge = jnp.stack([at_row, at_col])
    routes_t = routes.T
    outgoing = pack(strips, routes_t, senders, per_pair)
    arrived = lax.all_to_all(outgoing, axes, split_axis=0, concat_axis=0, tiled=True)
    first = first_table(conv1_weight, conv1_bias)
    second = second_table(conv2_weight)
    bias = jnp.broadcast_to(conv2_bias[:, None], (C2, HALF))
    first_rim, second_rim = rim_tables(conv1_weight, conv1_bias, conv2_weight)
    joined, messages, own_columns = join((rows, cols), edge, arrived, per_pair)
    received = lax.all_to_all(messages, axes, split_axis=0, concat_axis=0, tiled=True)
    inner_out = inner(joined, first, second, bias)
    features = rim(
        (rows, cols), edge, joined, received, own_columns, inner_out, first, second, bias, first_rim, second_rim
    )
    return features.reshape(C2, 1, BY // 2, HALF)


def solution(mesh):
    in_specs = (P(("gx", "gy"), None, None, None), P(("gx", "gy"), None), P(), P(), P(), P())
    out_specs = P(None, None, "gx", "gy")
    return jax.shard_map(body, mesh=mesh, in_specs=in_specs, out_specs=out_specs, check_vma=False)
```

```python
import jax
import jax.numpy as jnp
import numpy as np
from jax import lax
from jax.experimental import pallas as pl
from jax.experimental.pallas import tpu as pltpu
from jax.sharding import PartitionSpec as P

BZ = 2
BY = 128
BX = 128
BLK = 2
STRIPS = 64
SY = 16
SX = 128
C1 = 16
C2 = 32

COLS = BX * BLK
HALF = COLS // 2
TOP = 2
SROW = 136
OUT_ROWS = 4
HID_ROWS = 9
WIN = 16
BLOCKS = BY // (2 * OUT_ROWS)
PHASES = 5
JOIN_UNROLL = 8
K1 = 3 * BZ * WIN
HID = HID_ROWS * C1 * BZ
K2 = 3 * HID
OUTM = OUT_ROWS * C2

EXACT = lax.Precision.HIGHEST
F32 = jnp.float32
BF16 = jnp.bfloat16


def iota(shape, dim):
    return lax.broadcasted_iota(jnp.int32, shape, dim)


def split_kernel(x):
    hi = x.astype(BF16)
    return hi, (x - hi.astype(F32)).astype(BF16)


def split_host(x):
    hi = lax.reduce_precision(x, 8, 7)
    return hi.astype(BF16), (x - hi).astype(BF16)


def chunk_of(per_pair):
    return BZ * SY // 2 * per_pair + 1


def pack_body(per_pair, routes, route_rows, strips, payload, count, sems):
    pairs = BZ * SY // 2
    chunk = chunk_of(per_pair)
    held = route_rows.shape[1]
    senders = payload.shape[0] // chunk
    full = held == STRIPS

    def clear(i, carry):
        count[i] = 0
        return carry

    lax.fori_loop(0, senders, clear, 0, unroll=8)

    def copy(k, at):
        source = strips.at[pl.ds(k * pairs, pairs)]
        return pltpu.make_async_copy(source, payload.at[pl.ds(at, pairs)], sems.at[0 if full else k])

    def when_live(k, run):
        if full:
            run()
        else:
            pl.when(routes[1, k] == 1)(run)

    def place(k, carry):
        def run():
            dest = routes[0, k]
            rank = jnp.minimum(count[dest], per_pair - 1)
            count[dest] = rank + 1
            copy(k, dest * chunk + rank * pairs).start()

        when_live(k, run)
        return carry

    lax.fori_loop(0, held, place, 0, unroll=8)

    match = (route_rows[0:1, :] == iota((senders, held), 0)) & (route_rows[1:2, :] == 1)
    flags = jnp.where(match, 1.0, 0.0)
    before = jnp.where(iota((held, held), 0) < iota((held, held), 1), 1.0, 0.0)
    earlier = jnp.dot(flags.astype(BF16), before.astype(BF16), preferred_element_type=F32)
    fields = jnp.concatenate([route_rows[...].astype(F32), jnp.zeros((120, held), F32)], axis=0)
    fields = fields.astype(BF16)
    for r in range(per_pair):
        chosen = jnp.where(match & (earlier == float(r)), 1.0, 0.0).astype(BF16)
        sent = lax.dot_general(
            chosen, fields, (((1,), (1,)), ((), ())), preferred_element_type=F32
        )
        for dest in range(senders):
            payload[dest * chunk + chunk - 1, r : r + 1, :] = sent[dest : dest + 1, :]

    if full:
        everything = held * pairs
        pltpu.make_async_copy(strips, payload.at[pl.ds(0, everything)], sems.at[0]).wait()
    else:

        def finish(k, carry):
            when_live(k, lambda: copy(k, 0).wait())
            return carry

        lax.fori_loop(0, held, finish, 0)


def pack(strips, routes_t, senders, per_pair):
    held = strips.shape[0]
    pairs = BZ * SY // 2
    vmem = pl.BlockSpec(memory_space=pltpu.VMEM)
    return pl.pallas_call(
        lambda *refs: pack_body(per_pair, *refs),
        in_specs=[
            pl.BlockSpec(memory_space=pltpu.SMEM),
            vmem,
            pl.BlockSpec(memory_space=pl.ANY),
        ],
        out_specs=vmem,
        out_shape=jax.ShapeDtypeStruct((senders * chunk_of(per_pair), 2, SX), F32),
        scratch_shapes=[
            pltpu.SMEM((senders,), jnp.int32),
            pltpu.SemaphoreType.DMA((1 if held == STRIPS else held,)),
        ],
        name="pack",
    )(routes_t, routes_t, strips.reshape(held * pairs, 2, SX))


EDGE_COLUMNS = (COLS - 4, COLS - 3, COLS - 2, COLS - 1, 0, 1, 2)


def edge_column(i):
    return jnp.where(i < 4, COLS - 4 + i, i - 4)


def pick_columns():
    row = iota((8, COLS), 0)
    col = iota((8, COLS), 1)
    chosen = None
    for i, x in enumerate(EDGE_COLUMNS):
        here = (row == i) & (col == x // 2 + (x % 2) * HALF)
        chosen = here if chosen is None else chosen | here
    return jnp.where(chosen, 1.0, 0.0)


def join_body(per_pair, grid, edge, routes, strips, joined, messages, own_columns, data, place_y, params, sem):
    senders = routes.shape[0]
    slots = senders * per_pair
    chunk = 2 * chunk_of(per_pair)
    fetch = pltpu.make_async_copy(routes.at[:, chunk_of(per_pair) - 1], params, sem)
    fetch.start()
    columns = jnp.concatenate(
        [strips[pl.ds(chunk - 2 + r, senders, stride=chunk), :] for r in range(per_pair)], axis=0
    ).astype(jnp.int32)

    def field(q):
        return columns[:, q : q + 1]

    live = field(1)
    top = field(2)
    left = field(3)
    ramp = field(7)
    y = iota((slots, BY), 1) - top
    weight_y = jnp.where((y >= 0) & (y < SY), jnp.minimum(jnp.minimum(y + 1, SY - y), ramp), 0)
    col = iota((slots, COLS), 1)
    x = jnp.where(col < HALF, 2 * col, 2 * (col - HALF) + 1) - left
    weight_x = jnp.where((x >= 0) & (x < SX), jnp.minimum(jnp.minimum(x + 1, SX - x), ramp), 0)
    weight_y = jnp.where(live == 1, weight_y, 0).astype(F32).astype(BF16)
    weight_x = weight_x.astype(F32).astype(BF16)
    over_rows = (((0,), (0,)), ((), ()))
    total = lax.dot_general(weight_y, weight_x, over_rows, preferred_element_type=F32)
    fetch.wait()
    lane = iota((SY, SX), 1)
    row_lane = iota((SY, BY), 1)
    row_sub = iota((SY, BY), 0)

    def one(h, r):
        k = h * per_pair + r
        live = params[h, r, 1].astype(jnp.int32)
        top = params[h, r, 2].astype(jnp.int32)
        left = params[h, r, 3].astype(jnp.int32)
        frac_z = params[h, r, 4] * (1.0 / 16.0)
        frac_y = params[h, r, 5] * (1.0 / 16.0)
        frac_x = params[h, r, 6] * (1.0 / 16.0)
        ramp = params[h, r, 7].astype(jnp.int32)
        weight = jnp.minimum(jnp.minimum(lane + 1, SX - lane), ramp).astype(F32)
        here = weight * (1.0 - frac_x)
        there = jnp.where(lane < SX - 1, weight * frac_x, 0.0)
        stay_z = 1.0 - frac_z
        move_z = frac_z
        at = h * chunk + r * BZ * SY
        first = strips[pl.ds(at, SY), :]
        second = strips[pl.ds(at + SY, SY), :]
        if slots != STRIPS:
            first = jnp.where(live == 1, first, 0.0)
            second = jnp.where(live == 1, second, 0.0)
        plane0 = stay_z * first + move_z * second
        plane1 = stay_z * second
        shift = left & (SX - 1)
        for z, plane in enumerate((plane0, plane1)):
            piece = here * plane + there * pltpu.roll(plane, SX - 1, 1)
            turned = pltpu.roll(piece, shift, 1)
            low = jnp.where(lane >= left, turned, 0.0)
            high = jnp.where(lane < left, turned, 0.0)
            for side, part in enumerate((low, high)):
                coarse, fine = split_kernel(part)
                at = z * COLS + side * SX
                data[pl.ds(k * SY, SY), at : at + SX] = coarse
                data[pl.ds(k * SY, SY), BZ * COLS + at : BZ * COLS + at + SX] = fine
        y = row_lane - top
        weight_y = jnp.minimum(jnp.minimum(y + 1, SY - y), ramp).astype(F32)
        spread = jnp.where(row_sub == y, weight_y * (1.0 - frac_y), 0.0) + jnp.where(
            row_sub == y + 1, weight_y * frac_y, 0.0
        )
        place_y[pl.ds(k * SY, SY), :] = spread.astype(BF16)

    def holder(h, carry):
        for r in range(per_pair):
            one(h, r)
        return carry

    lax.fori_loop(0, senders, holder, 0, unroll=JOIN_UNROLL)

    sums = lax.dot_general(place_y[...], data[...], over_rows, preferred_element_type=F32)
    sums = sums[:, : BZ * COLS] + sums[:, BZ * COLS :]

    src = iota((COLS, COLS), 0)
    dst = iota((COLS, COLS), 1)
    order = (src == jnp.where(dst < HALF, 2 * dst, 2 * (dst - HALF) + 1)).astype(F32).astype(BF16)
    along = iota((8, COLS), 1)
    natural = edge_column(iota((8, COLS), 0))
    pick = jnp.where(along == natural, 1.0, 0.0).astype(BF16)
    x = edge_column(iota((slots, 8), 1)) - left
    rim_weight = jnp.where((x >= 0) & (x < SX), jnp.minimum(jnp.minimum(x + 1, SX - x), ramp), 0)
    rim_weight = rim_weight.astype(F32).astype(BF16)
    rim_total = lax.dot_general(rim_weight, weight_y, over_rows, preferred_element_type=F32)
    right_rows = []
    left_rows = []
    down_rows = []
    up_rows = []
    for z in range(BZ):
        coarse, fine = split_kernel(sums[:, z * COLS : (z + 1) * COLS])
        ordered = jnp.dot(coarse, order, preferred_element_type=F32) + jnp.dot(
            fine, order, preferred_element_type=F32
        )
        value = ordered / total
        joined[z] = value
        over_lanes = (((1,), (1,)), ((), ()))
        columns_as_rows = lax.dot_general(
            pick, coarse, over_lanes, preferred_element_type=F32
        ) + lax.dot_general(pick, fine, over_lanes, preferred_element_type=F32)
        columns_as_rows = columns_as_rows / rim_total
        own_columns[8 * z : 8 * z + 8, :] = columns_as_rows
        right_rows.append(columns_as_rows[2:4])
        left_rows.append(columns_as_rows[4:5])
        for half in range(2):
            cut = value[:, half * HALF : (half + 1) * HALF]
            down_rows.append(cut[BY - 2 : BY])
            up_rows.append(cut[0:1])

    def tile(rows):
        have = sum(r.shape[0] for r in rows)
        if have < 8:
            rows = rows + [jnp.zeros((8 - have, HALF), F32)]
        return jnp.concatenate(rows, axis=0)

    right = tile(right_rows)
    left = tile(left_rows)
    down = tile(down_rows)
    up = tile(up_rows)
    at_row = edge[0]
    at_col = edge[1]
    rows, cols = grid

    def send(dy, dx, values):
        to_row = at_row + dy
        to_col = at_col + dx

        @pl.when((to_row >= 0) & (to_row < rows) & (to_col >= 0) & (to_col < cols))
        def _():
            messages[to_row * cols + to_col] = values

    for dy in (-1, 0, 1):
        send(dy, 1, right)
        send(dy, -1, left)
    send(1, 0, down)
    send(-1, 0, up)


def join(grid, edge, arrived, per_pair):
    senders = arrived.shape[0] // chunk_of(per_pair)
    slots = senders * per_pair
    vmem = pl.BlockSpec(memory_space=pltpu.VMEM)
    return pl.pallas_call(
        lambda *refs: join_body(per_pair, grid, *refs),
        in_specs=[pl.BlockSpec(memory_space=pltpu.SMEM), pl.BlockSpec(memory_space=pl.ANY), vmem],
        out_specs=[vmem, vmem, vmem],
        out_shape=[
            jax.ShapeDtypeStruct((BZ, BY, COLS), F32),
            jax.ShapeDtypeStruct((senders, 8, HALF), F32),
            jax.ShapeDtypeStruct((8 * BZ, BY), F32),
        ],
        scratch_shapes=[
            pltpu.VMEM((slots * SY, 2 * BZ * COLS), BF16),
            pltpu.VMEM((slots * SY, BY), BF16),
            pltpu.SMEM((senders, 2, SX), F32),
            pltpu.SemaphoreType.DMA,
        ],
        compiler_params=pltpu.CompilerParams(vmem_limit_bytes=48 * 2**20),
        name="join",
    )(
        edge,
        arrived.reshape(senders, chunk_of(per_pair), 2, SX),
        arrived.reshape(arrived.shape[0] * 2, SX),
    )


def two_blocks(wide, blocks, keep, first, second, bias, out, coarse_h, fine_h, keep_top=None):
    ones = jnp.ones((16, 256), BF16)
    for group in range(3):
        coarse = [wide[group + dx, z][0] for dx in range(3) for z in range(BZ)]
        fine = [wide[group + dx, z][1] for dx in range(3) for z in range(BZ)]
        stacked = jnp.concatenate(coarse + fine + coarse + [ones], axis=0)
        hidden = jnp.dot(first[...], stacked, preferred_element_type=F32)
        hidden = jnp.maximum(hidden, 0.0)
        if group == 0 and keep is not None:
            hidden = hidden * keep
        if keep_top is not None:
            top = C1 * BZ
            hidden = jnp.concatenate([hidden[:top] * keep_top, hidden[top:]], axis=0)
        coarse, fine = split_kernel(hidden)
        coarse_h[group * HID : (group + 1) * HID, :] = coarse
        fine_h[group * HID : (group + 1) * HID, :] = fine
    both = jnp.dot(second[...], coarse_h[...], preferred_element_type=F32)
    rest = jnp.dot(second[:OUTM, :], fine_h[...], preferred_element_type=F32)
    result = both[:OUTM] + both[OUTM:] + rest
    for side, b in enumerate(blocks):
        for r in range(OUT_ROWS):
            out[pl.ds(OUT_ROWS * b + r, C2, stride=BY // 2), :] = (
                result[r * C2 : (r + 1) * C2, side * HALF : (side + 1) * HALF] + bias[...]
            )


def inner_body(joined, first, second, bias, out, phases, coarse_h, fine_h):
    for z in range(BZ):
        even = joined[z, :, :HALF]
        odd = joined[z, :, HALF:]
        parts = (pltpu.roll(even, 1, 1), pltpu.roll(odd, 1, 1), even, odd, pltpu.roll(even, HALF - 1, 1))
        for j, part in enumerate(parts):
            phases[j, z, TOP : TOP + BY, :] = part
    half = (BLOCKS - 2) // 2
    for step in range(half):
        blocks = (1 + step, 1 + step + half)
        wide = {}
        for j in range(PHASES):
            for z in range(BZ):
                cut = [phases[j, z, 8 * b : 8 * b + WIN, :] for b in blocks]
                wide[j, z] = split_kernel(jnp.concatenate(cut, axis=1))
        slot = step % 2
        two_blocks(
            wide, blocks, None, first, second, bias, out, coarse_h.at[slot], fine_h.at[slot]
        )


def inner(joined, first, second, bias):
    vmem = pl.BlockSpec(memory_space=pltpu.VMEM)
    return pl.pallas_call(
        inner_body,
        in_specs=[vmem] * 4,
        out_specs=vmem,
        out_shape=jax.ShapeDtypeStruct((C2 * BY // 2, HALF), F32),
        scratch_shapes=[
            pltpu.VMEM((PHASES, BZ, SROW, HALF), F32),
            pltpu.VMEM((2, K2, 256), BF16),
            pltpu.VMEM((2, K2, 256), BF16),
        ],
        compiler_params=pltpu.CompilerParams(vmem_limit_bytes=48 * 2**20),
        name="inner",
    )(joined, first, second, bias)


def rim_body(
    grid, edge, joined, received, own_columns, inner_out, first, second, bias, first_rim, second_rim,
    out, coarse_h, fine_h,
):
    at_row = edge[0]
    at_col = edge[1]
    rows, cols = grid
    halo = {}
    for dy in (-1, 0, 1):
        for dx in (-1, 0, 1):
            if (dy, dx) == (0, 0):
                continue
            row = at_row + dy
            col = at_col + dx
            there = (row >= 0) & (row < rows) & (col >= 0) & (col < cols)
            index = jnp.where(there, row * cols + col, 0)
            halo[dy, dx] = jnp.where(there, received[index], 0.0)
    no_row = at_row == 0
    no_col = at_col == 0
    wide_lane = iota((8, 256), 1)

    def stored(above, here, below):
        zero = jnp.zeros((8, 128), F32)
        turned = [
            pltpu.roll(jnp.concatenate([part, zero], axis=1), by, 1)
            for part, by in ((above, 256 - (BY - TOP)), (here, TOP), (below, TOP + BY))
        ]
        low = jnp.where(wide_lane < TOP, turned[0], turned[1])
        return jnp.where(
            wide_lane < TOP + BY, low, jnp.where(wide_lane == TOP + BY, turned[2], 0.0)
        )

    from_left = stored(halo[-1, -1], halo[0, -1], halo[1, -1])
    from_right = stored(halo[-1, 1], halo[0, 1], halo[1, 1])
    from_above = halo[-1, 0]
    from_below = halo[1, 0]

    tall_lane = iota((2 * WIN, HALF), 1)
    sides = jnp.concatenate([from_left[:4], from_right[:4]], axis=0)
    ends = jnp.concatenate(
        [sides[:, :WIN], sides[:, SROW - WIN : SROW], jnp.zeros((8, 128 - 2 * WIN), F32)], axis=1
    )
    side_columns = jnp.transpose(ends)[: 2 * WIN]

    def column(row):
        return side_columns[:, row : row + 1]

    wide = {}
    for z in range(BZ):
        halves = []
        for half in range(2):
            own = joined[z, :, half * HALF : (half + 1) * HALF]
            at = 4 * z + 2 * half
            bottom = 2 * z + half
            ends = [
                from_above[at : at + 2],
                own[: WIN - TOP],
                own[SROW - WIN - TOP :],
                from_below[bottom : bottom + 1],
                jnp.zeros((SROW - BY - TOP - 1, HALF), F32),
            ]
            halves.append(jnp.concatenate(ends, axis=0))
        even, odd = halves
        parts = (
            jnp.where(tall_lane == 0, column(2 * z), pltpu.roll(even, 1, 1)),
            jnp.where(tall_lane == 0, column(2 * z + 1), pltpu.roll(odd, 1, 1)),
            even,
            odd,
            jnp.where(
                tall_lane == HALF - 1, column(4 + z), pltpu.roll(even, HALF - 1, 1)
            ),
        )
        for j, part in enumerate(parts):
            wide[j, z] = split_kernel(jnp.concatenate([part[:WIN], part[WIN:]], axis=1))

    left_rows = []
    right_rows = []
    cut = []
    for z in range(BZ):
        for c in range(2):
            at = 4 * z + c
            cut.append(jnp.concatenate([from_above[at : at + 1], from_above[at + 2 : at + 3]], axis=1))
        cut.append(jnp.concatenate([from_below[2 * z : 2 * z + 1], from_below[2 * z + 1 : 2 * z + 2]], axis=1))
        cut.append(jnp.zeros((5, COLS), F32))
    outer_all = lax.dot_general(
        pick_columns(),
        jnp.concatenate(cut, axis=0),
        (((1,), (1,)), ((), ())),
        precision=EXACT,
        preferred_element_type=F32,
    )
    outer_all = jnp.concatenate([outer_all, jnp.zeros((8, 256 - 8 * BZ), F32)], axis=1)
    for z in range(BZ):
        outer = pltpu.roll(outer_all, 256 - 8 * z, 1) if z else outer_all
        here = jnp.concatenate([own_columns[8 * z : 8 * z + 8, :], jnp.zeros((8, BY), F32)], axis=1)
        own = jnp.where(
            wide_lane < TOP,
            outer,
            jnp.where(
                wide_lane < TOP + BY,
                pltpu.roll(here, TOP, 1),
                jnp.where(wide_lane == TOP + BY, pltpu.roll(outer, BY, 1), 0.0),
            ),
        )
        one = jnp.ones((1, 256), F32)
        rest = jnp.zeros((2, 256), F32)
        left_rows += [from_left[2 * z : 2 * z + 2], own[4:7], one, rest]
        right_rows += [own[0:4], from_right[z : z + 1], one, rest]
    both = jnp.concatenate(
        [jnp.concatenate(left_rows, axis=0), jnp.concatenate(right_rows, axis=0)], axis=1
    )

    def reach(values):
        return jnp.concatenate([values] + [pltpu.roll(values, 512 - dy, 1) for dy in (1, 2)], axis=0)

    def product(table, values):
        coarse, fine = split_kernel(reach(values))
        stacked = jnp.concatenate([coarse, fine, coarse], axis=0)
        return jnp.dot(table[...], stacked, preferred_element_type=F32)

    hidden = product(first_rim, both)
    hidden = jnp.maximum(hidden, 0.0)
    lane = iota((3 * C1 * BZ, 512), 1)
    depth = iota((3 * C1 * BZ, 512), 0)
    outside = no_row & ((lane & 255) == 0)
    outside = outside | (no_col & (lane < 256) & (depth < C1 * BZ))
    hidden = jnp.where(outside, 0.0, hidden)
    found = product(second_rim, hidden)
    every = jnp.where(iota((BY // 2, 256), 1) == 2 * iota((BY // 2, 256), 0), 1.0, 0.0).astype(BF16)
    parts = []
    for side in range(2):
        parts += split_kernel(found[:, side * 256 : (side + 1) * 256] + bias[:, :1])
    turned = lax.dot_general(
        every,
        jnp.concatenate(parts, axis=0),
        (((1,), (1,)), ((), ())),
        preferred_element_type=F32,
    )
    columns = [
        turned[:, 2 * side * C2 : (2 * side + 1) * C2] + turned[:, (2 * side + 1) * C2 : (2 * side + 2) * C2]
        for side in range(2)
    ]
    out_lane = iota((BY // 2, HALF), 1)
    for o in range(C2):
        at = o * (BY // 2)
        values = inner_out[at : at + BY // 2, :]
        values = jnp.where(out_lane == 0, columns[0][:, o : o + 1], values)
        out[at : at + BY // 2, :] = jnp.where(out_lane == HALF - 1, columns[1][:, o : o + 1], values)

    keep = jnp.where(no_col & ((iota((1, 256), 1) & (HALF - 1)) == 0), 0.0, 1.0)
    keep_top = jnp.where(no_row & (iota((1, 256), 1) < HALF), 0.0, 1.0)
    two_blocks(
        wide, (0, BLOCKS - 1), keep, first, second, bias, out, coarse_h, fine_h, keep_top=keep_top
    )


def rim(grid, edge, joined, received, own_columns, inner_out, first, second, bias, first_rim, second_rim):
    vmem = pl.BlockSpec(memory_space=pltpu.VMEM)
    return pl.pallas_call(
        lambda *refs: rim_body(grid, *refs),
        in_specs=[pl.BlockSpec(memory_space=pltpu.SMEM)] + [vmem] * 9,
        out_specs=vmem,
        out_shape=jax.ShapeDtypeStruct((C2 * BY // 2, HALF), F32),
        scratch_shapes=[pltpu.VMEM((K2, 256), BF16), pltpu.VMEM((K2, 256), BF16)],
        compiler_params=pltpu.CompilerParams(vmem_limit_bytes=48 * 2**20),
        name="rim",
    )(edge, joined, received, own_columns, inner_out, first, second, bias, first_rim, second_rim)


def rim_tables(weight1, bias1, weight2):
    kernel = weight1[:, 0]
    planes = jnp.stack([kernel[:, 1:3], kernel[:, 0:2]], axis=1)
    reach = np.zeros((3, 3, 8), np.float32)
    for i in range(3):
        for dx in range(3):
            reach[i, dx, i + dx] = 1.0
    table = jnp.einsum("czpyx,kxq->kczypq", planes, jnp.asarray(reach), precision=EXACT)
    ones = np.zeros((3, BZ, 8), np.float32)
    ones[0, 0, PHASES] = 1.0
    table = table + bias1[None, :, None, None, None, None] * jnp.asarray(ones)
    first = table.reshape(3 * C1 * BZ, 3 * BZ * 8)
    second = jnp.transpose(weight2[:, :, 1:3], (0, 3, 4, 1, 2)).reshape(C2, 9 * C1 * BZ)

    def stacked(values):
        coarse, fine = split_host(values)
        return jnp.concatenate([coarse, coarse, fine], axis=1)

    return stacked(first), stacked(second)


def first_table(weight, bias):
    kernel = weight[:, 0]
    planes = jnp.stack([kernel[:, 1:3], kernel[:, 0:2]], axis=1)
    reach = np.zeros((HID_ROWS, 3, WIN), np.float32)
    for i in range(HID_ROWS):
        for dy in range(3):
            reach[i, dy, i + dy] = 1.0
    table = jnp.einsum("czpyx,iys->iczxps", planes, jnp.asarray(reach), precision=EXACT)
    coarse, fine = split_host(table.reshape(HID, K1))
    each = jnp.tile(jnp.repeat(bias, BZ), HID_ROWS)
    one = lax.reduce_precision(each, 8, 7)
    two = lax.reduce_precision(each - one, 8, 7)
    three = each - one - two
    tail = jnp.stack([one, two, three], axis=1).astype(BF16)
    tail = jnp.pad(tail, ((0, 0), (0, 16 - 3)))
    return jnp.concatenate([coarse, coarse, fine, tail], axis=1)


def second_table(weight):
    reach = np.zeros((OUT_ROWS, 3, HID_ROWS), np.float32)
    for i in range(OUT_ROWS):
        for dy in range(3):
            reach[i, dy, 2 * i + dy] = 1.0
    table = jnp.einsum("oczyx,iyh->ioxhcz", weight[:, :, 1:3], jnp.asarray(reach), precision=EXACT)
    coarse, fine = split_host(table.reshape(OUTM, K2))
    return jnp.concatenate([coarse, fine], axis=0)


def body(strips, routes, conv1_weight, conv1_bias, conv2_weight, conv2_bias):
    rows = lax.axis_size("gx")
    cols = lax.axis_size("gy")
    senders = rows * cols
    per_pair = max(1, STRIPS // senders)
    axes = ("gx", "gy")
    at_row = lax.axis_index("gx").astype(jnp.int32)
    at_col = lax.axis_index("gy").astype(jnp.int32)
    edge = jnp.stack([at_row, at_col])
    routes_t = routes.T
    outgoing = pack(strips, routes_t, senders, per_pair)
    arrived = lax.all_to_all(outgoing, axes, split_axis=0, concat_axis=0, tiled=True)
    first = first_table(conv1_weight, conv1_bias)
    second = second_table(conv2_weight)
    bias = jnp.broadcast_to(conv2_bias[:, None], (C2, HALF))
    first_rim, second_rim = rim_tables(conv1_weight, conv1_bias, conv2_weight)
    joined, messages, own_columns = join((rows, cols), edge, arrived, per_pair)
    received = lax.all_to_all(messages, axes, split_axis=0, concat_axis=0, tiled=True)
    inner_out = inner(joined, first, second, bias)
    features = rim(
        (rows, cols), edge, joined, received, own_columns, inner_out, first, second, bias, first_rim, second_rim
    )
    return features.reshape(C2, 1, BY // 2, HALF)


def solution(mesh):
    in_specs = (P(("gx", "gy"), None, None, None), P(("gx", "gy"), None), P(), P(), P(), P())
    out_specs = P(None, None, "gx", "gy")
    return jax.shard_map(body, mesh=mesh, in_specs=in_specs, out_specs=out_specs, check_vma=False)
```

```python
import jax
import jax.numpy as jnp
import numpy as np
from jax import lax
from jax.experimental import pallas as pl
from jax.experimental.pallas import tpu as pltpu
from jax.sharding import PartitionSpec as P

BZ = 2
BY = 128
BX = 128
BLK = 2
STRIPS = 64
SY = 16
SX = 128
C1 = 16
C2 = 32

COLS = BX * BLK
HALF = COLS // 2
TOP = 2
SROW = 136
OUT_ROWS = 4
HID_ROWS = 9
WIN = 16
BLOCKS = BY // (2 * OUT_ROWS)
PHASES = 5
JOIN_UNROLL = 8
K1 = 3 * BZ * WIN
HID = HID_ROWS * C1 * BZ
K2 = 3 * HID
OUTM = OUT_ROWS * C2

EXACT = lax.Precision.HIGHEST
F32 = jnp.float32
BF16 = jnp.bfloat16


def iota(shape, dim):
    return lax.broadcasted_iota(jnp.int32, shape, dim)


def split_kernel(x):
    hi = x.astype(BF16)
    return hi, (x - hi.astype(F32)).astype(BF16)


def split_host(x):
    hi = lax.reduce_precision(x, 8, 7)
    return hi.astype(BF16), (x - hi).astype(BF16)


def chunk_of(per_pair):
    return BZ * SY // 2 * per_pair + 1


def sent_routes(per_pair, senders, route_rows):
    held = route_rows.shape[1]
    match = (route_rows[0:1, :] == iota((senders, held), 0)) & (route_rows[1:2, :] == 1)
    flags = jnp.where(match, 1.0, 0.0)
    before = jnp.where(iota((held, held), 0) < iota((held, held), 1), 1.0, 0.0)
    earlier = jnp.dot(flags.astype(BF16), before.astype(BF16), preferred_element_type=F32)
    fields = jnp.concatenate([route_rows[...].astype(F32), jnp.zeros((120, held), F32)], axis=0)
    fields = fields.astype(BF16)
    return [
        lax.dot_general(
            jnp.where(match & (earlier == float(r)), 1.0, 0.0).astype(BF16),
            fields,
            (((1,), (1,)), ((), ())),
            preferred_element_type=F32,
        )
        for r in range(per_pair)
    ]


def pack_body(per_pair, routes, route_rows, strips, payload, count, sems):
    pairs = BZ * SY // 2
    chunk = chunk_of(per_pair)
    held = route_rows.shape[1]
    senders = payload.shape[0] // chunk
    full = held == STRIPS

    def clear(i, carry):
        count[i] = 0
        return carry

    lax.fori_loop(0, senders, clear, 0, unroll=8)

    def copy(k, at):
        source = strips.at[pl.ds(k * pairs, pairs)]
        return pltpu.make_async_copy(source, payload.at[pl.ds(at, pairs)], sems.at[0 if full else k])

    def when_live(k, run):
        if full:
            run()
        else:
            pl.when(routes[1, k] == 1)(run)

    def place(k, carry):
        def run():
            dest = routes[0, k]
            rank = jnp.minimum(count[dest], per_pair - 1)
            count[dest] = rank + 1
            copy(k, dest * chunk + rank * pairs).start()

        when_live(k, run)
        return carry

    lax.fori_loop(0, held, place, 0, unroll=8)

    for r, rows in enumerate(sent_routes(per_pair, senders, route_rows)):
        for dest in range(senders):
            payload[dest * chunk + chunk - 1, r : r + 1, :] = rows[dest : dest + 1, :]

    if full:
        everything = held * pairs
        pltpu.make_async_copy(strips, payload.at[pl.ds(0, everything)], sems.at[0]).wait()
    else:

        def finish(k, carry):
            when_live(k, lambda: copy(k, 0).wait())
            return carry

        lax.fori_loop(0, held, finish, 0)


def pack_full_body(per_pair, routes, route_rows, strips, payload, buffer, sent, count, sems_in, sems_out):
    pairs = BZ * SY // 2
    senders = payload.shape[0]
    held = senders * per_pair
    groups = sems_in.shape[0]
    per_group = senders // groups

    def fetch(g):
        at = pl.ds(g * per_group, per_group)
        return pltpu.make_async_copy(strips.at[at], buffer.at[at], sems_in.at[g])

    for g in range(groups):
        fetch(g).start()

    def clear(i, carry):
        count[i] = 0
        return carry

    lax.fori_loop(0, senders, clear, 0, unroll=8)
    for r, rows in enumerate(sent_routes(per_pair, senders, route_rows)):
        for dest in range(senders):
            sent[dest, r : r + 1, :] = rows[dest : dest + 1, :]
    tail = pltpu.make_async_copy(sent, payload.at[:, per_pair * pairs], sems_out.at[0])
    tail.start()

    def place(row, carry):
        for r in range(per_pair):
            dest = routes[0, row * per_pair + r]
            rank = jnp.minimum(count[dest], per_pair - 1)
            count[dest] = rank + 1
            pltpu.make_async_copy(
                buffer.at[row, pl.ds(r * pairs, pairs)],
                payload.at[dest, pl.ds(rank * pairs, pairs)],
                sems_out.at[1],
            ).start()
        return carry

    for g in range(groups):
        fetch(g).wait()
        lax.fori_loop(g * per_group, (g + 1) * per_group, place, 0, unroll=4)
    tail.wait()
    pltpu.make_async_copy(buffer, payload.at[:, pl.ds(0, per_pair * pairs)], sems_out.at[1]).wait()


def pack_full(strips, routes_t, senders, per_pair):
    pairs = BZ * SY // 2
    strips = strips.reshape(senders, per_pair * pairs, 2, SX)
    payload = pl.pallas_call(
        lambda *refs: pack_full_body(per_pair, *refs),
        in_specs=[
            pl.BlockSpec(memory_space=pltpu.SMEM),
            pl.BlockSpec(memory_space=pltpu.VMEM),
            pl.BlockSpec(memory_space=pl.ANY),
        ],
        out_specs=pl.BlockSpec(memory_space=pl.ANY),
        out_shape=jax.ShapeDtypeStruct((senders, chunk_of(per_pair), 2, SX), F32),
        scratch_shapes=[
            pltpu.VMEM(strips.shape, F32),
            pltpu.VMEM((senders, 2, SX), F32),
            pltpu.SMEM((senders,), jnp.int32),
            pltpu.SemaphoreType.DMA((4,)),
            pltpu.SemaphoreType.DMA((2,)),
        ],
        name="pack",
    )(routes_t, routes_t, strips)
    return payload.reshape(senders * chunk_of(per_pair), 2, SX)


def pack(strips, routes_t, senders, per_pair):
    held = strips.shape[0]
    if held == STRIPS and held == senders * per_pair and per_pair == 2 and senders % 16 == 0:
        return pack_full(strips, routes_t, senders, per_pair)
    pairs = BZ * SY // 2
    vmem = pl.BlockSpec(memory_space=pltpu.VMEM)
    return pl.pallas_call(
        lambda *refs: pack_body(per_pair, *refs),
        in_specs=[
            pl.BlockSpec(memory_space=pltpu.SMEM),
            vmem,
            pl.BlockSpec(memory_space=pl.ANY),
        ],
        out_specs=vmem,
        out_shape=jax.ShapeDtypeStruct((senders * chunk_of(per_pair), 2, SX), F32),
        scratch_shapes=[
            pltpu.SMEM((senders,), jnp.int32),
            pltpu.SemaphoreType.DMA((1 if held == STRIPS else held,)),
        ],
        name="pack",
    )(routes_t, routes_t, strips.reshape(held * pairs, 2, SX))


EDGE_COLUMNS = (COLS - 4, COLS - 3, COLS - 2, COLS - 1, 0, 1, 2)


def edge_column(i):
    return jnp.where(i < 4, COLS - 4 + i, i - 4)


def pick_columns():
    row = iota((8, COLS), 0)
    col = iota((8, COLS), 1)
    chosen = None
    for i, x in enumerate(EDGE_COLUMNS):
        here = (row == i) & (col == x // 2 + (x % 2) * HALF)
        chosen = here if chosen is None else chosen | here
    return jnp.where(chosen, 1.0, 0.0)


def join_body(per_pair, grid, edge, routes, strips, joined, messages, own_columns, data, place_y, pieces, route_rows, params, sem):
    senders = routes.shape[0]
    slots = senders * per_pair
    chunk = 2 * chunk_of(per_pair)
    fetch = pltpu.make_async_copy(routes.at[:, chunk_of(per_pair) - 1], params, sem)
    fetch.start()
    columns = jnp.concatenate(
        [strips[pl.ds(chunk - 2 + r, senders, stride=chunk), :] for r in range(per_pair)], axis=0
    )
    route_rows[...] = columns
    columns = columns.astype(jnp.int32)

    def field(q):
        return columns[:, q : q + 1]

    live = field(1)
    top = field(2)
    left = field(3)
    ramp = field(7)
    y = iota((slots, BY), 1) - top
    weight_y = jnp.where((y >= 0) & (y < SY), jnp.minimum(jnp.minimum(y + 1, SY - y), ramp), 0)
    col = iota((slots, COLS), 1)
    x = jnp.where(col < HALF, 2 * col, 2 * (col - HALF) + 1) - left
    weight_x = jnp.where((x >= 0) & (x < SX), jnp.minimum(jnp.minimum(x + 1, SX - x), ramp), 0)
    weight_y = jnp.where(live == 1, weight_y, 0).astype(F32).astype(BF16)
    weight_x = weight_x.astype(F32).astype(BF16)
    over_rows = (((0,), (0,)), ((), ()))
    total = lax.dot_general(weight_y, weight_x, over_rows, preferred_element_type=F32)
    lane = iota((8, SX), 1)
    row_lane = iota((8, BY), 1)
    row_sub = iota((SY, BY), 0)
    to_edge = jnp.minimum(lane + 1, SX - lane).astype(F32)

    def twice(values):
        return jnp.concatenate([values, values], axis=0)

    def prepare(group, carry):
        blocks = [
            route_rows[pl.ds(pl.multiple_of(r * senders + 8 * group, 8), 8), :] for r in range(per_pair)
        ]
        for inside, r in [(i, r) for i in range(8) for r in range(per_pair)]:
            h = 8 * group + inside
            k = h * per_pair + r
            route = blocks[r][inside : inside + 1, :]

            def value(q):
                return jnp.broadcast_to(route[:, q : q + 1], (8, SX))

            frac_z = twice(value(4) * (1.0 / 16.0))
            frac_y = value(5) * (1.0 / 16.0)
            frac_x = value(6) * (1.0 / 16.0)
            ramp = value(7)
            weight = jnp.minimum(to_edge, ramp)
            here = twice(weight * (1.0 - frac_x))
            there = twice(jnp.where(lane < SX - 1, weight * frac_x, 0.0))
            at = h * chunk + r * BZ * SY
            first = strips[pl.ds(at, SY), :]
            second = strips[pl.ds(at + SY, SY), :]
            if slots != STRIPS:
                live = twice(value(1)) == 1.0
                first = jnp.where(live, first, 0.0)
                second = jnp.where(live, second, 0.0)
            plane0 = (1.0 - frac_z) * first + frac_z * second
            plane1 = (1.0 - frac_z) * second
            for z, plane in enumerate((plane0, plane1)):
                pieces[k, z * SY : (z + 1) * SY, :] = here * plane + there * pltpu.roll(plane, SX - 1, 1)
            y = row_lane - value(2).astype(jnp.int32)
            weight_y = jnp.minimum(jnp.minimum(y + 1, SY - y).astype(F32), ramp)
            stay_y = twice(weight_y * (1.0 - frac_y))
            move_y = twice(weight_y * frac_y)
            ahead = row_sub - twice(y)
            spread = jnp.where(ahead == 0, stay_y, jnp.where(ahead == 1, move_y, 0.0))
            place_y[pl.ds(k * SY, SY), :] = spread.astype(BF16)
        return carry

    lax.fori_loop(0, senders // 8, prepare, 0)
    fetch.wait()
    wide_lane = iota((SY, SX), 1)

    def shift(h, carry):
        for r in range(per_pair):
            k = h * per_pair + r
            left = params[h, r, 3].astype(jnp.int32)
            low_side = wide_lane >= left
            for z in range(BZ):
                turned = pltpu.roll(pieces[k, z * SY : (z + 1) * SY, :], left & (SX - 1), 1)
                low = jnp.where(low_side, turned, 0.0)
                high = jnp.where(low_side, 0.0, turned)
                for side, part in enumerate((low, high)):
                    coarse, fine = split_kernel(part)
                    at = z * COLS + side * SX
                    data[pl.ds(k * SY, SY), at : at + SX] = coarse
                    data[pl.ds(k * SY, SY), BZ * COLS + at : BZ * COLS + at + SX] = fine
        return carry

    lax.fori_loop(0, senders, shift, 0, unroll=JOIN_UNROLL)

    sums = lax.dot_general(place_y[...], data[...], over_rows, preferred_element_type=F32)
    sums = sums[:, : BZ * COLS] + sums[:, BZ * COLS :]

    src = iota((COLS, COLS), 0)
    dst = iota((COLS, COLS), 1)
    order = (src == jnp.where(dst < HALF, 2 * dst, 2 * (dst - HALF) + 1)).astype(F32).astype(BF16)
    along = iota((8, COLS), 1)
    natural = edge_column(iota((8, COLS), 0))
    pick = jnp.where(along == natural, 1.0, 0.0).astype(BF16)
    x = edge_column(iota((slots, 8), 1)) - left
    rim_weight = jnp.where((x >= 0) & (x < SX), jnp.minimum(jnp.minimum(x + 1, SX - x), ramp), 0)
    rim_weight = rim_weight.astype(F32).astype(BF16)
    rim_total = lax.dot_general(rim_weight, weight_y, over_rows, preferred_element_type=F32)
    right_rows = []
    left_rows = []
    down_rows = []
    up_rows = []
    for z in range(BZ):
        coarse, fine = split_kernel(sums[:, z * COLS : (z + 1) * COLS])
        ordered = jnp.dot(coarse, order, preferred_element_type=F32) + jnp.dot(
            fine, order, preferred_element_type=F32
        )
        value = ordered / total
        joined[z] = value
        over_lanes = (((1,), (1,)), ((), ()))
        columns_as_rows = lax.dot_general(
            pick, coarse, over_lanes, preferred_element_type=F32
        ) + lax.dot_general(pick, fine, over_lanes, preferred_element_type=F32)
        columns_as_rows = columns_as_rows / rim_total
        own_columns[8 * z : 8 * z + 8, :] = columns_as_rows
        right_rows.append(columns_as_rows[2:4])
        left_rows.append(columns_as_rows[4:5])
        for half in range(2):
            cut = value[:, half * HALF : (half + 1) * HALF]
            down_rows.append(cut[BY - 2 : BY])
            up_rows.append(cut[0:1])

    def tile(rows):
        have = sum(r.shape[0] for r in rows)
        if have < 8:
            rows = rows + [jnp.zeros((8 - have, HALF), F32)]
        return jnp.concatenate(rows, axis=0)

    right = tile(right_rows)
    left = tile(left_rows)
    down = tile(down_rows)
    up = tile(up_rows)
    at_row = edge[0]
    at_col = edge[1]
    rows, cols = grid

    def send(dy, dx, values):
        to_row = at_row + dy
        to_col = at_col + dx

        @pl.when((to_row >= 0) & (to_row < rows) & (to_col >= 0) & (to_col < cols))
        def _():
            messages[to_row * cols + to_col] = values

    for dy in (-1, 0, 1):
        send(dy, 1, right)
        send(dy, -1, left)
    send(1, 0, down)
    send(-1, 0, up)


def join(grid, edge, arrived, per_pair):
    senders = arrived.shape[0] // chunk_of(per_pair)
    slots = senders * per_pair
    vmem = pl.BlockSpec(memory_space=pltpu.VMEM)
    return pl.pallas_call(
        lambda *refs: join_body(per_pair, grid, *refs),
        in_specs=[pl.BlockSpec(memory_space=pltpu.SMEM), pl.BlockSpec(memory_space=pl.ANY), vmem],
        out_specs=[vmem, vmem, vmem],
        out_shape=[
            jax.ShapeDtypeStruct((BZ, BY, COLS), F32),
            jax.ShapeDtypeStruct((senders, 8, HALF), F32),
            jax.ShapeDtypeStruct((8 * BZ, BY), F32),
        ],
        scratch_shapes=[
            pltpu.VMEM((slots * SY, 2 * BZ * COLS), BF16),
            pltpu.VMEM((slots * SY, BY), BF16),
            pltpu.VMEM((slots, BZ * SY, SX), F32),
            pltpu.VMEM((slots, SX), F32),
            pltpu.SMEM((senders, 2, SX), F32),
            pltpu.SemaphoreType.DMA,
        ],
        compiler_params=pltpu.CompilerParams(vmem_limit_bytes=48 * 2**20),
        name="join",
    )(
        edge,
        arrived.reshape(senders, chunk_of(per_pair), 2, SX),
        arrived.reshape(arrived.shape[0] * 2, SX),
    )


def two_blocks(wide, blocks, keep, first, second, bias, out, coarse_h, fine_h, keep_top=None):
    ones = jnp.ones((16, 256), BF16)
    for group in range(3):
        coarse = [wide[group + dx, z][0] for dx in range(3) for z in range(BZ)]
        fine = [wide[group + dx, z][1] for dx in range(3) for z in range(BZ)]
        stacked = jnp.concatenate(coarse + fine + coarse + [ones], axis=0)
        hidden = jnp.dot(first[...], stacked, preferred_element_type=F32)
        hidden = jnp.maximum(hidden, 0.0)
        if group == 0 and keep is not None:
            hidden = hidden * keep
        if keep_top is not None:
            top = C1 * BZ
            hidden = jnp.concatenate([hidden[:top] * keep_top, hidden[top:]], axis=0)
        coarse, fine = split_kernel(hidden)
        coarse_h[group * HID : (group + 1) * HID, :] = coarse
        fine_h[group * HID : (group + 1) * HID, :] = fine
    both = jnp.dot(second[...], coarse_h[...], preferred_element_type=F32)
    rest = jnp.dot(second[:OUTM, :], fine_h[...], preferred_element_type=F32)
    result = both[:OUTM] + both[OUTM:] + rest
    for side, b in enumerate(blocks):
        for r in range(OUT_ROWS):
            out[pl.ds(OUT_ROWS * b + r, C2, stride=BY // 2), :] = (
                result[r * C2 : (r + 1) * C2, side * HALF : (side + 1) * HALF] + bias[...]
            )


def inner_body(joined, first, second, bias, out, phases, coarse_h, fine_h):
    for z in range(BZ):
        even = joined[z, :, :HALF]
        odd = joined[z, :, HALF:]
        parts = (pltpu.roll(even, 1, 1), pltpu.roll(odd, 1, 1), even, odd, pltpu.roll(even, HALF - 1, 1))
        for j, part in enumerate(parts):
            phases[j, z, TOP : TOP + BY, :] = part
    half = (BLOCKS - 2) // 2
    for step in range(half):
        blocks = (1 + step, 1 + step + half)
        wide = {}
        for j in range(PHASES):
            for z in range(BZ):
                cut = [phases[j, z, 8 * b : 8 * b + WIN, :] for b in blocks]
                wide[j, z] = split_kernel(jnp.concatenate(cut, axis=1))
        slot = step % 2
        two_blocks(
            wide, blocks, None, first, second, bias, out, coarse_h.at[slot], fine_h.at[slot]
        )


def inner(joined, first, second, bias):
    vmem = pl.BlockSpec(memory_space=pltpu.VMEM)
    return pl.pallas_call(
        inner_body,
        in_specs=[vmem] * 4,
        out_specs=vmem,
        out_shape=jax.ShapeDtypeStruct((C2 * BY // 2, HALF), F32),
        scratch_shapes=[
            pltpu.VMEM((PHASES, BZ, SROW, HALF), F32),
            pltpu.VMEM((2, K2, 256), BF16),
            pltpu.VMEM((2, K2, 256), BF16),
        ],
        compiler_params=pltpu.CompilerParams(vmem_limit_bytes=48 * 2**20),
        name="inner",
    )(joined, first, second, bias)


def rim_body(
    grid, edge, joined, received, own_columns, inner_out, first, second, bias, first_rim, second_rim,
    out, coarse_h, fine_h,
):
    at_row = edge[0]
    at_col = edge[1]
    rows, cols = grid
    halo = {}
    for dy in (-1, 0, 1):
        for dx in (-1, 0, 1):
            if (dy, dx) == (0, 0):
                continue
            row = at_row + dy
            col = at_col + dx
            there = (row >= 0) & (row < rows) & (col >= 0) & (col < cols)
            index = jnp.where(there, row * cols + col, 0)
            halo[dy, dx] = jnp.where(there, received[index], 0.0)
    no_row = at_row == 0
    no_col = at_col == 0
    wide_lane = iota((8, 256), 1)

    def stored(above, here, below):
        zero = jnp.zeros((8, 128), F32)
        turned = [
            pltpu.roll(jnp.concatenate([part, zero], axis=1), by, 1)
            for part, by in ((above, 256 - (BY - TOP)), (here, TOP), (below, TOP + BY))
        ]
        low = jnp.where(wide_lane < TOP, turned[0], turned[1])
        return jnp.where(
            wide_lane < TOP + BY, low, jnp.where(wide_lane == TOP + BY, turned[2], 0.0)
        )

    from_left = stored(halo[-1, -1], halo[0, -1], halo[1, -1])
    from_right = stored(halo[-1, 1], halo[0, 1], halo[1, 1])
    from_above = halo[-1, 0]
    from_below = halo[1, 0]

    tall_lane = iota((2 * WIN, HALF), 1)
    sides = jnp.concatenate([from_left[:4], from_right[:4]], axis=0)
    ends = jnp.concatenate(
        [sides[:, :WIN], sides[:, SROW - WIN : SROW], jnp.zeros((8, 128 - 2 * WIN), F32)], axis=1
    )
    side_columns = jnp.transpose(ends)[: 2 * WIN]

    def column(row):
        return side_columns[:, row : row + 1]

    wide = {}
    for z in range(BZ):
        halves = []
        for half in range(2):
            own = joined[z, :, half * HALF : (half + 1) * HALF]
            at = 4 * z + 2 * half
            bottom = 2 * z + half
            ends = [
                from_above[at : at + 2],
                own[: WIN - TOP],
                own[SROW - WIN - TOP :],
                from_below[bottom : bottom + 1],
                jnp.zeros((SROW - BY - TOP - 1, HALF), F32),
            ]
            halves.append(jnp.concatenate(ends, axis=0))
        even, odd = halves
        parts = (
            jnp.where(tall_lane == 0, column(2 * z), pltpu.roll(even, 1, 1)),
            jnp.where(tall_lane == 0, column(2 * z + 1), pltpu.roll(odd, 1, 1)),
            even,
            odd,
            jnp.where(
                tall_lane == HALF - 1, column(4 + z), pltpu.roll(even, HALF - 1, 1)
            ),
        )
        for j, part in enumerate(parts):
            wide[j, z] = split_kernel(jnp.concatenate([part[:WIN], part[WIN:]], axis=1))

    left_rows = []
    right_rows = []
    cut = []
    for z in range(BZ):
        for c in range(2):
            at = 4 * z + c
            cut.append(jnp.concatenate([from_above[at : at + 1], from_above[at + 2 : at + 3]], axis=1))
        cut.append(jnp.concatenate([from_below[2 * z : 2 * z + 1], from_below[2 * z + 1 : 2 * z + 2]], axis=1))
        cut.append(jnp.zeros((5, COLS), F32))
    outer_all = lax.dot_general(
        pick_columns(),
        jnp.concatenate(cut, axis=0),
        (((1,), (1,)), ((), ())),
        precision=EXACT,
        preferred_element_type=F32,
    )
    outer_all = jnp.concatenate([outer_all, jnp.zeros((8, 256 - 8 * BZ), F32)], axis=1)
    for z in range(BZ):
        outer = pltpu.roll(outer_all, 256 - 8 * z, 1) if z else outer_all
        here = jnp.concatenate([own_columns[8 * z : 8 * z + 8, :], jnp.zeros((8, BY), F32)], axis=1)
        own = jnp.where(
            wide_lane < TOP,
            outer,
            jnp.where(
                wide_lane < TOP + BY,
                pltpu.roll(here, TOP, 1),
                jnp.where(wide_lane == TOP + BY, pltpu.roll(outer, BY, 1), 0.0),
            ),
        )
        one = jnp.ones((1, 256), F32)
        rest = jnp.zeros((2, 256), F32)
        left_rows += [from_left[2 * z : 2 * z + 2], own[4:7], one, rest]
        right_rows += [own[0:4], from_right[z : z + 1], one, rest]
    both = jnp.concatenate(
        [jnp.concatenate(left_rows, axis=0), jnp.concatenate(right_rows, axis=0)], axis=1
    )

    def reach(values):
        return jnp.concatenate([values] + [pltpu.roll(values, 512 - dy, 1) for dy in (1, 2)], axis=0)

    def product(table, values):
        coarse, fine = split_kernel(reach(values))
        stacked = jnp.concatenate([coarse, fine, coarse], axis=0)
        return jnp.dot(table[...], stacked, preferred_element_type=F32)

    hidden = product(first_rim, both)
    hidden = jnp.maximum(hidden, 0.0)
    lane = iota((3 * C1 * BZ, 512), 1)
    depth = iota((3 * C1 * BZ, 512), 0)
    outside = no_row & ((lane & 255) == 0)
    outside = outside | (no_col & (lane < 256) & (depth < C1 * BZ))
    hidden = jnp.where(outside, 0.0, hidden)
    found = product(second_rim, hidden)
    every = jnp.where(iota((BY // 2, 256), 1) == 2 * iota((BY // 2, 256), 0), 1.0, 0.0).astype(BF16)
    parts = []
    for side in range(2):
        parts += split_kernel(found[:, side * 256 : (side + 1) * 256] + bias[:, :1])
    turned = lax.dot_general(
        every,
        jnp.concatenate(parts, axis=0),
        (((1,), (1,)), ((), ())),
        preferred_element_type=F32,
    )
    columns = [
        turned[:, 2 * side * C2 : (2 * side + 1) * C2] + turned[:, (2 * side + 1) * C2 : (2 * side + 2) * C2]
        for side in range(2)
    ]
    out_lane = iota((BY // 2, HALF), 1)
    for o in range(C2):
        at = o * (BY // 2)
        values = inner_out[at : at + BY // 2, :]
        values = jnp.where(out_lane == 0, columns[0][:, o : o + 1], values)
        out[at : at + BY // 2, :] = jnp.where(out_lane == HALF - 1, columns[1][:, o : o + 1], values)

    keep = jnp.where(no_col & ((iota((1, 256), 1) & (HALF - 1)) == 0), 0.0, 1.0)
    keep_top = jnp.where(no_row & (iota((1, 256), 1) < HALF), 0.0, 1.0)
    two_blocks(
        wide, (0, BLOCKS - 1), keep, first, second, bias, out, coarse_h, fine_h, keep_top=keep_top
    )


def rim(grid, edge, joined, received, own_columns, inner_out, first, second, bias, first_rim, second_rim):
    vmem = pl.BlockSpec(memory_space=pltpu.VMEM)
    return pl.pallas_call(
        lambda *refs: rim_body(grid, *refs),
        in_specs=[pl.BlockSpec(memory_space=pltpu.SMEM)] + [vmem] * 9,
        out_specs=vmem,
        out_shape=jax.ShapeDtypeStruct((C2 * BY // 2, HALF), F32),
        scratch_shapes=[pltpu.VMEM((K2, 256), BF16), pltpu.VMEM((K2, 256), BF16)],
        compiler_params=pltpu.CompilerParams(vmem_limit_bytes=48 * 2**20),
        name="rim",
    )(edge, joined, received, own_columns, inner_out, first, second, bias, first_rim, second_rim)


def rim_tables(weight1, bias1, weight2):
    kernel = weight1[:, 0]
    planes = jnp.stack([kernel[:, 1:3], kernel[:, 0:2]], axis=1)
    reach = np.zeros((3, 3, 8), np.float32)
    for i in range(3):
        for dx in range(3):
            reach[i, dx, i + dx] = 1.0
    table = jnp.einsum("czpyx,kxq->kczypq", planes, jnp.asarray(reach), precision=EXACT)
    ones = np.zeros((3, BZ, 8), np.float32)
    ones[0, 0, PHASES] = 1.0
    table = table + bias1[None, :, None, None, None, None] * jnp.asarray(ones)
    first = table.reshape(3 * C1 * BZ, 3 * BZ * 8)
    second = jnp.transpose(weight2[:, :, 1:3], (0, 3, 4, 1, 2)).reshape(C2, 9 * C1 * BZ)

    def stacked(values):
        coarse, fine = split_host(values)
        return jnp.concatenate([coarse, coarse, fine], axis=1)

    return stacked(first), stacked(second)


def first_table(weight, bias):
    kernel = weight[:, 0]
    planes = jnp.stack([kernel[:, 1:3], kernel[:, 0:2]], axis=1)
    reach = np.zeros((HID_ROWS, 3, WIN), np.float32)
    for i in range(HID_ROWS):
        for dy in range(3):
            reach[i, dy, i + dy] = 1.0
    table = jnp.einsum("czpyx,iys->iczxps", planes, jnp.asarray(reach), precision=EXACT)
    coarse, fine = split_host(table.reshape(HID, K1))
    each = jnp.tile(jnp.repeat(bias, BZ), HID_ROWS)
    one = lax.reduce_precision(each, 8, 7)
    two = lax.reduce_precision(each - one, 8, 7)
    three = each - one - two
    tail = jnp.stack([one, two, three], axis=1).astype(BF16)
    tail = jnp.pad(tail, ((0, 0), (0, 16 - 3)))
    return jnp.concatenate([coarse, coarse, fine, tail], axis=1)


def second_table(weight):
    reach = np.zeros((OUT_ROWS, 3, HID_ROWS), np.float32)
    for i in range(OUT_ROWS):
        for dy in range(3):
            reach[i, dy, 2 * i + dy] = 1.0
    table = jnp.einsum("oczyx,iyh->ioxhcz", weight[:, :, 1:3], jnp.asarray(reach), precision=EXACT)
    coarse, fine = split_host(table.reshape(OUTM, K2))
    return jnp.concatenate([coarse, fine], axis=0)


def body(strips, routes, conv1_weight, conv1_bias, conv2_weight, conv2_bias):
    rows = lax.axis_size("gx")
    cols = lax.axis_size("gy")
    senders = rows * cols
    per_pair = max(1, STRIPS // senders)
    axes = ("gx", "gy")
    at_row = lax.axis_index("gx").astype(jnp.int32)
    at_col = lax.axis_index("gy").astype(jnp.int32)
    edge = jnp.stack([at_row, at_col])
    routes_t = routes.T
    outgoing = pack(strips, routes_t, senders, per_pair)
    arrived = lax.all_to_all(outgoing, axes, split_axis=0, concat_axis=0, tiled=True)
    first = first_table(conv1_weight, conv1_bias)
    second = second_table(conv2_weight)
    bias = jnp.broadcast_to(conv2_bias[:, None], (C2, HALF))
    first_rim, second_rim = rim_tables(conv1_weight, conv1_bias, conv2_weight)
    joined, messages, own_columns = join((rows, cols), edge, arrived, per_pair)
    received = lax.all_to_all(messages, axes, split_axis=0, concat_axis=0, tiled=True)
    inner_out = inner(joined, first, second, bias)
    features = rim(
        (rows, cols), edge, joined, received, own_columns, inner_out, first, second, bias, first_rim, second_rim
    )
    return features.reshape(C2, 1, BY // 2, HALF)


def solution(mesh):
    in_specs = (P(("gx", "gy"), None, None, None), P(("gx", "gy"), None), P(), P(), P(), P())
    out_specs = P(None, None, "gx", "gy")
    return jax.shard_map(body, mesh=mesh, in_specs=in_specs, out_specs=out_specs, check_vma=False)
```

```python
import jax
import jax.numpy as jnp
import numpy as np
from jax import lax
from jax.experimental import pallas as pl
from jax.experimental.pallas import tpu as pltpu
from jax.sharding import PartitionSpec as P

BZ = 2
BY = 128
BX = 128
BLK = 2
STRIPS = 64
SY = 16
SX = 128
C1 = 16
C2 = 32

COLS = BX * BLK
HALF = COLS // 2
TOP = 2
SROW = 136
OUT_ROWS = 4
HID_ROWS = 9
WIN = 16
BLOCKS = BY // (2 * OUT_ROWS)
PHASES = 5
JOIN_UNROLL = 8
K1 = 3 * BZ * WIN
HID = HID_ROWS * C1 * BZ
K2 = 3 * HID
OUTM = OUT_ROWS * C2
LAST = BY - 2
ROW_HID = 3 * C1 * BZ

EXACT = lax.Precision.HIGHEST
F32 = jnp.float32
BF16 = jnp.bfloat16


def iota(shape, dim):
    return lax.broadcasted_iota(jnp.int32, shape, dim)


def split_kernel(x):
    hi = x.astype(BF16)
    return hi, (x - hi.astype(F32)).astype(BF16)


def split_host(x):
    hi = lax.reduce_precision(x, 8, 7)
    return hi.astype(BF16), (x - hi).astype(BF16)


def chunk_of(per_pair):
    return BZ * SY // 2 * per_pair + 1


def sent_routes(per_pair, senders, route_rows):
    held = route_rows.shape[1]
    match = (route_rows[0:1, :] == iota((senders, held), 0)) & (route_rows[1:2, :] == 1)
    flags = jnp.where(match, 1.0, 0.0)
    before = jnp.where(iota((held, held), 0) < iota((held, held), 1), 1.0, 0.0)
    earlier = jnp.dot(flags.astype(BF16), before.astype(BF16), preferred_element_type=F32)
    fields = jnp.concatenate([route_rows[...].astype(F32), jnp.zeros((120, held), F32)], axis=0)
    fields = fields.astype(BF16)
    return [
        lax.dot_general(
            jnp.where(match & (earlier == float(r)), 1.0, 0.0).astype(BF16),
            fields,
            (((1,), (1,)), ((), ())),
            preferred_element_type=F32,
        )
        for r in range(per_pair)
    ]


def pack_body(per_pair, routes, route_rows, strips, payload, count, sems):
    pairs = BZ * SY // 2
    chunk = chunk_of(per_pair)
    held = route_rows.shape[1]
    senders = payload.shape[0] // chunk
    full = held == STRIPS

    def clear(i, carry):
        count[i] = 0
        return carry

    lax.fori_loop(0, senders, clear, 0, unroll=8)

    def copy(k, at):
        source = strips.at[pl.ds(k * pairs, pairs)]
        return pltpu.make_async_copy(source, payload.at[pl.ds(at, pairs)], sems.at[0 if full else k])

    def when_live(k, run):
        if full:
            run()
        else:
            pl.when(routes[1, k] == 1)(run)

    def place(k, carry):
        def run():
            dest = routes[0, k]
            rank = jnp.minimum(count[dest], per_pair - 1)
            count[dest] = rank + 1
            copy(k, dest * chunk + rank * pairs).start()

        when_live(k, run)
        return carry

    lax.fori_loop(0, held, place, 0, unroll=8)

    for r, rows in enumerate(sent_routes(per_pair, senders, route_rows)):
        for dest in range(senders):
            payload[dest * chunk + chunk - 1, r : r + 1, :] = rows[dest : dest + 1, :]

    if full:
        everything = held * pairs
        pltpu.make_async_copy(strips, payload.at[pl.ds(0, everything)], sems.at[0]).wait()
    else:

        def finish(k, carry):
            when_live(k, lambda: copy(k, 0).wait())
            return carry

        lax.fori_loop(0, held, finish, 0)


def pack_full_body(per_pair, routes, route_rows, strips, payload, buffer, sent, count, sems_in, sems_out):
    pairs = BZ * SY // 2
    senders = payload.shape[0]
    held = senders * per_pair
    groups = sems_in.shape[0]
    per_group = senders // groups

    def fetch(g):
        at = pl.ds(g * per_group, per_group)
        return pltpu.make_async_copy(strips.at[at], buffer.at[at], sems_in.at[g])

    for g in range(groups):
        fetch(g).start()

    def clear(i, carry):
        count[i] = 0
        return carry

    lax.fori_loop(0, senders, clear, 0, unroll=8)
    for r, rows in enumerate(sent_routes(per_pair, senders, route_rows)):
        for dest in range(senders):
            sent[dest, r : r + 1, :] = rows[dest : dest + 1, :]
    tail = pltpu.make_async_copy(sent, payload.at[:, per_pair * pairs], sems_out.at[0])
    tail.start()

    def place(row, carry):
        for r in range(per_pair):
            dest = routes[0, row * per_pair + r]
            rank = jnp.minimum(count[dest], per_pair - 1)
            count[dest] = rank + 1
            pltpu.make_async_copy(
                buffer.at[row, pl.ds(r * pairs, pairs)],
                payload.at[dest, pl.ds(rank * pairs, pairs)],
                sems_out.at[1],
            ).start()
        return carry

    for g in range(groups):
        fetch(g).wait()
        lax.fori_loop(g * per_group, (g + 1) * per_group, place, 0, unroll=4)
    tail.wait()
    pltpu.make_async_copy(buffer, payload.at[:, pl.ds(0, per_pair * pairs)], sems_out.at[1]).wait()


def pack_full(strips, routes_t, senders, per_pair):
    pairs = BZ * SY // 2
    strips = strips.reshape(senders, per_pair * pairs, 2, SX)
    payload = pl.pallas_call(
        lambda *refs: pack_full_body(per_pair, *refs),
        in_specs=[
            pl.BlockSpec(memory_space=pltpu.SMEM),
            pl.BlockSpec(memory_space=pltpu.VMEM),
            pl.BlockSpec(memory_space=pl.ANY),
        ],
        out_specs=pl.BlockSpec(memory_space=pl.ANY),
        out_shape=jax.ShapeDtypeStruct((senders, chunk_of(per_pair), 2, SX), F32),
        scratch_shapes=[
            pltpu.VMEM(strips.shape, F32),
            pltpu.VMEM((senders, 2, SX), F32),
            pltpu.SMEM((senders,), jnp.int32),
            pltpu.SemaphoreType.DMA((4,)),
            pltpu.SemaphoreType.DMA((2,)),
        ],
        name="pack",
    )(routes_t, routes_t, strips)
    return payload.reshape(senders * chunk_of(per_pair), 2, SX)


def pack(strips, routes_t, senders, per_pair):
    held = strips.shape[0]
    if held == STRIPS and held == senders * per_pair and per_pair == 2 and senders % 16 == 0:
        return pack_full(strips, routes_t, senders, per_pair)
    pairs = BZ * SY // 2
    vmem = pl.BlockSpec(memory_space=pltpu.VMEM)
    return pl.pallas_call(
        lambda *refs: pack_body(per_pair, *refs),
        in_specs=[
            pl.BlockSpec(memory_space=pltpu.SMEM),
            vmem,
            pl.BlockSpec(memory_space=pl.ANY),
        ],
        out_specs=vmem,
        out_shape=jax.ShapeDtypeStruct((senders * chunk_of(per_pair), 2, SX), F32),
        scratch_shapes=[
            pltpu.SMEM((senders,), jnp.int32),
            pltpu.SemaphoreType.DMA((1 if held == STRIPS else held,)),
        ],
        name="pack",
    )(routes_t, routes_t, strips.reshape(held * pairs, 2, SX))


EDGE_COLUMNS = (COLS - 4, COLS - 3, COLS - 2, COLS - 1, 0, 1, 2)


def edge_column(i):
    return jnp.where(i < 4, COLS - 4 + i, i - 4)


def pick_columns():
    row = iota((8, COLS), 0)
    col = iota((8, COLS), 1)
    chosen = None
    for i, x in enumerate(EDGE_COLUMNS):
        here = (row == i) & (col == x // 2 + (x % 2) * HALF)
        chosen = here if chosen is None else chosen | here
    return jnp.where(chosen, 1.0, 0.0)


def join_body(per_pair, grid, edge, routes, strips, joined, messages, own_columns, data, place_y, pieces, route_rows, params, sem):
    senders = routes.shape[0]
    slots = senders * per_pair
    chunk = 2 * chunk_of(per_pair)
    fetch = pltpu.make_async_copy(routes.at[:, chunk_of(per_pair) - 1], params, sem)
    fetch.start()
    columns = jnp.concatenate(
        [strips[pl.ds(chunk - 2 + r, senders, stride=chunk), :] for r in range(per_pair)], axis=0
    )
    route_rows[...] = columns
    columns = columns.astype(jnp.int32)

    def field(q):
        return columns[:, q : q + 1]

    live = field(1)
    top = field(2)
    left = field(3)
    ramp = field(7)
    y = iota((slots, BY), 1) - top
    weight_y = jnp.where((y >= 0) & (y < SY), jnp.minimum(jnp.minimum(y + 1, SY - y), ramp), 0)
    col = iota((slots, COLS), 1)
    x = jnp.where(col < HALF, 2 * col, 2 * (col - HALF) + 1) - left
    weight_x = jnp.where((x >= 0) & (x < SX), jnp.minimum(jnp.minimum(x + 1, SX - x), ramp), 0)
    weight_y = jnp.where(live == 1, weight_y, 0).astype(F32).astype(BF16)
    weight_x = weight_x.astype(F32).astype(BF16)
    over_rows = (((0,), (0,)), ((), ()))
    total = lax.dot_general(weight_y, weight_x, over_rows, preferred_element_type=F32)
    lane = iota((8, SX), 1)
    row_lane = iota((8, BY), 1)
    row_sub = iota((SY, BY), 0)
    to_edge = jnp.minimum(lane + 1, SX - lane).astype(F32)

    def twice(values):
        return jnp.concatenate([values, values], axis=0)

    def prepare(group, carry):
        blocks = [
            route_rows[pl.ds(pl.multiple_of(r * senders + 8 * group, 8), 8), :] for r in range(per_pair)
        ]
        for inside, r in [(i, r) for i in range(8) for r in range(per_pair)]:
            h = 8 * group + inside
            k = h * per_pair + r
            route = blocks[r][inside : inside + 1, :]

            def value(q):
                return jnp.broadcast_to(route[:, q : q + 1], (8, SX))

            frac_z = twice(value(4) * (1.0 / 16.0))
            frac_y = value(5) * (1.0 / 16.0)
            frac_x = value(6) * (1.0 / 16.0)
            ramp = value(7)
            weight = jnp.minimum(to_edge, ramp)
            here = twice(weight * (1.0 - frac_x))
            there = twice(jnp.where(lane < SX - 1, weight * frac_x, 0.0))
            at = h * chunk + r * BZ * SY
            first = strips[pl.ds(at, SY), :]
            second = strips[pl.ds(at + SY, SY), :]
            if slots != STRIPS:
                live = twice(value(1)) == 1.0
                first = jnp.where(live, first, 0.0)
                second = jnp.where(live, second, 0.0)
            plane0 = (1.0 - frac_z) * first + frac_z * second
            plane1 = (1.0 - frac_z) * second
            for z, plane in enumerate((plane0, plane1)):
                pieces[k, z * SY : (z + 1) * SY, :] = here * plane + there * pltpu.roll(plane, SX - 1, 1)
            y = row_lane - value(2).astype(jnp.int32)
            weight_y = jnp.minimum(jnp.minimum(y + 1, SY - y).astype(F32), ramp)
            stay_y = twice(weight_y * (1.0 - frac_y))
            move_y = twice(weight_y * frac_y)
            ahead = row_sub - twice(y)
            spread = jnp.where(ahead == 0, stay_y, jnp.where(ahead == 1, move_y, 0.0))
            place_y[pl.ds(k * SY, SY), :] = spread.astype(BF16)
        return carry

    lax.fori_loop(0, senders // 8, prepare, 0)
    fetch.wait()
    wide_lane = iota((SY, SX), 1)

    def shift(h, carry):
        for r in range(per_pair):
            k = h * per_pair + r
            left = params[h, r, 3].astype(jnp.int32)
            low_side = wide_lane >= left
            for z in range(BZ):
                turned = pltpu.roll(pieces[k, z * SY : (z + 1) * SY, :], left & (SX - 1), 1)
                low = jnp.where(low_side, turned, 0.0)
                high = jnp.where(low_side, 0.0, turned)
                for side, part in enumerate((low, high)):
                    coarse, fine = split_kernel(part)
                    at = z * COLS + side * SX
                    data[pl.ds(k * SY, SY), at : at + SX] = coarse
                    data[pl.ds(k * SY, SY), BZ * COLS + at : BZ * COLS + at + SX] = fine
        return carry

    lax.fori_loop(0, senders, shift, 0, unroll=JOIN_UNROLL)

    sums = lax.dot_general(place_y[...], data[...], over_rows, preferred_element_type=F32)
    sums = sums[:, : BZ * COLS] + sums[:, BZ * COLS :]

    src = iota((COLS, COLS), 0)
    dst = iota((COLS, COLS), 1)
    order = (src == jnp.where(dst < HALF, 2 * dst, 2 * (dst - HALF) + 1)).astype(F32).astype(BF16)
    along = iota((8, COLS), 1)
    natural = edge_column(iota((8, COLS), 0))
    pick = jnp.where(along == natural, 1.0, 0.0).astype(BF16)
    x = edge_column(iota((slots, 8), 1)) - left
    rim_weight = jnp.where((x >= 0) & (x < SX), jnp.minimum(jnp.minimum(x + 1, SX - x), ramp), 0)
    rim_weight = rim_weight.astype(F32).astype(BF16)
    rim_total = lax.dot_general(rim_weight, weight_y, over_rows, preferred_element_type=F32)
    right_rows = []
    left_rows = []
    down_rows = []
    up_rows = []
    for z in range(BZ):
        coarse, fine = split_kernel(sums[:, z * COLS : (z + 1) * COLS])
        ordered = jnp.dot(coarse, order, preferred_element_type=F32) + jnp.dot(
            fine, order, preferred_element_type=F32
        )
        value = ordered / total
        joined[z] = value
        over_lanes = (((1,), (1,)), ((), ()))
        columns_as_rows = lax.dot_general(
            pick, coarse, over_lanes, preferred_element_type=F32
        ) + lax.dot_general(pick, fine, over_lanes, preferred_element_type=F32)
        columns_as_rows = columns_as_rows / rim_total
        own_columns[8 * z : 8 * z + 8, :] = columns_as_rows
        right_rows.append(columns_as_rows[2:4])
        left_rows.append(columns_as_rows[4:5])
        for half in range(2):
            cut = value[:, half * HALF : (half + 1) * HALF]
            down_rows.append(cut[BY - 2 : BY])
            up_rows.append(cut[0:1])

    def tile(rows):
        have = sum(r.shape[0] for r in rows)
        if have < 8:
            rows = rows + [jnp.zeros((8 - have, HALF), F32)]
        return jnp.concatenate(rows, axis=0)

    right = tile(right_rows)
    left = tile(left_rows)
    down = tile(down_rows)
    up = tile(up_rows)
    at_row = edge[0]
    at_col = edge[1]
    rows, cols = grid

    def send(dy, dx, values):
        to_row = at_row + dy
        to_col = at_col + dx

        @pl.when((to_row >= 0) & (to_row < rows) & (to_col >= 0) & (to_col < cols))
        def _():
            messages[to_row * cols + to_col] = values

    for dy in (-1, 0, 1):
        send(dy, 1, right)
        send(dy, -1, left)
    send(1, 0, down)
    send(-1, 0, up)


def join(grid, edge, arrived, per_pair):
    senders = arrived.shape[0] // chunk_of(per_pair)
    slots = senders * per_pair
    vmem = pl.BlockSpec(memory_space=pltpu.VMEM)
    return pl.pallas_call(
        lambda *refs: join_body(per_pair, grid, *refs),
        in_specs=[pl.BlockSpec(memory_space=pltpu.SMEM), pl.BlockSpec(memory_space=pl.ANY), vmem],
        out_specs=[vmem, vmem, vmem],
        out_shape=[
            jax.ShapeDtypeStruct((BZ, BY, COLS), F32),
            jax.ShapeDtypeStruct((senders, 8, HALF), F32),
            jax.ShapeDtypeStruct((8 * BZ, BY), F32),
        ],
        scratch_shapes=[
            pltpu.VMEM((slots * SY, 2 * BZ * COLS), BF16),
            pltpu.VMEM((slots * SY, BY), BF16),
            pltpu.VMEM((slots, BZ * SY, SX), F32),
            pltpu.VMEM((slots, SX), F32),
            pltpu.SMEM((senders, 2, SX), F32),
            pltpu.SemaphoreType.DMA,
        ],
        compiler_params=pltpu.CompilerParams(vmem_limit_bytes=48 * 2**20),
        name="join",
    )(
        edge,
        arrived.reshape(senders, chunk_of(per_pair), 2, SX),
        arrived.reshape(arrived.shape[0] * 2, SX),
    )


def hidden_parts(wide, table, count, coarse_h, fine_h, keep=None, keep_top=None):
    ones = jnp.ones((16, 256), BF16)
    for group in range(3):
        coarse = [wide[group + dx, z][0] for dx in range(3) for z in range(BZ)]
        fine = [wide[group + dx, z][1] for dx in range(3) for z in range(BZ)]
        stacked = jnp.concatenate(coarse + fine + coarse + [ones], axis=0)
        hidden = jnp.dot(table, stacked, preferred_element_type=F32)
        hidden = jnp.maximum(hidden, 0.0)
        if group == 0 and keep is not None:
            hidden = hidden * keep
        if keep_top is not None:
            top = C1 * BZ
            hidden = jnp.concatenate([hidden[:top] * keep_top, hidden[top:]], axis=0)
        coarse, fine = split_kernel(hidden)
        coarse_h[group * count : (group + 1) * count, :] = coarse
        fine_h[group * count : (group + 1) * count, :] = fine


def results(second, count, coarse_h, fine_h):
    both = jnp.dot(second[...], coarse_h[...], preferred_element_type=F32)
    rest = jnp.dot(second[:count, :], fine_h[...], preferred_element_type=F32)
    return both[:count] + both[count:] + rest


def inner_body(joined, first, second, bias, out, phases, coarse_h, fine_h):
    for z in range(BZ):
        even = joined[z, :, :HALF]
        odd = joined[z, :, HALF:]
        parts = (pltpu.roll(even, 1, 1), pltpu.roll(odd, 1, 1), even, odd, pltpu.roll(even, HALF - 1, 1))
        for j, part in enumerate(parts):
            phases[j, z, 0:8, :] = jnp.zeros((8, HALF), F32)
            phases[j, z, SROW - 8 : SROW, :] = jnp.zeros((8, HALF), F32)
            phases[j, z, TOP : TOP + BY, :] = part
    half = BLOCKS // 2
    for step in range(half):
        blocks = (step, step + half)
        wide = {}
        for j in range(PHASES):
            for z in range(BZ):
                cut = [phases[j, z, 8 * b : 8 * b + WIN, :] for b in blocks]
                wide[j, z] = split_kernel(jnp.concatenate(cut, axis=1))
        scratch = (coarse_h.at[step % 2], fine_h.at[step % 2])
        hidden_parts(wide, first[...], HID, *scratch)
        result = results(second, OUTM, *scratch)
        for side, b in enumerate(blocks):
            for r in range(OUT_ROWS):
                out[pl.ds(OUT_ROWS * b + r, C2, stride=BY // 2), :] = (
                    result[r * C2 : (r + 1) * C2, side * HALF : (side + 1) * HALF] + bias[...]
                )


def inner(joined, first, second, bias):
    vmem = pl.BlockSpec(memory_space=pltpu.VMEM)
    return pl.pallas_call(
        inner_body,
        in_specs=[vmem] * 4,
        out_specs=vmem,
        out_shape=jax.ShapeDtypeStruct((C2 * BY // 2, HALF), F32),
        scratch_shapes=[
            pltpu.VMEM((PHASES, BZ, SROW, HALF), F32),
            pltpu.VMEM((2, K2, 256), BF16),
            pltpu.VMEM((2, K2, 256), BF16),
        ],
        compiler_params=pltpu.CompilerParams(vmem_limit_bytes=48 * 2**20),
        name="inner",
    )(joined, first, second, bias)


def rim_body(
    grid, edge, joined, received, own_columns, inner_out, first, second, bias, first_rim, second_rim,
    out, coarse_h, fine_h,
):
    at_row = edge[0]
    at_col = edge[1]
    rows, cols = grid
    halo = {}
    for dy in (-1, 0, 1):
        for dx in (-1, 0, 1):
            if (dy, dx) == (0, 0):
                continue
            row = at_row + dy
            col = at_col + dx
            there = (row >= 0) & (row < rows) & (col >= 0) & (col < cols)
            index = jnp.where(there, row * cols + col, 0)
            halo[dy, dx] = jnp.where(there, received[index], 0.0)
    no_row = at_row == 0
    no_col = at_col == 0
    wide_lane = iota((8, 256), 1)

    def stored(above, here, below):
        zero = jnp.zeros((8, 128), F32)
        turned = [
            pltpu.roll(jnp.concatenate([part, zero], axis=1), by, 1)
            for part, by in ((above, 256 - (BY - TOP)), (here, TOP), (below, TOP + BY))
        ]
        low = jnp.where(wide_lane < TOP, turned[0], turned[1])
        return jnp.where(
            wide_lane < TOP + BY, low, jnp.where(wide_lane == TOP + BY, turned[2], 0.0)
        )

    from_left = stored(halo[-1, -1], halo[0, -1], halo[1, -1])
    from_right = stored(halo[-1, 1], halo[0, 1], halo[1, 1])
    from_above = halo[-1, 0]
    from_below = halo[1, 0]

    tall_lane = iota((2 * WIN, HALF), 1)
    sides = jnp.concatenate([from_left[:4], from_right[:4]], axis=0)
    ends = jnp.concatenate(
        [sides[:, :WIN], sides[:, LAST : LAST + WIN], jnp.zeros((8, 128 - 2 * WIN), F32)], axis=1
    )
    side_columns = jnp.transpose(ends)[: 2 * WIN]

    def column(row):
        return side_columns[:, row : row + 1]

    wide = {}
    for z in range(BZ):
        halves = []
        for half in range(2):
            own = joined[z, :, half * HALF : (half + 1) * HALF]
            at = 4 * z + 2 * half
            bottom = 2 * z + half
            ends = [
                from_above[at : at + 2],
                own[: WIN - TOP],
                own[LAST - TOP :],
                from_below[bottom : bottom + 1],
                jnp.zeros((LAST + WIN - BY - TOP - 1, HALF), F32),
            ]
            halves.append(jnp.concatenate(ends, axis=0))
        even, odd = halves
        parts = (
            jnp.where(tall_lane == 0, column(2 * z), pltpu.roll(even, 1, 1)),
            jnp.where(tall_lane == 0, column(2 * z + 1), pltpu.roll(odd, 1, 1)),
            even,
            odd,
            jnp.where(
                tall_lane == HALF - 1, column(4 + z), pltpu.roll(even, HALF - 1, 1)
            ),
        )
        for j, part in enumerate(parts):
            wide[j, z] = split_kernel(jnp.concatenate([part[:WIN], part[WIN:]], axis=1))

    left_rows = []
    right_rows = []
    cut = []
    for z in range(BZ):
        for c in range(2):
            at = 4 * z + c
            cut.append(jnp.concatenate([from_above[at : at + 1], from_above[at + 2 : at + 3]], axis=1))
        cut.append(jnp.concatenate([from_below[2 * z : 2 * z + 1], from_below[2 * z + 1 : 2 * z + 2]], axis=1))
        cut.append(jnp.zeros((5, COLS), F32))
    outer_all = lax.dot_general(
        pick_columns(),
        jnp.concatenate(cut, axis=0),
        (((1,), (1,)), ((), ())),
        precision=EXACT,
        preferred_element_type=F32,
    )
    outer_all = jnp.concatenate([outer_all, jnp.zeros((8, 256 - 8 * BZ), F32)], axis=1)
    for z in range(BZ):
        outer = pltpu.roll(outer_all, 256 - 8 * z, 1) if z else outer_all
        here = jnp.concatenate([own_columns[8 * z : 8 * z + 8, :], jnp.zeros((8, BY), F32)], axis=1)
        own = jnp.where(
            wide_lane < TOP,
            outer,
            jnp.where(
                wide_lane < TOP + BY,
                pltpu.roll(here, TOP, 1),
                jnp.where(wide_lane == TOP + BY, pltpu.roll(outer, BY, 1), 0.0),
            ),
        )
        one = jnp.ones((1, 256), F32)
        rest = jnp.zeros((2, 256), F32)
        left_rows += [from_left[2 * z : 2 * z + 2], own[4:7], one, rest]
        right_rows += [own[0:4], from_right[z : z + 1], one, rest]
    coarse, fine = split_kernel(jnp.concatenate(left_rows + right_rows, axis=0))
    src = iota((256, 256), 0)
    dst = iota((256, 256), 1)
    apart = src == jnp.where(dst < 128, 2 * dst, 2 * (dst - 128) + 1)
    apart = jnp.where(apart, 1.0, 0.0).astype(BF16)
    lines = jnp.dot(jnp.concatenate([coarse, fine], axis=0), apart, preferred_element_type=F32)
    lines = lines[:32] + lines[32:]
    out_rows = BY // 2
    line_lane = iota((16, 128), 1)

    def stored_rows(t):
        cut = lines[:, (t % 2) * 128 : (t % 2) * 128 + 128]
        return jnp.where(
            line_lane < out_rows,
            pltpu.roll(cut[:16], (128 - t // 2) % 128, 1) if t // 2 else cut[:16],
            pltpu.roll(cut[16:], out_rows - t // 2, 1),
        )

    taken = [stored_rows(t) for t in range(5)]

    def product(table, values):
        coarse, fine = split_kernel(values)
        stacked = jnp.concatenate([coarse, fine, coarse], axis=0)
        return jnp.dot(table[...], stacked, preferred_element_type=F32)

    reach = [jnp.concatenate([taken[row + dy] for row in range(3)], axis=1) for dy in range(3)]
    hidden = jnp.maximum(product(first_rim, jnp.concatenate(reach, axis=0)), 0.0)
    lane = iota((3 * C1 * BZ, 384), 1)
    depth = iota((3 * C1 * BZ, 384), 0)
    outside = no_row & ((lane == 0) | (lane == out_rows))
    outside = outside | (no_col & ((lane & 127) < out_rows) & (depth < C1 * BZ))
    hidden = jnp.where(outside, 0.0, hidden)
    reach = [hidden[:, row * 128 : (row + 1) * 128] for row in range(3)]
    found = product(second_rim, jnp.concatenate(reach, axis=0)) + bias[...]
    turned = jnp.transpose(found)
    columns = [turned[:out_rows], turned[out_rows:]]
    out_lane = iota((BY // 2, HALF), 1)
    for o in range(C2):
        at = o * (BY // 2)
        values = inner_out[at : at + BY // 2, :]
        values = jnp.where(out_lane == 0, columns[0][:, o : o + 1], values)
        out[at : at + BY // 2, :] = jnp.where(out_lane == HALF - 1, columns[1][:, o : o + 1], values)

    keep = jnp.where(no_col & ((iota((1, 256), 1) & (HALF - 1)) == 0), 0.0, 1.0)
    keep_top = jnp.where(no_row & (iota((1, 256), 1) < HALF), 0.0, 1.0)
    hidden_parts(wide, first[:ROW_HID, :], ROW_HID, coarse_h, fine_h, keep, keep_top)
    result = results(second, C2, coarse_h, fine_h)
    for side, at in enumerate((0, BY // 2 - 1)):
        out[pl.ds(at, C2, stride=BY // 2), :] = (
            result[:, side * HALF : (side + 1) * HALF] + bias[...]
        )


def rim(grid, edge, joined, received, own_columns, inner_out, first, second, bias, first_rim, second_rim):
    vmem = pl.BlockSpec(memory_space=pltpu.VMEM)
    return pl.pallas_call(
        lambda *refs: rim_body(grid, *refs),
        in_specs=[pl.BlockSpec(memory_space=pltpu.SMEM)] + [vmem] * 9,
        out_specs=vmem,
        out_shape=jax.ShapeDtypeStruct((C2 * BY // 2, HALF), F32),
        scratch_shapes=[pltpu.VMEM((3 * ROW_HID, 256), BF16), pltpu.VMEM((3 * ROW_HID, 256), BF16)],
        compiler_params=pltpu.CompilerParams(vmem_limit_bytes=48 * 2**20),
        name="rim",
    )(edge, joined, received, own_columns, inner_out, first, second, bias, first_rim, second_rim)


def rim_tables(weight1, bias1, weight2):
    kernel = weight1[:, 0]
    planes = jnp.stack([kernel[:, 1:3], kernel[:, 0:2]], axis=1)
    reach = np.zeros((3, 3, 8), np.float32)
    for i in range(3):
        for dx in range(3):
            reach[i, dx, i + dx] = 1.0
    table = jnp.einsum("czpyx,kxq->kczypq", planes, jnp.asarray(reach), precision=EXACT)
    ones = np.zeros((3, BZ, 8), np.float32)
    ones[0, 0, PHASES] = 1.0
    table = table + bias1[None, :, None, None, None, None] * jnp.asarray(ones)
    first = table.reshape(3 * C1 * BZ, 3 * BZ * 8)
    second = jnp.transpose(weight2[:, :, 1:3], (0, 3, 4, 1, 2)).reshape(C2, 9 * C1 * BZ)

    def stacked(values):
        coarse, fine = split_host(values)
        return jnp.concatenate([coarse, coarse, fine], axis=1)

    row = jnp.transpose(weight2[:, :, 1:3], (0, 4, 3, 1, 2)).reshape(C2, 3 * ROW_HID)
    return stacked(first), stacked(second), jnp.concatenate(split_host(row), axis=0)


def first_table(weight, bias):
    kernel = weight[:, 0]
    planes = jnp.stack([kernel[:, 1:3], kernel[:, 0:2]], axis=1)
    reach = np.zeros((HID_ROWS, 3, WIN), np.float32)
    for i in range(HID_ROWS):
        for dy in range(3):
            reach[i, dy, i + dy] = 1.0
    table = jnp.einsum("czpyx,iys->iczxps", planes, jnp.asarray(reach), precision=EXACT)
    coarse, fine = split_host(table.reshape(HID, K1))
    each = jnp.tile(jnp.repeat(bias, BZ), HID_ROWS)
    one = lax.reduce_precision(each, 8, 7)
    two = lax.reduce_precision(each - one, 8, 7)
    three = each - one - two
    tail = jnp.stack([one, two, three], axis=1).astype(BF16)
    tail = jnp.pad(tail, ((0, 0), (0, 16 - 3)))
    return jnp.concatenate([coarse, coarse, fine, tail], axis=1)


def second_table(weight):
    reach = np.zeros((OUT_ROWS, 3, HID_ROWS), np.float32)
    for i in range(OUT_ROWS):
        for dy in range(3):
            reach[i, dy, 2 * i + dy] = 1.0
    table = jnp.einsum("oczyx,iyh->ioxhcz", weight[:, :, 1:3], jnp.asarray(reach), precision=EXACT)
    coarse, fine = split_host(table.reshape(OUTM, K2))
    return jnp.concatenate([coarse, fine], axis=0)


def body(strips, routes, conv1_weight, conv1_bias, conv2_weight, conv2_bias):
    rows = lax.axis_size("gx")
    cols = lax.axis_size("gy")
    senders = rows * cols
    per_pair = max(1, STRIPS // senders)
    axes = ("gx", "gy")
    at_row = lax.axis_index("gx").astype(jnp.int32)
    at_col = lax.axis_index("gy").astype(jnp.int32)
    edge = jnp.stack([at_row, at_col])
    routes_t = routes.T
    outgoing = pack(strips, routes_t, senders, per_pair)
    arrived = lax.all_to_all(outgoing, axes, split_axis=0, concat_axis=0, tiled=True)
    first = first_table(conv1_weight, conv1_bias)
    second = second_table(conv2_weight)
    bias = jnp.broadcast_to(conv2_bias[:, None], (C2, HALF))
    first_rim, second_rim, second_row = rim_tables(conv1_weight, conv1_bias, conv2_weight)
    joined, messages, own_columns = join((rows, cols), edge, arrived, per_pair)
    received = lax.all_to_all(messages, axes, split_axis=0, concat_axis=0, tiled=True)
    inner_out = inner(joined, first, second, bias)
    features = rim(
        (rows, cols), edge, joined, received, own_columns, inner_out, first, second_row, bias, first_rim, second_rim
    )
    return features.reshape(C2, 1, BY // 2, HALF)


def solution(mesh):
    in_specs = (P(("gx", "gy"), None, None, None), P(("gx", "gy"), None), P(), P(), P(), P())
    out_specs = P(None, None, "gx", "gy")
    return jax.shard_map(body, mesh=mesh, in_specs=in_specs, out_specs=out_specs, check_vma=False)
```

```python
import jax
import jax.numpy as jnp
import numpy as np
from jax import lax
from jax.experimental import pallas as pl
from jax.experimental.pallas import tpu as pltpu
from jax.sharding import PartitionSpec as P

BZ = 2
BY = 128
BX = 128
BLK = 2
STRIPS = 64
SY = 16
SX = 128
C1 = 16
C2 = 32

COLS = BX * BLK
HALF = COLS // 2
TOP = 2
SROW = 136
OUT_ROWS = 4
HID_ROWS = 9
WIN = 16
BLOCKS = BY // (2 * OUT_ROWS)
PHASES = 5
JOIN_UNROLL = 8
K1 = 3 * BZ * WIN
HID = HID_ROWS * C1 * BZ
K2 = 3 * HID
OUTM = OUT_ROWS * C2
LAST = BY - 2
ROW_HID = 3 * C1 * BZ

EXACT = lax.Precision.HIGHEST
F32 = jnp.float32
BF16 = jnp.bfloat16


def iota(shape, dim):
    return lax.broadcasted_iota(jnp.int32, shape, dim)


def split_kernel(x):
    hi = x.astype(BF16)
    return hi, (x - hi.astype(F32)).astype(BF16)


def split_host(x):
    hi = lax.reduce_precision(x, 8, 7)
    return hi.astype(BF16), (x - hi).astype(BF16)


def chunk_of(per_pair):
    return BZ * SY // 2 * per_pair + 1


def sent_routes(per_pair, senders, route_rows):
    held = route_rows.shape[1]
    match = (route_rows[0:1, :] == iota((senders, held), 0)) & (route_rows[1:2, :] == 1)
    flags = jnp.where(match, 1.0, 0.0)
    before = jnp.where(iota((held, held), 0) < iota((held, held), 1), 1.0, 0.0)
    earlier = jnp.dot(flags.astype(BF16), before.astype(BF16), preferred_element_type=F32)
    fields = jnp.concatenate([route_rows[...].astype(F32), jnp.zeros((120, held), F32)], axis=0)
    fields = fields.astype(BF16)
    return [
        lax.dot_general(
            jnp.where(match & (earlier == float(r)), 1.0, 0.0).astype(BF16),
            fields,
            (((1,), (1,)), ((), ())),
            preferred_element_type=F32,
        )
        for r in range(per_pair)
    ]


def pack_body(per_pair, routes, route_rows, strips, payload, count, sems):
    pairs = BZ * SY // 2
    chunk = chunk_of(per_pair)
    held = route_rows.shape[1]
    senders = payload.shape[0] // chunk
    full = held == STRIPS

    def clear(i, carry):
        count[i] = 0
        return carry

    lax.fori_loop(0, senders, clear, 0, unroll=8)

    def copy(k, at):
        source = strips.at[pl.ds(k * pairs, pairs)]
        return pltpu.make_async_copy(source, payload.at[pl.ds(at, pairs)], sems.at[0 if full else k])

    def when_live(k, run):
        if full:
            run()
        else:
            pl.when(routes[1, k] == 1)(run)

    def place(k, carry):
        def run():
            dest = routes[0, k]
            rank = jnp.minimum(count[dest], per_pair - 1)
            count[dest] = rank + 1
            copy(k, dest * chunk + rank * pairs).start()

        when_live(k, run)
        return carry

    lax.fori_loop(0, held, place, 0, unroll=8)

    for r, rows in enumerate(sent_routes(per_pair, senders, route_rows)):
        for dest in range(senders):
            payload[dest * chunk + chunk - 1, r : r + 1, :] = rows[dest : dest + 1, :]

    if full:
        everything = held * pairs
        pltpu.make_async_copy(strips, payload.at[pl.ds(0, everything)], sems.at[0]).wait()
    else:

        def finish(k, carry):
            when_live(k, lambda: copy(k, 0).wait())
            return carry

        lax.fori_loop(0, held, finish, 0)


def pack_full_body(per_pair, routes, route_rows, strips, payload, buffer, sent, count, sems_in, sems_out):
    pairs = BZ * SY // 2
    senders = payload.shape[0]
    held = senders * per_pair
    groups = sems_in.shape[0]
    per_group = senders // groups

    def fetch(g):
        at = pl.ds(g * per_group, per_group)
        return pltpu.make_async_copy(strips.at[at], buffer.at[at], sems_in.at[g])

    for g in range(groups):
        fetch(g).start()

    def clear(i, carry):
        count[i] = 0
        return carry

    lax.fori_loop(0, senders, clear, 0, unroll=8)
    for r, rows in enumerate(sent_routes(per_pair, senders, route_rows)):
        for dest in range(senders):
            sent[dest, r : r + 1, :] = rows[dest : dest + 1, :]
    tail = pltpu.make_async_copy(sent, payload.at[:, per_pair * pairs], sems_out.at[0])
    tail.start()

    def place(row, carry):
        for r in range(per_pair):
            dest = routes[0, row * per_pair + r]
            rank = jnp.minimum(count[dest], per_pair - 1)
            count[dest] = rank + 1
            pltpu.make_async_copy(
                buffer.at[row, pl.ds(r * pairs, pairs)],
                payload.at[dest, pl.ds(rank * pairs, pairs)],
                sems_out.at[1],
            ).start()
        return carry

    for g in range(groups):
        fetch(g).wait()
        lax.fori_loop(g * per_group, (g + 1) * per_group, place, 0, unroll=4)
    tail.wait()
    pltpu.make_async_copy(buffer, payload.at[:, pl.ds(0, per_pair * pairs)], sems_out.at[1]).wait()


def pack_full(strips, routes_t, senders, per_pair):
    pairs = BZ * SY // 2
    strips = strips.reshape(senders, per_pair * pairs, 2, SX)
    payload = pl.pallas_call(
        lambda *refs: pack_full_body(per_pair, *refs),
        in_specs=[
            pl.BlockSpec(memory_space=pltpu.SMEM),
            pl.BlockSpec(memory_space=pltpu.VMEM),
            pl.BlockSpec(memory_space=pl.ANY),
        ],
        out_specs=pl.BlockSpec(memory_space=pl.ANY),
        out_shape=jax.ShapeDtypeStruct((senders, chunk_of(per_pair), 2, SX), F32),
        scratch_shapes=[
            pltpu.VMEM(strips.shape, F32),
            pltpu.VMEM((senders, 2, SX), F32),
            pltpu.SMEM((senders,), jnp.int32),
            pltpu.SemaphoreType.DMA((4,)),
            pltpu.SemaphoreType.DMA((2,)),
        ],
        name="pack",
    )(routes_t, routes_t, strips)
    return payload.reshape(senders * chunk_of(per_pair), 2, SX)


def pack(strips, routes_t, senders, per_pair):
    held = strips.shape[0]
    if held == STRIPS and held == senders * per_pair and per_pair == 2 and senders % 16 == 0:
        return pack_full(strips, routes_t, senders, per_pair)
    pairs = BZ * SY // 2
    vmem = pl.BlockSpec(memory_space=pltpu.VMEM)
    return pl.pallas_call(
        lambda *refs: pack_body(per_pair, *refs),
        in_specs=[
            pl.BlockSpec(memory_space=pltpu.SMEM),
            vmem,
            pl.BlockSpec(memory_space=pl.ANY),
        ],
        out_specs=vmem,
        out_shape=jax.ShapeDtypeStruct((senders * chunk_of(per_pair), 2, SX), F32),
        scratch_shapes=[
            pltpu.SMEM((senders,), jnp.int32),
            pltpu.SemaphoreType.DMA((1 if held == STRIPS else held,)),
        ],
        name="pack",
    )(routes_t, routes_t, strips.reshape(held * pairs, 2, SX))


EDGE_COLUMNS = (COLS - 4, COLS - 3, COLS - 2, COLS - 1, 0, 1, 2)


def edge_column(i):
    return jnp.where(i < 4, COLS - 4 + i, i - 4)


def pick_columns():
    row = iota((8, COLS), 0)
    col = iota((8, COLS), 1)
    chosen = None
    for i, x in enumerate(EDGE_COLUMNS):
        here = (row == i) & (col == x // 2 + (x % 2) * HALF)
        chosen = here if chosen is None else chosen | here
    return jnp.where(chosen, 1.0, 0.0)


def join_body(per_pair, grid, edge, routes, strips, joined, messages, own_columns, data, place_y, pieces, route_rows, params, sem, tiles, tile_sems):
    senders = routes.shape[0]
    slots = senders * per_pair
    chunk = 2 * chunk_of(per_pair)
    fetch = pltpu.make_async_copy(routes.at[:, chunk_of(per_pair) - 1], params, sem)
    fetch.start()
    columns = jnp.concatenate(
        [strips[pl.ds(chunk - 2 + r, senders, stride=chunk), :] for r in range(per_pair)], axis=0
    )
    route_rows[...] = columns
    columns = columns.astype(jnp.int32)

    def field(q):
        return columns[:, q : q + 1]

    live = field(1)
    top = field(2)
    left = field(3)
    ramp = field(7)
    y = iota((slots, BY), 1) - top
    weight_y = jnp.where((y >= 0) & (y < SY), jnp.minimum(jnp.minimum(y + 1, SY - y), ramp), 0)
    col = iota((slots, COLS), 1)
    x = jnp.where(col < HALF, 2 * col, 2 * (col - HALF) + 1) - left
    weight_x = jnp.where((x >= 0) & (x < SX), jnp.minimum(jnp.minimum(x + 1, SX - x), ramp), 0)
    weight_y = jnp.where(live == 1, weight_y, 0).astype(F32).astype(BF16)
    weight_x = weight_x.astype(F32).astype(BF16)
    over_rows = (((0,), (0,)), ((), ()))
    total = lax.dot_general(weight_y, weight_x, over_rows, preferred_element_type=F32)
    lane = iota((8, SX), 1)
    row_lane = iota((8, BY), 1)
    row_sub = iota((SY, BY), 0)
    to_edge = jnp.minimum(lane + 1, SX - lane).astype(F32)

    def twice(values):
        return jnp.concatenate([values, values], axis=0)

    def prepare(group, carry):
        blocks = [
            route_rows[pl.ds(pl.multiple_of(r * senders + 8 * group, 8), 8), :] for r in range(per_pair)
        ]
        for inside, r in [(i, r) for i in range(8) for r in range(per_pair)]:
            h = 8 * group + inside
            k = h * per_pair + r
            route = blocks[r][inside : inside + 1, :]

            def value(q):
                return jnp.broadcast_to(route[:, q : q + 1], (8, SX))

            frac_z = twice(value(4) * (1.0 / 16.0))
            frac_y = value(5) * (1.0 / 16.0)
            frac_x = value(6) * (1.0 / 16.0)
            ramp = value(7)
            weight = jnp.minimum(to_edge, ramp)
            here = twice(weight * (1.0 - frac_x))
            there = twice(jnp.where(lane < SX - 1, weight * frac_x, 0.0))
            at = h * chunk + r * BZ * SY
            first = strips[pl.ds(at, SY), :]
            second = strips[pl.ds(at + SY, SY), :]
            if slots != STRIPS:
                live = twice(value(1)) == 1.0
                first = jnp.where(live, first, 0.0)
                second = jnp.where(live, second, 0.0)
            plane0 = (1.0 - frac_z) * first + frac_z * second
            plane1 = (1.0 - frac_z) * second
            for z, plane in enumerate((plane0, plane1)):
                pieces[k, z * SY : (z + 1) * SY, :] = here * plane + there * pltpu.roll(plane, SX - 1, 1)
            y = row_lane - value(2).astype(jnp.int32)
            weight_y = jnp.minimum(jnp.minimum(y + 1, SY - y).astype(F32), ramp)
            stay_y = twice(weight_y * (1.0 - frac_y))
            move_y = twice(weight_y * frac_y)
            ahead = row_sub - twice(y)
            spread = jnp.where(ahead == 0, stay_y, jnp.where(ahead == 1, move_y, 0.0))
            place_y[pl.ds(k * SY, SY), :] = spread.astype(BF16)
        return carry

    lax.fori_loop(0, senders // 8, prepare, 0)
    fetch.wait()
    wide_lane = iota((SY, SX), 1)

    def shift(h, carry):
        for r in range(per_pair):
            k = h * per_pair + r
            left = params[h, r, 3].astype(jnp.int32)
            low_side = wide_lane >= left
            for z in range(BZ):
                turned = pltpu.roll(pieces[k, z * SY : (z + 1) * SY, :], left & (SX - 1), 1)
                low = jnp.where(low_side, turned, 0.0)
                high = jnp.where(low_side, 0.0, turned)
                for side, part in enumerate((low, high)):
                    coarse, fine = split_kernel(part)
                    at = z * COLS + side * SX
                    data[pl.ds(k * SY, SY), at : at + SX] = coarse
                    data[pl.ds(k * SY, SY), BZ * COLS + at : BZ * COLS + at + SX] = fine
        return carry

    lax.fori_loop(0, senders, shift, 0, unroll=JOIN_UNROLL)

    sums = lax.dot_general(place_y[...], data[...], over_rows, preferred_element_type=F32)
    sums = sums[:, : BZ * COLS] + sums[:, BZ * COLS :]

    src = iota((COLS, COLS), 0)
    dst = iota((COLS, COLS), 1)
    order = (src == jnp.where(dst < HALF, 2 * dst, 2 * (dst - HALF) + 1)).astype(F32).astype(BF16)
    along = iota((8, COLS), 1)
    natural = edge_column(iota((8, COLS), 0))
    pick = jnp.where(along == natural, 1.0, 0.0).astype(BF16)
    x = edge_column(iota((slots, 8), 1)) - left
    rim_weight = jnp.where((x >= 0) & (x < SX), jnp.minimum(jnp.minimum(x + 1, SX - x), ramp), 0)
    rim_weight = rim_weight.astype(F32).astype(BF16)
    rim_total = lax.dot_general(rim_weight, weight_y, over_rows, preferred_element_type=F32)
    right_rows = []
    left_rows = []
    down_rows = []
    up_rows = []
    for z in range(BZ):
        coarse, fine = split_kernel(sums[:, z * COLS : (z + 1) * COLS])
        ordered = jnp.dot(coarse, order, preferred_element_type=F32) + jnp.dot(
            fine, order, preferred_element_type=F32
        )
        value = ordered / total
        joined[z] = value
        over_lanes = (((1,), (1,)), ((), ()))
        columns_as_rows = lax.dot_general(
            pick, coarse, over_lanes, preferred_element_type=F32
        ) + lax.dot_general(pick, fine, over_lanes, preferred_element_type=F32)
        columns_as_rows = columns_as_rows / rim_total
        own_columns[8 * z : 8 * z + 8, :] = columns_as_rows
        right_rows.append(columns_as_rows[2:4])
        left_rows.append(columns_as_rows[4:5])
        for half in range(2):
            cut = value[:, half * HALF : (half + 1) * HALF]
            down_rows.append(cut[BY - 2 : BY])
            up_rows.append(cut[0:1])

    def tile(rows):
        have = sum(r.shape[0] for r in rows)
        if have < 8:
            rows = rows + [jnp.zeros((8 - have, HALF), F32)]
        return jnp.concatenate(rows, axis=0)

    right = tile(right_rows)
    left = tile(left_rows)
    down = tile(down_rows)
    up = tile(up_rows)
    at_row = edge[0]
    at_col = edge[1]
    rows, cols = grid
    for i, values in enumerate((right, left, down, up)):
        tiles[i] = values
    sends = [(dy, 1, 0) for dy in (-1, 0, 1)] + [(dy, -1, 1) for dy in (-1, 0, 1)]
    sends += [(1, 0, 2), (-1, 0, 3)]

    def each(finish):
        for n, (dy, dx, i) in enumerate(sends):
            to_row = at_row + dy
            to_col = at_col + dx
            there = (to_row >= 0) & (to_row < rows) & (to_col >= 0) & (to_col < cols)
            at = jnp.where(there, to_row * cols + to_col, 0)
            copy = pltpu.make_async_copy(tiles.at[i], messages.at[at], tile_sems.at[n])
            pl.when(there)(copy.wait if finish else copy.start)

    each(False)
    each(True)


def join(grid, edge, arrived, per_pair):
    senders = arrived.shape[0] // chunk_of(per_pair)
    slots = senders * per_pair
    vmem = pl.BlockSpec(memory_space=pltpu.VMEM)
    return pl.pallas_call(
        lambda *refs: join_body(per_pair, grid, *refs),
        in_specs=[pl.BlockSpec(memory_space=pltpu.SMEM), pl.BlockSpec(memory_space=pl.ANY), vmem],
        out_specs=[vmem, pl.BlockSpec(memory_space=pl.ANY), vmem],
        out_shape=[
            jax.ShapeDtypeStruct((BZ, BY, COLS), F32),
            jax.ShapeDtypeStruct((senders, 8, HALF), F32),
            jax.ShapeDtypeStruct((8 * BZ, BY), F32),
        ],
        scratch_shapes=[
            pltpu.VMEM((slots * SY, 2 * BZ * COLS), BF16),
            pltpu.VMEM((slots * SY, BY), BF16),
            pltpu.VMEM((slots, BZ * SY, SX), F32),
            pltpu.VMEM((slots, SX), F32),
            pltpu.SMEM((senders, 2, SX), F32),
            pltpu.SemaphoreType.DMA,
            pltpu.VMEM((4, 8, HALF), F32),
            pltpu.SemaphoreType.DMA((8,)),
        ],
        compiler_params=pltpu.CompilerParams(vmem_limit_bytes=48 * 2**20),
        name="join",
    )(
        edge,
        arrived.reshape(senders, chunk_of(per_pair), 2, SX),
        arrived.reshape(arrived.shape[0] * 2, SX),
    )


def hidden_parts(wide, table, count, coarse_h, fine_h, keep=None, keep_top=None):
    ones = jnp.ones((16, 256), BF16)
    for group in range(3):
        coarse = [wide[group + dx, z][0] for dx in range(3) for z in range(BZ)]
        fine = [wide[group + dx, z][1] for dx in range(3) for z in range(BZ)]
        stacked = jnp.concatenate(coarse + fine + coarse + [ones], axis=0)
        hidden = jnp.dot(table, stacked, preferred_element_type=F32)
        hidden = jnp.maximum(hidden, 0.0)
        if group == 0 and keep is not None:
            hidden = hidden * keep
        if keep_top is not None:
            top = C1 * BZ
            hidden = jnp.concatenate([hidden[:top] * keep_top, hidden[top:]], axis=0)
        coarse, fine = split_kernel(hidden)
        coarse_h[group * count : (group + 1) * count, :] = coarse
        fine_h[group * count : (group + 1) * count, :] = fine


def results(second, count, coarse_h, fine_h):
    both = jnp.dot(second[...], coarse_h[...], preferred_element_type=F32)
    rest = jnp.dot(second[:count, :], fine_h[...], preferred_element_type=F32)
    return both[:count] + both[count:] + rest


def inner_body(joined, first, second, bias, out, phases, coarse_h, fine_h):
    for z in range(BZ):
        even = joined[z, :, :HALF]
        odd = joined[z, :, HALF:]
        parts = (pltpu.roll(even, 1, 1), pltpu.roll(odd, 1, 1), even, odd, pltpu.roll(even, HALF - 1, 1))
        for j, part in enumerate(parts):
            phases[j, z, 0:8, :] = jnp.zeros((8, HALF), F32)
            phases[j, z, SROW - 8 : SROW, :] = jnp.zeros((8, HALF), F32)
            phases[j, z, TOP : TOP + BY, :] = part
    half = BLOCKS // 2
    for step in range(half):
        blocks = (step, step + half)
        wide = {}
        for j in range(PHASES):
            for z in range(BZ):
                cut = [phases[j, z, 8 * b : 8 * b + WIN, :] for b in blocks]
                wide[j, z] = split_kernel(jnp.concatenate(cut, axis=1))
        scratch = (coarse_h.at[step % 2], fine_h.at[step % 2])
        hidden_parts(wide, first[...], HID, *scratch)
        result = results(second, OUTM, *scratch)
        for side, b in enumerate(blocks):
            for r in range(OUT_ROWS):
                out[pl.ds(OUT_ROWS * b + r, C2, stride=BY // 2), :] = (
                    result[r * C2 : (r + 1) * C2, side * HALF : (side + 1) * HALF] + bias[...]
                )


def inner(joined, first, second, bias):
    vmem = pl.BlockSpec(memory_space=pltpu.VMEM)
    return pl.pallas_call(
        inner_body,
        in_specs=[vmem] * 4,
        out_specs=vmem,
        out_shape=jax.ShapeDtypeStruct((C2 * BY // 2, HALF), F32),
        scratch_shapes=[
            pltpu.VMEM((PHASES, BZ, SROW, HALF), F32),
            pltpu.VMEM((2, K2, 256), BF16),
            pltpu.VMEM((2, K2, 256), BF16),
        ],
        compiler_params=pltpu.CompilerParams(vmem_limit_bytes=48 * 2**20),
        name="inner",
    )(joined, first, second, bias)


def rim_body(
    grid, edge, joined, received, own_columns, inner_out, first, second, bias, first_rim, second_rim,
    out, coarse_h, fine_h,
):
    at_row = edge[0]
    at_col = edge[1]
    rows, cols = grid
    halo = {}
    for dy in (-1, 0, 1):
        for dx in (-1, 0, 1):
            if (dy, dx) == (0, 0):
                continue
            row = at_row + dy
            col = at_col + dx
            there = (row >= 0) & (row < rows) & (col >= 0) & (col < cols)
            index = jnp.where(there, row * cols + col, 0)
            halo[dy, dx] = jnp.where(there, received[index], 0.0)
    no_row = at_row == 0
    no_col = at_col == 0
    wide_lane = iota((8, 256), 1)

    def stored(above, here, below):
        zero = jnp.zeros((8, 128), F32)
        turned = [
            pltpu.roll(jnp.concatenate([part, zero], axis=1), by, 1)
            for part, by in ((above, 256 - (BY - TOP)), (here, TOP), (below, TOP + BY))
        ]
        low = jnp.where(wide_lane < TOP, turned[0], turned[1])
        return jnp.where(
            wide_lane < TOP + BY, low, jnp.where(wide_lane == TOP + BY, turned[2], 0.0)
        )

    from_left = stored(halo[-1, -1], halo[0, -1], halo[1, -1])
    from_right = stored(halo[-1, 1], halo[0, 1], halo[1, 1])
    from_above = halo[-1, 0]
    from_below = halo[1, 0]

    tall_lane = iota((2 * WIN, HALF), 1)
    sides = jnp.concatenate([from_left[:4], from_right[:4]], axis=0)
    ends = jnp.concatenate(
        [sides[:, :WIN], sides[:, LAST : LAST + WIN], jnp.zeros((8, 128 - 2 * WIN), F32)], axis=1
    )
    side_columns = jnp.transpose(ends)[: 2 * WIN]

    def column(row):
        return side_columns[:, row : row + 1]

    wide = {}
    for z in range(BZ):
        halves = []
        for half in range(2):
            own = joined[z, :, half * HALF : (half + 1) * HALF]
            at = 4 * z + 2 * half
            bottom = 2 * z + half
            ends = [
                from_above[at : at + 2],
                own[: WIN - TOP],
                own[LAST - TOP :],
                from_below[bottom : bottom + 1],
                jnp.zeros((LAST + WIN - BY - TOP - 1, HALF), F32),
            ]
            halves.append(jnp.concatenate(ends, axis=0))
        even, odd = halves
        parts = (
            jnp.where(tall_lane == 0, column(2 * z), pltpu.roll(even, 1, 1)),
            jnp.where(tall_lane == 0, column(2 * z + 1), pltpu.roll(odd, 1, 1)),
            even,
            odd,
            jnp.where(
                tall_lane == HALF - 1, column(4 + z), pltpu.roll(even, HALF - 1, 1)
            ),
        )
        for j, part in enumerate(parts):
            wide[j, z] = split_kernel(jnp.concatenate([part[:WIN], part[WIN:]], axis=1))

    left_rows = []
    right_rows = []
    cut = []
    for z in range(BZ):
        for c in range(2):
            at = 4 * z + c
            cut.append(jnp.concatenate([from_above[at : at + 1], from_above[at + 2 : at + 3]], axis=1))
        cut.append(jnp.concatenate([from_below[2 * z : 2 * z + 1], from_below[2 * z + 1 : 2 * z + 2]], axis=1))
        cut.append(jnp.zeros((5, COLS), F32))
    outer_all = lax.dot_general(
        pick_columns(),
        jnp.concatenate(cut, axis=0),
        (((1,), (1,)), ((), ())),
        precision=EXACT,
        preferred_element_type=F32,
    )
    outer_all = jnp.concatenate([outer_all, jnp.zeros((8, 256 - 8 * BZ), F32)], axis=1)
    for z in range(BZ):
        outer = pltpu.roll(outer_all, 256 - 8 * z, 1) if z else outer_all
        here = jnp.concatenate([own_columns[8 * z : 8 * z + 8, :], jnp.zeros((8, BY), F32)], axis=1)
        own = jnp.where(
            wide_lane < TOP,
            outer,
            jnp.where(
                wide_lane < TOP + BY,
                pltpu.roll(here, TOP, 1),
                jnp.where(wide_lane == TOP + BY, pltpu.roll(outer, BY, 1), 0.0),
            ),
        )
        one = jnp.ones((1, 256), F32)
        rest = jnp.zeros((2, 256), F32)
        left_rows += [from_left[2 * z : 2 * z + 2], own[4:7], one, rest]
        right_rows += [own[0:4], from_right[z : z + 1], one, rest]
    coarse, fine = split_kernel(jnp.concatenate(left_rows + right_rows, axis=0))
    src = iota((256, 256), 0)
    dst = iota((256, 256), 1)
    apart = src == jnp.where(dst < 128, 2 * dst, 2 * (dst - 128) + 1)
    apart = jnp.where(apart, 1.0, 0.0).astype(BF16)
    lines = jnp.dot(jnp.concatenate([coarse, fine], axis=0), apart, preferred_element_type=F32)
    lines = lines[:32] + lines[32:]
    out_rows = BY // 2
    line_lane = iota((16, 128), 1)

    def stored_rows(t):
        cut = lines[:, (t % 2) * 128 : (t % 2) * 128 + 128]
        return jnp.where(
            line_lane < out_rows,
            pltpu.roll(cut[:16], (128 - t // 2) % 128, 1) if t // 2 else cut[:16],
            pltpu.roll(cut[16:], out_rows - t // 2, 1),
        )

    taken = [stored_rows(t) for t in range(5)]

    def product(table, values):
        coarse, fine = split_kernel(values)
        stacked = jnp.concatenate([coarse, fine, coarse], axis=0)
        return jnp.dot(table[...], stacked, preferred_element_type=F32)

    reach = [jnp.concatenate([taken[row + dy] for row in range(3)], axis=1) for dy in range(3)]
    hidden = jnp.maximum(product(first_rim, jnp.concatenate(reach, axis=0)), 0.0)
    lane = iota((3 * C1 * BZ, 384), 1)
    depth = iota((3 * C1 * BZ, 384), 0)
    outside = no_row & ((lane == 0) | (lane == out_rows))
    outside = outside | (no_col & ((lane & 127) < out_rows) & (depth < C1 * BZ))
    hidden = jnp.where(outside, 0.0, hidden)
    reach = [hidden[:, row * 128 : (row + 1) * 128] for row in range(3)]
    found = product(second_rim, jnp.concatenate(reach, axis=0)) + bias[...]
    turned = jnp.transpose(found)
    columns = [turned[:out_rows], turned[out_rows:]]
    out_lane = iota((BY // 2, HALF), 1)
    for o in range(C2):
        at = o * (BY // 2)
        values = inner_out[at : at + BY // 2, :]
        values = jnp.where(out_lane == 0, columns[0][:, o : o + 1], values)
        out[at : at + BY // 2, :] = jnp.where(out_lane == HALF - 1, columns[1][:, o : o + 1], values)

    keep = jnp.where(no_col & ((iota((1, 256), 1) & (HALF - 1)) == 0), 0.0, 1.0)
    keep_top = jnp.where(no_row & (iota((1, 256), 1) < HALF), 0.0, 1.0)
    hidden_parts(wide, first[:ROW_HID, :], ROW_HID, coarse_h, fine_h, keep, keep_top)
    result = results(second, C2, coarse_h, fine_h)
    for side, at in enumerate((0, BY // 2 - 1)):
        out[pl.ds(at, C2, stride=BY // 2), :] = (
            result[:, side * HALF : (side + 1) * HALF] + bias[...]
        )


def rim(grid, edge, joined, received, own_columns, inner_out, first, second, bias, first_rim, second_rim):
    vmem = pl.BlockSpec(memory_space=pltpu.VMEM)
    return pl.pallas_call(
        lambda *refs: rim_body(grid, *refs),
        in_specs=[pl.BlockSpec(memory_space=pltpu.SMEM)] + [vmem] * 9,
        out_specs=vmem,
        out_shape=jax.ShapeDtypeStruct((C2 * BY // 2, HALF), F32),
        scratch_shapes=[pltpu.VMEM((3 * ROW_HID, 256), BF16), pltpu.VMEM((3 * ROW_HID, 256), BF16)],
        compiler_params=pltpu.CompilerParams(vmem_limit_bytes=48 * 2**20),
        name="rim",
    )(edge, joined, received, own_columns, inner_out, first, second, bias, first_rim, second_rim)


def rim_tables(weight1, bias1, weight2):
    kernel = weight1[:, 0]
    planes = jnp.stack([kernel[:, 1:3], kernel[:, 0:2]], axis=1)
    reach = np.zeros((3, 3, 8), np.float32)
    for i in range(3):
        for dx in range(3):
            reach[i, dx, i + dx] = 1.0
    table = jnp.einsum("czpyx,kxq->kczypq", planes, jnp.asarray(reach), precision=EXACT)
    ones = np.zeros((3, BZ, 8), np.float32)
    ones[0, 0, PHASES] = 1.0
    table = table + bias1[None, :, None, None, None, None] * jnp.asarray(ones)
    first = table.reshape(3 * C1 * BZ, 3 * BZ * 8)
    second = jnp.transpose(weight2[:, :, 1:3], (0, 3, 4, 1, 2)).reshape(C2, 9 * C1 * BZ)

    def stacked(values):
        coarse, fine = split_host(values)
        return jnp.concatenate([coarse, coarse, fine], axis=1)

    row = jnp.transpose(weight2[:, :, 1:3], (0, 4, 3, 1, 2)).reshape(C2, 3 * ROW_HID)
    return stacked(first), stacked(second), jnp.concatenate(split_host(row), axis=0)


def first_table(weight, bias):
    kernel = weight[:, 0]
    planes = jnp.stack([kernel[:, 1:3], kernel[:, 0:2]], axis=1)
    reach = np.zeros((HID_ROWS, 3, WIN), np.float32)
    for i in range(HID_ROWS):
        for dy in range(3):
            reach[i, dy, i + dy] = 1.0
    table = jnp.einsum("czpyx,iys->iczxps", planes, jnp.asarray(reach), precision=EXACT)
    coarse, fine = split_host(table.reshape(HID, K1))
    each = jnp.tile(jnp.repeat(bias, BZ), HID_ROWS)
    one = lax.reduce_precision(each, 8, 7)
    two = lax.reduce_precision(each - one, 8, 7)
    three = each - one - two
    tail = jnp.stack([one, two, three], axis=1).astype(BF16)
    tail = jnp.pad(tail, ((0, 0), (0, 16 - 3)))
    return jnp.concatenate([coarse, coarse, fine, tail], axis=1)


def second_table(weight):
    reach = np.zeros((OUT_ROWS, 3, HID_ROWS), np.float32)
    for i in range(OUT_ROWS):
        for dy in range(3):
            reach[i, dy, 2 * i + dy] = 1.0
    table = jnp.einsum("oczyx,iyh->ioxhcz", weight[:, :, 1:3], jnp.asarray(reach), precision=EXACT)
    coarse, fine = split_host(table.reshape(OUTM, K2))
    return jnp.concatenate([coarse, fine], axis=0)


def body(strips, routes, conv1_weight, conv1_bias, conv2_weight, conv2_bias):
    rows = lax.axis_size("gx")
    cols = lax.axis_size("gy")
    senders = rows * cols
    per_pair = max(1, STRIPS // senders)
    axes = ("gx", "gy")
    at_row = lax.axis_index("gx").astype(jnp.int32)
    at_col = lax.axis_index("gy").astype(jnp.int32)
    edge = jnp.stack([at_row, at_col])
    routes_t = routes.T
    outgoing = pack(strips, routes_t, senders, per_pair)
    arrived = lax.all_to_all(outgoing, axes, split_axis=0, concat_axis=0, tiled=True)
    first = first_table(conv1_weight, conv1_bias)
    second = second_table(conv2_weight)
    bias = jnp.broadcast_to(conv2_bias[:, None], (C2, HALF))
    first_rim, second_rim, second_row = rim_tables(conv1_weight, conv1_bias, conv2_weight)
    joined, messages, own_columns = join((rows, cols), edge, arrived, per_pair)
    received = lax.all_to_all(messages, axes, split_axis=0, concat_axis=0, tiled=True)
    inner_out = inner(joined, first, second, bias)
    features = rim(
        (rows, cols), edge, joined, received, own_columns, inner_out, first, second_row, bias, first_rim, second_rim
    )
    return features.reshape(C2, 1, BY // 2, HALF)


def solution(mesh):
    in_specs = (P(("gx", "gy"), None, None, None), P(("gx", "gy"), None), P(), P(), P(), P())
    out_specs = P(None, None, "gx", "gy")
    return jax.shard_map(body, mesh=mesh, in_specs=in_specs, out_specs=out_specs, check_vma=False)
```
